32 devices in a mesh: dom: 8 (over z, x), rep: 4 (over y, core).
Axes of the slice: x: 2, y: 2, z: 4, core: 2. Of those that a mesh axis runs over, the one named last changes fastest.
Arguments:
- features: bfloat16 [2048, 256], P('dom'), may hold values from -6 to 6
- positions: float32 [3, 2048], P(None, 'dom'), may hold values from -6 to 6
- radial: bfloat16 [8, 256, 256], replicated, may hold values from -0.03125 to 0.03125
- mixing: bfloat16 [256, 256], replicated, may hold values from -0.375 to 0.375
- readout: float32 [256], replicated, may hold values from -4 to 4
- decay: float32 [8], replicated, may hold values from 0.1 to 1
- send_rows: int32 [4, 1024], P(None, 'dom'), may hold values from 0 to 255
- pair_home: int32 [1536], P(('dom', 'rep')), may hold values from 0 to 1
- pair_other: int32 [1536], P(('dom', 'rep')), may hold values from 0 to 5
- pair_kind: int32 [1536], P(('dom', 'rep')), may hold values from 0 to 7
- pair_image: int32 [3, 1536], P(None, ('dom', 'rep')), may hold values from -1 to 1
Outputs:
- grad_features: bfloat16 [2048, 256], P('dom')
- forces: float32 [3, 2048], P(None, 'dom')
- virials: float32 [6, 2048], P(None, 'dom')
- grad_mixing: float32 [256, 256], P('dom', 'rep')
The draws below stay inside these ranges and needn't reach their ends.
Inputs may be any that keep to these rules, and one draw needn't show every extreme that they name: `send_rows`: rows may repeat within a round.
All inputs are finite; a program needn't handle non-finite values.
Results may differ from the reference program's by a relative error of at most 0.006.
Values may be sent and summed in bfloat16 or wider, within the bound.
A program may use at most 128 MiB of HBM per device.

```python
import math
import jax
import jax.numpy as jnp
from jax import lax

C = 256
RADIAL = 8
TILE_ATOMS = 128
ROUNDS = 4
SUBDOMAIN_ATOMS = 256
PAIRS_DEV = 48
NATOM = 2048
PAIRS = 1536
N_DOM = 8
N_REP = 4


def plant(array, key, smallest, top_value):
    place = [jax.random.randint(jax.random.fold_in(key, axis), (), 0, length) for axis, length in enumerate(array.shape)]
    widest = array.shape.index(max(array.shape))
    next_to = place[:widest] + [(place[widest] + 1) % array.shape[widest]] + place[widest + 1:]
    return array.at[tuple(place)].set(smallest).at[tuple(next_to)].set(top_value)


def steps_of(own_key, extent, cuts, least, top_value):
    def one(position, blocks):
        steps = jax.random.uniform(jax.random.fold_in(jax.random.fold_in(own_key, 6), position), (blocks,), jnp.float32, least / len(cuts), top_value / len(cuts))
        return jnp.repeat(jnp.exp(steps), extent[position] // blocks).reshape((-1,) + (1,) * (len(extent) - position - 1))

    level = one(*cuts[0])
    for cut in cuts[1:]:
        level = level * one(*cut)
    return level


def scatter_about(own_key, dims, spread, bound, split=(), dtype=jnp.bfloat16):
    loudness = steps_of(own_key, dims, split, -0.22, 0.18) if split else 1.0
    entries = jax.random.normal(own_key, dims, jnp.float32) * spread * loudness
    return jnp.minimum(jnp.maximum(entries, -bound), bound).astype(dtype)


def setup_inputs(seed: int = 0) -> dict:
    arg_keys = jax.random.split(jax.random.key(seed), 12)
    return {
        "features": scatter_about(arg_keys[0], (NATOM, C), 1.0, 6.0, ((0, 8),)),
        "positions": scatter_about(arg_keys[1], (3, NATOM), 1.0, 6.0, ((1, 8),), jnp.float32),
        "radial": scatter_about(arg_keys[2], (RADIAL, C, C), (C * TILE_ATOMS) ** -0.5, 0.03125),
        "mixing": scatter_about(arg_keys[3], (C, C), C ** -0.5, 0.375),
        "readout": scatter_about(arg_keys[4], (C,), 1.0, 4.0, (), jnp.float32),
        "decay": jnp.clip(jnp.exp(jax.random.uniform(arg_keys[5], (RADIAL,), jnp.float32, math.log(0.1), math.log(1.0))), 0.1, 1.0),
        "send_rows": plant(jax.random.randint(arg_keys[6], (ROUNDS, TILE_ATOMS * N_DOM), 0, SUBDOMAIN_ATOMS), jax.random.fold_in(arg_keys[6], 1), 0, SUBDOMAIN_ATOMS - 1).astype(jnp.int32),
        "pair_home": plant(jax.random.randint(arg_keys[7], (PAIRS,), 0, SUBDOMAIN_ATOMS // TILE_ATOMS), jax.random.fold_in(arg_keys[7], 1), 0, (SUBDOMAIN_ATOMS // TILE_ATOMS) - 1).astype(jnp.int32),
        "pair_other": plant(jax.random.randint(arg_keys[8], (PAIRS,), 0, SUBDOMAIN_ATOMS // TILE_ATOMS + ROUNDS), jax.random.fold_in(arg_keys[8], 1), 0, (SUBDOMAIN_ATOMS // TILE_ATOMS + ROUNDS) - 1).astype(jnp.int32),
        "pair_kind": plant(jax.random.randint(arg_keys[9], (PAIRS,), 0, RADIAL), jax.random.fold_in(arg_keys[9], 1), 0, RADIAL - 1).astype(jnp.int32),
        "pair_image": plant(jax.random.randint(arg_keys[10], (3, PAIRS), -1, 2), jax.random.fold_in(arg_keys[10], 1), -1, 1).astype(jnp.int32),
    }


offsets = (1, -1, 2, -2)
cell_edge = 2.0
component_pairs = ((0, 0), (1, 1), (2, 2), (0, 1), (0, 2), (1, 2))
highest_precision = lax.Precision.HIGHEST


def lowered(values):
    return lax.optimization_barrier(values.astype(jnp.bfloat16)).astype(jnp.float32)


def pair_setup(ext_feat, ext_pos, home_tile, other_tile, radial_pick, image_shift, radial, decay):
    tiles_feat = ext_feat.reshape(-1, TILE_ATOMS, ext_feat.shape[1])
    tiles_pos = ext_pos.reshape(3, -1, TILE_ATOMS)
    far_end = jnp.take(tiles_pos, other_tile, axis=1) + image_shift[:, :, None].astype(jnp.float32) * cell_edge
    near_end = jnp.take(tiles_pos, home_tile, axis=1)
    separation = far_end[:, :, None, :] - near_end[:, :, :, None]
    rates = jnp.take(decay, radial_pick)
    kernel = jnp.exp(-rates[:, None, None] * jnp.sum(separation * separation, axis=0))
    partner_rows = jnp.take(tiles_feat, other_tile, axis=0).astype(jnp.float32)
    chosen = jnp.take(radial, radial_pick, axis=0).astype(jnp.float32)
    mapped = lowered(jnp.einsum('pbc,pcd->pbd', partner_rows, chosen, precision=highest_precision))
    return separation, rates, kernel, mapped, chosen


def reference(features, positions, radial, mixing, readout, decay, send_rows, pair_home, pair_other, pair_kind, pair_image):
    channel_count = features.shape[1]
    home_tiles = SUBDOMAIN_ATOMS // TILE_ATOMS
    extended_tiles = home_tiles + ROUNDS
    pair_count = PAIRS_DEV * N_REP
    domain_feat = features.reshape(N_DOM, SUBDOMAIN_ATOMS, channel_count)
    domain_pos = positions.reshape(3, N_DOM, SUBDOMAIN_ATOMS).transpose(1, 0, 2)
    send_table = send_rows.reshape(ROUNDS, N_DOM, TILE_ATOMS)
    halo_feat = []
    halo_pos = []
    for section_no in range(ROUNDS):
        picked_feat = jnp.take_along_axis(domain_feat, send_table[section_no][:, :, None], axis=1)
        picked_pos = jnp.take_along_axis(domain_pos, send_table[section_no][:, None, :], axis=2)
        halo_feat.append(jnp.roll(picked_feat, offsets[section_no], axis=0))
        halo_pos.append(jnp.roll(picked_pos, offsets[section_no], axis=0))
    ext_feat = jnp.concatenate([domain_feat] + halo_feat, axis=1)
    ext_pos = jnp.concatenate([domain_pos] + halo_pos, axis=2)
    home_tile = pair_home.reshape(N_DOM, pair_count)
    other_tile = pair_other.reshape(N_DOM, pair_count)
    radial_pick = pair_kind.reshape(N_DOM, pair_count)
    image_shift = pair_image.reshape(3, N_DOM, pair_count).transpose(1, 0, 2)
    home_iota = lax.iota(jnp.int32, home_tiles)
    ext_iota = lax.iota(jnp.int32, extended_tiles)

    def forward_domain(inputs):
        feat_one, pos_one, home_one, other_one, pick_one, shift_one = inputs
        separation, rates, kernel, mapped, chosen = pair_setup(feat_one, pos_one, home_one, other_one, pick_one, shift_one, radial, decay)
        message_rows = jnp.einsum('pab,pbd->pad', lowered(kernel), mapped, precision=highest_precision)
        home_lookup_table = (home_one[None, :] == home_iota[:, None]).astype(jnp.float32)
        return jnp.einsum('so,oxe->sxe', home_lookup_table, message_rows, precision=highest_precision).reshape(SUBDOMAIN_ATOMS, channel_count)

    message = lax.map(forward_domain, (ext_feat, ext_pos, home_tile, other_tile, radial_pick, image_shift))
    message = message.reshape(NATOM, channel_count)
    packed = message.astype(jnp.bfloat16)
    mixed_rows = jnp.dot(packed, mixing, preferred_element_type=jnp.float32)
    sigmoid_rows = jax.nn.sigmoid(mixed_rows)
    slope_rows = (readout * sigmoid_rows * (1.0 + mixed_rows * (1.0 - sigmoid_rows))).astype(jnp.bfloat16)
    adjoint = jnp.dot(slope_rows, mixing.T, preferred_element_type=jnp.float32).astype(jnp.bfloat16)
    grad_mixing = jnp.dot(packed.T, slope_rows, preferred_element_type=jnp.float32)
    adjoint_dom = adjoint.reshape(N_DOM, SUBDOMAIN_ATOMS, channel_count)

    def backward_domain(inputs):
        feat_one, pos_one, home_one, other_one, pick_one, shift_one, adjoint_one = inputs
        separation, rates, kernel, mapped, chosen = pair_setup(feat_one, pos_one, home_one, other_one, pick_one, shift_one, radial, decay)
        kernel_low = lowered(kernel)
        adjoint_tiles = jnp.take(adjoint_one.reshape(home_tiles, TILE_ATOMS, channel_count), home_one, axis=0).astype(jnp.float32)
        kernel_grad = jnp.einsum('pad,pbd->pab', adjoint_tiles, mapped, precision=highest_precision)
        mapped_grad = lowered(jnp.einsum('pab,pad->pbd', kernel_low, adjoint_tiles, precision=highest_precision))
        feature_grad = jnp.einsum('pbd,pcd->pbc', mapped_grad, chosen, precision=highest_precision)
        weight = -2.0 * rates[:, None, None] * kernel * kernel_grad
        home_atom_side = []
        partner_side = []
        for axis_one in range(3):
            pull = weight * separation[axis_one]
            home_atom_side.append(jnp.sum(pull, axis=2))
            partner_side.append(-jnp.sum(pull, axis=1))
        for axis_one, axis_two in component_pairs:
            product = weight * separation[axis_one] * separation[axis_two]
            home_atom_side.append(-0.5 * jnp.sum(product, axis=2))
            partner_side.append(-0.5 * jnp.sum(product, axis=1))
        home_atom_side = jnp.stack(home_atom_side)
        partner_side = jnp.stack(partner_side)
        home_lookup_table = (home_one[None, :] == home_iota[:, None]).astype(jnp.float32)
        partner_table = (other_one[None, :] == ext_iota[:, None]).astype(jnp.float32)
        ext_grad = jnp.einsum('jp,pbc->jbc', partner_table, feature_grad, precision=highest_precision).reshape(extended_tiles * TILE_ATOMS, channel_count)
        extended_side = jnp.einsum('it,ztq->ziq', partner_table, partner_side, precision=highest_precision).reshape(9, extended_tiles * TILE_ATOMS)
        self_side = jnp.einsum('qk,gkv->gqv', home_lookup_table, home_atom_side, precision=highest_precision).reshape(9, SUBDOMAIN_ATOMS) + extended_side[:, :SUBDOMAIN_ATOMS]
        return ext_grad[:SUBDOMAIN_ATOMS], self_side, ext_grad[SUBDOMAIN_ATOMS:], extended_side[:, SUBDOMAIN_ATOMS:]

    own_grad, self_side, halo_grad, halo_side = lax.map(backward_domain, (ext_feat, ext_pos, home_tile, other_tile, radial_pick, image_shift, adjoint_dom))
    atom_iota = lax.iota(jnp.int32, SUBDOMAIN_ATOMS)
    for section_no in range(ROUNDS):
        returned_grad = jnp.roll(halo_grad[:, section_no * TILE_ATOMS:(section_no + 1) * TILE_ATOMS], -offsets[section_no], axis=0)
        returned_side = jnp.roll(halo_side[:, :, section_no * TILE_ATOMS:(section_no + 1) * TILE_ATOMS], -offsets[section_no], axis=0)
        send_onehot = (send_table[section_no][:, :, None] == atom_iota[None, None, :]).astype(jnp.float32)
        own_grad = own_grad + jnp.einsum('dta,dtc->dac', send_onehot, returned_grad, precision=highest_precision)
        self_side = self_side + jnp.einsum('dta,dct->dca', send_onehot, returned_side, precision=highest_precision)
    grad_features = own_grad.reshape(NATOM, channel_count).astype(jnp.bfloat16)
    forces = self_side[:, :3].transpose(1, 0, 2).reshape(3, NATOM)
    virials = self_side[:, 3:].transpose(1, 0, 2).reshape(6, NATOM)
    return grad_features, forces, virials, grad_mixing
```

```python
import functools
import types

import jax
import jax.numpy as jnp
from jax import lax
from jax.experimental import pallas as pl
from jax.experimental.pallas import tpu as pltpu
from jax.sharding import PartitionSpec as P

TILE = 128
OFFSETS = (1, -1, 2, -2)
CELL = 2.0
GROUP = 4
FORWARD_GROUP = 8
BACK_GROUP = 12
F32 = jnp.float32
BF16 = jnp.bfloat16
MESH = pl.DeviceIdType.MESH
VMEM = pl.BlockSpec(memory_space=pltpu.VMEM)
HBM = pl.BlockSpec(memory_space=pltpu.HBM)
INPUTS = ("feat_h", "pos_h", "rows_h", "radial_h", "mixing_h", "readout_h", "decay_h", "home_h", "other_h",
          "kind_h", "image_h", "home_row_h", "other_row_h", "kind_row_h")
OUTPUTS = ("out_feat", "out_force", "out_virial", "out_mix")


def nt(a, b):
    return lax.dot_general(a, b, (((1,), (1,)), ((), ())), preferred_element_type=F32)


def tn(a, b):
    return lax.dot_general(a, b, (((0,), (0,)), ((), ())), preferred_element_type=F32)


def mm(a, b):
    return jnp.dot(a, b, preferred_element_type=F32)


def split3(x):
    hi = x.astype(BF16)
    rest = x - hi.astype(F32)
    mid = rest.astype(BF16)
    low = (rest - mid.astype(F32)).astype(BF16)
    return hi, mid, low


def order_pairs(seg, lanes, subs):
    row = jnp.broadcast_to(seg, (TILE, TILE))
    col = jnp.transpose(row)
    before = (col < row) | ((col == row) & (subs < lanes))
    rank = jnp.sum(before.astype(jnp.int32), axis=0, keepdims=True)
    rank = jnp.transpose(jnp.broadcast_to(rank, (TILE, TILE)))
    order = jnp.sum(jnp.where(rank == lanes, subs, 0), axis=0, keepdims=True)
    upto = jnp.sum((col <= lanes).astype(jnp.int32), axis=0, keepdims=True)
    below = jnp.sum((col < lanes).astype(jnp.int32), axis=0, keepdims=True)
    return order, jnp.where(upto > below, upto, 0)


def kernel(names, n_dom, n_rep, *refs):
    m = types.SimpleNamespace(**dict(zip(names, refs)))
    d = lax.axis_index("dom")
    r = lax.axis_index("rep")
    y = lax.div(r, 2)
    c = lax.rem(r, 2)
    mate = 1 - c
    partner = r + 1 - 2 * c
    across = r + 2 - 4 * y
    atoms, channels = m.feat.shape
    own = atoms // TILE
    pairs = m.home.shape[0]
    kinds = m.radial.shape[0]
    n_ext = m.tiles.shape[0]

    def dom_at(o):
        return lax.rem(d + o + n_dom, n_dom)

    def at(dom, rep):
        return {"dom": dom, "rep": rep}

    loads = [pltpu.make_async_copy(src, dst, m.load.at[i]) for i, (src, dst) in enumerate((
        (m.rows_h, m.rows), (m.feat_h, m.feat), (m.pos_h, m.pos), (m.home_row_h, m.home_row),
        (m.other_row_h, m.other_row), (m.kind_row_h, m.kind_row), (m.radial_h, m.radial), (m.decay_h, m.decay),
        (m.home_h, m.home), (m.other_h, m.other), (m.kind_h, m.kind), (m.image_h, m.image),
        (m.mixing_h, m.mixing), (m.readout_h, m.readout)))]
    for copy in loads:
        copy.start()
    barrier = pltpu.get_barrier_semaphore()
    mine = (c + 1, -(c + 1))
    theirs = (2 - c, c - 2)
    peers = [lax.rem(r + i, n_rep) for i in range(1, n_rep)]

    def hello(dom, rep):
        pl.semaphore_signal(barrier, inc=1, device_id=at(dom, rep), device_id_type=MESH)

    def greet(i, _):
        hello(lax.rem(d + i, n_dom), r)
        return 0

    lax.fori_loop(1, n_dom, greet, 0)
    for o in mine:
        hello(dom_at(o), partner)
        hello(dom_at(o), across)
    for o in theirs:
        hello(dom_at(o), partner)
    for q in peers:
        hello(d, q)

    started = []

    def push(src, dst, ss, rs, target):
        copy = pltpu.make_async_remote_copy(src, dst, ss, rs, device_id=target, device_id_type=MESH)
        copy.start()
        started.append(copy)

    def take(dst, ss, rs):
        pltpu.make_async_remote_copy(dst, dst, ss, rs, device_id=at(d, partner), device_id_type=MESH).wait_recv()

    for copy in loads[:3]:
        copy.wait()
    iota = lax.broadcasted_iota(jnp.int32, (atoms, TILE), 0)
    hots = []
    for q in range(2):
        hot = (iota == m.rows[pl.ds(2 * c + q, 1), :]).astype(F32)
        hots.append(hot.astype(BF16))
        m.sendp[q] = jnp.dot(m.pos[...], hot, precision=lax.Precision.HIGHEST, preferred_element_type=F32)
    pl.semaphore_wait(barrier, 6 + n_rep - 1 + n_dom - 1)
    for q in range(2):
        for i, rep in enumerate((r, partner)):
            push(m.sendp.at[q], m.recvp.at[2 * c + q], m.s_pos.at[q, i], m.r_pos.at[2 * c + q],
                 at(dom_at(mine[q]), rep))
    for q in range(2):
        m.sendf[q] = tn(hots[q], m.feat[...]).astype(BF16)
        push(m.sendf.at[q], m.ext.at[own + 2 * c + q], m.s_feat.at[q], m.r_feat.at[2 * c + q],
             at(dom_at(mine[q]), r))

    for copy in loads[3:6]:
        copy.wait()
    m.raw[...] = jnp.zeros_like(m.raw)
    for i, src in enumerate((m.home_row, m.kind_row, m.other_row)):
        m.raw[i:i + 1, :pairs] = src[...]
    raw = m.raw[...]
    lanes = lax.broadcasted_iota(jnp.int32, (TILE, TILE), 1)
    subs = lax.broadcasted_iota(jnp.int32, (TILE, TILE), 0)
    real = lanes[0:1] < pairs
    order_f, end_f = order_pairs(jnp.where(real, raw[0:1] * kinds + raw[1:2], TILE), lanes, subs)
    order_b, end_b = order_pairs(jnp.where(real, raw[2:3], TILE), lanes, subs)
    m.plan_v[...] = jnp.concatenate(
        [order_f, order_b, end_f, end_b, jnp.zeros((4, TILE), jnp.int32)], axis=0)
    plan_copy = pltpu.make_async_copy(m.plan_v, m.plan, m.s_plan)
    plan_copy.start()

    def columns(j):
        for x in range(3):
            m.col[j, x] = jnp.transpose(jnp.broadcast_to(m.tiles[j][x:x + 1, :], (TILE, TILE)))

    def table(j):
        pos = m.tiles[j]
        x, yy, z = pos[0:1, :], pos[1:2, :], pos[2:3, :]
        zero = jnp.zeros((2, TILE), F32)
        one_rows = jnp.concatenate([x, yy, z, x, x, yy, zero], axis=0)
        two_rows = jnp.concatenate([x, yy, z, yy, z, z, zero], axis=0)
        m.first[j] = one_rows
        m.second[j] = two_rows
        stack = jnp.concatenate([one_rows * two_rows, one_rows, two_rows], axis=0)
        parts = [v.astype(F32) for v in split3(stack)]
        m.moments[j] = jnp.concatenate(
            [parts[0], jnp.ones((8, TILE), F32), parts[1], parts[2]], axis=0).astype(BF16)

    for j in range(own):
        m.tiles[j] = m.pos[:, j * TILE:(j + 1) * TILE]
        m.ext[j] = m.feat[j * TILE:(j + 1) * TILE, :]
        columns(j)
        table(j)
    m.sums[0] = jnp.zeros_like(m.sums[0])
    m.far[0] = jnp.zeros_like(m.far[0])
    m.near[...] = jnp.zeros_like(m.near)
    for copy in loads[6:]:
        copy.wait()
    for t in range(4):
        take(m.recvp.at[t], m.s_pos.at[0, 0], m.r_pos.at[t])
        m.tiles[own + t] = m.recvp[t]
        columns(own + t)
        table(own + t)

    def kernels(g, _):
        for u in range(GROUP):
            p = g * GROUP + u
            h, o, k = m.home[p], m.other[p], m.kind[p]
            shift = [m.image[x, p].astype(F32) * CELL for x in range(3)]
            rate = -m.decay[k]
            row, back = m.tiles[o], m.tiles[h]
            d2 = None
            e2 = None
            for x in range(3):
                sep = (row[x:x + 1, :] + shift[x]) - m.col[h, x]
                d2 = sep * sep if d2 is None else d2 + sep * sep
                sep = m.col[o, x] - (back[x:x + 1, :] - shift[x])
                e2 = sep * sep if e2 is None else e2 + sep * sep
            m.kern_ab[p] = jnp.exp(d2 * rate).astype(BF16)
            m.kern_ba[p] = jnp.exp(e2 * rate)
        return 0

    half_steps = pairs // GROUP // 2
    lax.fori_loop(0, half_steps, kernels, 0)
    for q in range(2):
        t = 2 * c + q
        take(m.ext.at[own + t], m.s_feat.at[q], m.r_feat.at[t])
        push(m.ext.at[own + t], m.ext.at[own + t], m.s_relay.at[q], m.r_relay.at[t], at(d, partner))
    lax.fori_loop(half_steps, pairs // GROUP, kernels, 0)
    plan_copy.wait()
    for q in range(2):
        t = 2 * mate + q
        take(m.ext.at[own + t], m.s_relay.at[q], m.r_relay.at[t])

    def pair_at(row, i):
        return jnp.clip(m.plan[row, i], 0, pairs - 1)

    def sum_at(row, i):
        return jnp.clip(m.plan[row, i], 0, pairs)

    def seg_f(p):
        return m.home[p] * kinds + m.kind[p]

    def forward(g, _):
        acc = m.sums[g * FORWARD_GROUP]
        for u in range(FORWARD_GROUP):
            i = g * FORWARD_GROUP + u
            p = pair_at(0, i)
            last = pair_at(0, jnp.maximum(i - 1, 0))
            keep = (seg_f(p) == seg_f(last)).astype(F32)
            acc = acc * keep + mm(m.kern_ab[p], m.ext[m.other[p]])
            m.sums[i + 1] = acc
        return 0

    lax.fori_loop(0, pairs // FORWARD_GROUP, forward, 0)

    def message(h):
        left = [m.sums[sum_at(2, h * kinds + k)].astype(BF16) for k in range(kinds)]
        return mm(jnp.concatenate(left, axis=1), m.radial[...].reshape(kinds * channels, channels))

    m.msg[...] = message(mate).astype(BF16)
    push(m.msg, m.msg_in, m.s_msg.at[0], m.r_msg.at[0], at(d, partner))
    value = message(c)
    take(m.msg_in, m.s_msg.at[0], m.r_msg.at[0])
    value = (value + m.msg_in[...].astype(F32)).astype(BF16)
    m.chip[...] = value
    push(m.chip, m.chip_in, m.s_msg.at[1], m.r_msg.at[1], at(d, across))
    take(m.chip_in, m.s_msg.at[1], m.r_msg.at[1])
    low = (value.astype(F32) + m.chip_in[...].astype(F32)).astype(BF16)
    mixed = mm(low, m.mixing[...])
    sig = jax.nn.sigmoid(mixed)
    slope = (m.readout[...] * sig * (1.0 + mixed * (1.0 - sig))).astype(BF16)
    adj = nt(slope, m.mixing[...]).astype(BF16)
    m.adjoint[c] = adj
    push(m.adjoint.at[c], m.adjoint.at[c], m.s_adj.at[0], m.r_adj.at[0], at(d, partner))
    m.slope[c] = slope
    push(m.slope.at[c], m.slope.at[c], m.s_adj.at[1], m.r_adj.at[1], at(d, partner))
    m.packed[c] = low
    push(m.packed.at[c], m.packed.at[c], m.s_adj.at[2], m.r_adj.at[2], at(d, partner))

    def spread(h):
        value = m.adjoint[h]
        for k in range(kinds):
            m.weights[h * kinds + k] = nt(value, m.radial[k]).astype(BF16)

    spread(c)
    take(m.adjoint.at[mate], m.s_adj.at[0], m.r_adj.at[0])
    spread(mate)

    sub = lax.broadcasted_iota(jnp.int32, (8, TILE), 0)
    is_x1, is_y1 = (sub == 0) | (sub == 3) | (sub == 4), (sub == 1) | (sub == 5)
    is_x2, is_y2 = (sub == 0), (sub == 1) | (sub == 3)

    def combine(res, a, b):
        quad = res[0:8] + res[32:40] + res[56:64]
        lin1 = res[8:16] + res[40:48] + res[64:72]
        lin2 = res[16:24] + res[48:56] + res[72:80]
        one = res[24:32]
        force = lin1 - a * one
        virial = -0.5 * (quad - a * lin2 - b * lin1 + a * b * one)
        return jnp.concatenate([force, virial], axis=0)

    def backward(g, _):
        found = []
        for u in range(BACK_GROUP):
            i = g * BACK_GROUP + u
            p = pair_at(1, i)
            last = pair_at(1, jnp.maximum(i - 1, 0))
            h, o, k = m.home[p], m.other[p], m.kind[p]
            keep = (o == m.other[last]).astype(F32)
            kern = m.kern_ba[p]
            right = m.weights[h * kinds + k]
            weight = ((-2.0 * m.decay[k]) * kern * nt(m.ext[o], right)).astype(BF16)
            found.append((i, p, h, o, keep, kern.astype(BF16), right, weight))
        acc = m.sums[g * BACK_GROUP]
        far = m.far[g * BACK_GROUP]
        near = [m.near[j] for j in range(own)]
        for i, p, h, o, keep, kern, right, weight in found:
            shift = [m.image[x, p].astype(F32) * CELL for x in range(3)]
            s1 = jnp.where(is_x1, shift[0], jnp.where(is_y1, shift[1], shift[2]))
            s2 = jnp.where(is_x2, shift[0], jnp.where(is_y2, shift[1], shift[2]))
            near_side = combine(mm(m.moments[o], weight), m.first[h] - s1, m.second[h] - s2)
            far_side = combine(nt(m.moments[h], weight), m.first[o] + s1, m.second[o] + s2)
            for j in range(own):
                near[j] = near[j] + near_side * (h == j).astype(F32)
            far = far * keep + far_side
            m.far[i + 1] = far
            acc = acc * keep + mm(kern, right)
            m.sums[i + 1] = acc
        for j in range(own):
            m.near[j] = near[j]
        return 0

    lax.fori_loop(0, pairs // BACK_GROUP, backward, 0)

    def settle(j, local):
        at_end = sum_at(3, j)
        total = m.sums[at_end]
        for half in range(2):
            m.gfeat[j, half] = total[:, half * TILE:(half + 1) * TILE].astype(BF16)
        m.side[j] = m.far[at_end] + m.near[j] if local else m.far[at_end]

    for slot, j in ((1, 2 + 2 * mate), (2, 3 + 2 * mate), (0, mate)):
        settle(j, slot == 0)
        push(m.gfeat.at[j], m.gp.at[slot], m.s_gp.at[slot], m.r_gp.at[slot], at(d, partner))
        push(m.side.at[j], m.gs.at[slot], m.s_gs.at[slot], m.r_gs.at[slot], at(d, partner))
    for slot, j in ((1, 2 + 2 * c), (2, 3 + 2 * c), (0, c)):
        settle(j, slot == 0)
    take(m.slope.at[mate], m.s_adj.at[1], m.r_adj.at[1])
    take(m.packed.at[mate], m.s_adj.at[2], m.r_adj.at[2])
    share = channels // n_rep
    pick = (lax.broadcasted_iota(jnp.int32, (channels, share), 0)
            == lax.broadcasted_iota(jnp.int32, (channels, share), 1) + r * share).astype(BF16)
    cols = mm(m.slope[...].reshape(atoms, channels), pick).astype(BF16)
    m.mix[...] = tn(m.packed[...].reshape(atoms, channels), cols).reshape(m.mix.shape)
    for slot, j in ((1, 2 + 2 * c), (2, 3 + 2 * c), (0, c)):
        take(m.gp.at[slot], m.s_gp.at[slot], m.r_gp.at[slot])
        take(m.gs.at[slot], m.s_gs.at[slot], m.r_gs.at[slot])
        m.sb[slot] = (m.gfeat[j].astype(F32) + m.gp[slot].astype(F32)).astype(BF16)
        m.ss[slot] = m.side[j] + m.gs[slot]
        for half in ((0, 1) if slot else (1 - y,)):
            dest = at(dom_at(-mine[slot - 1]) if slot else d, 2 * half + c)
            push(m.sb.at[slot, half], m.rf.at[slot, y], m.s_rf.at[slot, half], m.r_rf.at[slot, y], dest)
            push(m.ss.at[slot], m.rs.at[slot, y], m.s_rs.at[slot, half], m.r_rs.at[slot, y], dest)

    def mix_copy(i):
        to = lax.rem(d + i, n_dom)
        return pltpu.make_async_remote_copy(m.mix.at[to], m.rm.at[d], m.s_mix.at[i], m.r_mix.at[d],
                                            device_id=at(to, r), device_id_type=MESH)

    lax.fori_loop(1, n_dom, lambda i, _: (mix_copy(i).start(), 0)[1], 0)
    take(m.rf.at[0, 1 - y], m.s_rf.at[0, 0], m.r_rf.at[0, 1 - y])
    take(m.rs.at[0, 1 - y], m.s_rs.at[0, 0], m.r_rs.at[0, 1 - y])
    feat_self = m.sb[0, y].astype(F32) + m.rf[0, 1 - y].astype(F32)
    side_self = m.ss[0] + m.rs[0, 1 - y]
    is_low = c == 0
    zero = jnp.zeros_like(feat_self)
    total = jnp.concatenate([jnp.where(is_low, feat_self, zero), jnp.where(is_low, zero, feat_self)], axis=0)
    zside = jnp.zeros_like(side_self)
    total_side = jnp.concatenate([jnp.where(is_low, side_self, zside), jnp.where(is_low, zside, side_self)],
                                 axis=1)
    for q in range(2):
        hot = (iota == m.rows[pl.ds(2 * c + q, 1), :]).astype(F32).astype(BF16)
        slot = 1 + q
        got = None
        for s in range(2):
            take(m.rf.at[slot, s], m.s_rf.at[0, 0], m.r_rf.at[slot, s])
            take(m.rs.at[slot, s], m.s_rs.at[0, 0], m.r_rs.at[slot, s])
            total = total + mm(hot, m.rf[slot, s])
            got = m.rs[slot, s] if got is None else got + m.rs[slot, s]
        for v in split3(got):
            total_side = total_side + nt(v, hot)
    m.part[r] = total.astype(BF16)
    m.pside[...] = total_side
    for i, q in enumerate(peers):
        push(m.part.at[r], m.part.at[r], m.s_part.at[i], m.r_part.at[r], at(d, q))
    push(m.pside, m.qside, m.s_side, m.r_side, at(d, partner))

    def mix_add(i, value):
        frm = lax.rem(d + i, n_dom)
        take(m.rm.at[frm], m.s_mix.at[0], m.r_mix.at[frm])
        return value + m.rm[frm]

    m.out_mix[...] = lax.fori_loop(1, n_dom, mix_add, m.mix[d])
    take(m.qside, m.s_side, m.r_side)
    final = total_side + m.qside[...]
    m.out_force[...] = final[0:3]
    m.out_virial[...] = final[8:14]
    for q in peers:
        take(m.part.at[q], m.s_part.at[0], m.r_part.at[q])
    for half in range(2):
        m.out_feat[:, half * TILE:(half + 1) * TILE] = (
            m.part[2 * half].astype(F32) + m.part[2 * half + 1].astype(F32)).astype(BF16)
    for copy in started:
        copy.wait_send()
    lax.fori_loop(1, n_dom, lambda i, _: (mix_copy(i).wait_send(), 0)[1], 0)


def copy_out(a, b, c, d, a_h, b_h, c_h, d_h, sem):
    copies = [pltpu.make_async_copy(src, dst, sem.at[i])
              for i, (src, dst) in enumerate(((a, a_h), (b, b_h), (c, c_h), (d, d_h)))]
    for copy in copies:
        copy.start()
    for copy in copies:
        copy.wait()


def on_device(n_dom, n_rep, features, positions, radial, mixing, readout, decay, send_rows, pair_home,
              pair_other, pair_kind, pair_image):
    atoms, channels = features.shape
    own = atoms // TILE
    n_ext = own + len(OFFSETS)
    kinds = radial.shape[0]
    pairs = pair_home.shape[0]
    dma = pltpu.SemaphoreType.DMA
    mix_rows, mix_cols = channels // n_dom, channels // n_rep
    half = (2, TILE, channels // 2)
    readout_row = readout.reshape(1, channels)
    pair_rows = [a.reshape(1, pairs) for a in (pair_home, pair_other, pair_kind)]

    scratch = {
        "feat": pltpu.VMEM(features.shape, BF16), "pos": pltpu.VMEM(positions.shape, F32),
        "rows": pltpu.VMEM(send_rows.shape, jnp.int32), "radial": pltpu.VMEM(radial.shape, BF16),
        "mixing": pltpu.VMEM(mixing.shape, BF16), "readout": pltpu.VMEM(readout_row.shape, F32),
        "decay": pltpu.SMEM(decay.shape, F32), "home": pltpu.SMEM(pair_home.shape, jnp.int32),
        "other": pltpu.SMEM(pair_other.shape, jnp.int32), "kind": pltpu.SMEM(pair_kind.shape, jnp.int32),
        "image": pltpu.SMEM(pair_image.shape, jnp.int32),
        "home_row": pltpu.VMEM((1, pairs), jnp.int32), "other_row": pltpu.VMEM((1, pairs), jnp.int32),
        "kind_row": pltpu.VMEM((1, pairs), jnp.int32),
        "raw": pltpu.VMEM((8, TILE), jnp.int32), "plan_v": pltpu.VMEM((8, TILE), jnp.int32),
        "plan": pltpu.SMEM((8, TILE), jnp.int32),
        "sendf": pltpu.VMEM((2, TILE, channels), BF16), "sendp": pltpu.VMEM((2, 3, TILE), F32),
        "recvp": pltpu.VMEM((4, 3, TILE), F32), "ext": pltpu.VMEM((n_ext, TILE, channels), BF16),
        "tiles": pltpu.VMEM((n_ext, 3, TILE), F32), "col": pltpu.VMEM((n_ext, 3, TILE, TILE), F32),
        "moments": pltpu.VMEM((n_ext, 80, TILE), BF16),
        "first": pltpu.VMEM((n_ext, 8, TILE), F32), "second": pltpu.VMEM((n_ext, 8, TILE), F32),
        "kern_ab": pltpu.VMEM((pairs, TILE, TILE), BF16), "kern_ba": pltpu.VMEM((pairs, TILE, TILE), F32),
        "sums": pltpu.VMEM((pairs + 1, TILE, channels), F32), "far": pltpu.VMEM((pairs + 1, 16, TILE), F32),
        "near": pltpu.VMEM((own, 16, TILE), F32),
        "msg": pltpu.VMEM((TILE, channels), BF16), "msg_in": pltpu.VMEM((TILE, channels), BF16),
        "chip": pltpu.VMEM((TILE, channels), BF16), "chip_in": pltpu.VMEM((TILE, channels), BF16),
        "adjoint": pltpu.VMEM((own, TILE, channels), BF16), "slope": pltpu.VMEM((own, TILE, channels), BF16),
        "packed": pltpu.VMEM((own, TILE, channels), BF16),
        "weights": pltpu.VMEM((own * kinds, TILE, channels), BF16),
        "gfeat": pltpu.VMEM((n_ext, *half), BF16), "side": pltpu.VMEM((n_ext, 16, TILE), F32),
        "gp": pltpu.VMEM((3, *half), BF16), "gs": pltpu.VMEM((3, 16, TILE), F32),
        "sb": pltpu.VMEM((3, *half), BF16), "ss": pltpu.VMEM((3, 16, TILE), F32),
        "rf": pltpu.VMEM((3, *half), BF16), "rs": pltpu.VMEM((3, 2, 16, TILE), F32),
        "mix": pltpu.VMEM((n_dom, mix_rows, mix_cols), F32), "rm": pltpu.VMEM((n_dom, mix_rows, mix_cols), F32),
        "part": pltpu.VMEM((n_rep, atoms, channels // 2), BF16),
        "pside": pltpu.VMEM((16, atoms), F32), "qside": pltpu.VMEM((16, atoms), F32),
        "load": dma((len(INPUTS),)), "s_plan": dma, "s_pos": dma((2, 2)), "r_pos": dma((4,)),
        "s_feat": dma((2,)), "r_feat": dma((4,)), "s_relay": dma((2,)), "r_relay": dma((4,)),
        "s_msg": dma((2,)), "r_msg": dma((2,)), "s_adj": dma((3,)), "r_adj": dma((3,)),
        "s_gp": dma((3,)), "r_gp": dma((3,)), "s_gs": dma((3,)), "r_gs": dma((3,)),
        "s_rf": dma((3, 2)), "r_rf": dma((3, 2)), "s_rs": dma((3, 2)), "r_rs": dma((3, 2)),
        "s_mix": dma((n_dom,)), "r_mix": dma((n_dom,)), "s_part": dma((n_rep,)), "r_part": dma((n_rep,)),
        "s_side": dma, "r_side": dma,
    }

    def shape(dims, dtype):
        return jax.ShapeDtypeStruct(dims, dtype)

    results = pl.pallas_call(
        functools.partial(kernel, INPUTS + OUTPUTS + tuple(scratch), n_dom, n_rep),
        out_shape=(shape((atoms, channels), BF16), shape((3, atoms), F32), shape((6, atoms), F32),
                   shape((mix_rows, mix_cols), F32)),
        in_specs=[HBM] * len(INPUTS),
        out_specs=(VMEM,) * 4,
        scratch_shapes=list(scratch.values()),
        compiler_params=pltpu.CompilerParams(collective_id=0, has_side_effects=True, vmem_limit_bytes=48 << 20),
        name="layer",
    )(*[pltpu.with_memory_space_constraint(a, pltpu.HBM) for a in (
        features, positions, send_rows, radial, mixing, readout_row, decay, pair_home, pair_other, pair_kind,
        pair_image, *pair_rows)])
    return pl.pallas_call(
        copy_out,
        out_shape=tuple(shape(a.shape, a.dtype) for a in results),
        in_specs=[VMEM] * 4,
        out_specs=(HBM,) * 4,
        scratch_shapes=[dma((4,))],
        compiler_params=pltpu.CompilerParams(vmem_limit_bytes=4 << 20),
        name="copy_out",
    )(*results)


def solution(mesh):
    in_specs = (
        P("dom", None),
        P(None, "dom"),
        P(),
        P(),
        P(),
        P(),
        P(None, "dom"),
        P(("dom", "rep")),
        P(("dom", "rep")),
        P(("dom", "rep")),
        P(None, ("dom", "rep")),
    )
    out_specs = (P("dom", None), P(None, "dom"), P(None, "dom"), P("dom", "rep"))
    body = functools.partial(on_device, mesh.shape["dom"], mesh.shape["rep"])
    return jax.shard_map(body, mesh=mesh, in_specs=in_specs, out_specs=out_specs, check_vma=False)
```

```python
import functools
import types

import jax
import jax.numpy as jnp
from jax import lax
from jax.experimental import pallas as pl
from jax.experimental.pallas import tpu as pltpu
from jax.sharding import PartitionSpec as P

TILE = 128
OFFSETS = (1, -1, 2, -2)
CELL = 2.0
GROUP = 4
FORWARD_GROUP = 8
BACK_GROUP = 12
SPREAD_GROUP = 8
F32 = jnp.float32
BF16 = jnp.bfloat16
MESH = pl.DeviceIdType.MESH
VMEM = pl.BlockSpec(memory_space=pltpu.VMEM)
HBM = pl.BlockSpec(memory_space=pltpu.HBM)
INPUTS = ("feat_h", "pos_h", "rows_h", "radial_h", "mixing_h", "readout_h", "decay_h", "home_h", "other_h",
          "kind_h", "image_h", "home_row_h", "other_row_h", "kind_row_h")
OUTPUTS = ("out_feat", "out_force", "out_virial", "out_mix")


def nt(a, b):
    return lax.dot_general(a, b, (((1,), (1,)), ((), ())), preferred_element_type=F32)


def tn(a, b):
    return lax.dot_general(a, b, (((0,), (0,)), ((), ())), preferred_element_type=F32)


def mm(a, b):
    return jnp.dot(a, b, preferred_element_type=F32)


def split3(x):
    hi = x.astype(BF16)
    rest = x - hi.astype(F32)
    mid = rest.astype(BF16)
    low = (rest - mid.astype(F32)).astype(BF16)
    return hi, mid, low


def order_pairs(seg, lanes, subs):
    row = jnp.broadcast_to(seg, (TILE, TILE))
    col = jnp.transpose(row)
    before = (col < row) | ((col == row) & (subs < lanes))
    rank = jnp.sum(before.astype(jnp.int32), axis=0, keepdims=True)
    rank = jnp.transpose(jnp.broadcast_to(rank, (TILE, TILE)))
    order = jnp.sum(jnp.where(rank == lanes, subs, 0), axis=0, keepdims=True)
    upto = jnp.sum((col <= lanes).astype(jnp.int32), axis=0, keepdims=True)
    below = jnp.sum((col < lanes).astype(jnp.int32), axis=0, keepdims=True)
    return order, jnp.where(upto > below, upto, 0)


def kernel(names, n_dom, n_rep, *refs):
    m = types.SimpleNamespace(**dict(zip(names, refs)))
    d = lax.axis_index("dom")
    r = lax.axis_index("rep")
    y = lax.div(r, 2)
    c = lax.rem(r, 2)
    mate = 1 - c
    partner = r + 1 - 2 * c
    across = r + 2 - 4 * y
    atoms, channels = m.feat.shape
    own = atoms // TILE
    pairs = m.home.shape[0]
    kinds = m.radial.shape[0]
    n_ext = m.tiles.shape[0]

    def dom_at(o):
        return lax.rem(d + o + n_dom, n_dom)

    def at(dom, rep):
        return {"dom": dom, "rep": rep}

    loads = [pltpu.make_async_copy(src, dst, m.load.at[i]) for i, (src, dst) in enumerate((
        (m.rows_h, m.rows), (m.feat_h, m.feat), (m.pos_h, m.pos), (m.home_row_h, m.home_row),
        (m.other_row_h, m.other_row), (m.kind_row_h, m.kind_row), (m.radial_h, m.radial), (m.decay_h, m.decay),
        (m.home_h, m.home), (m.other_h, m.other), (m.kind_h, m.kind), (m.image_h, m.image),
        (m.mixing_h, m.mixing), (m.readout_h, m.readout)))]
    for copy in loads[:3]:
        copy.start()
    barrier = pltpu.get_barrier_semaphore()
    mine = (c + 1, -(c + 1))
    theirs = (2 - c, c - 2)
    peers = [lax.rem(r + i, n_rep) for i in range(1, n_rep)]

    def hello(dom, rep):
        pl.semaphore_signal(barrier, inc=1, device_id=at(dom, rep), device_id_type=MESH)

    def greet(i, _):
        hello(lax.rem(d + i, n_dom), r)
        return 0

    lax.fori_loop(1, n_dom, greet, 0)
    for o in mine:
        hello(dom_at(o), partner)
        hello(dom_at(o), across)
    for o in theirs:
        hello(dom_at(o), partner)
    for q in peers:
        hello(d, q)
    for copy in loads[3:]:
        copy.start()

    started = []

    def push(src, dst, ss, rs, target):
        copy = pltpu.make_async_remote_copy(src, dst, ss, rs, device_id=target, device_id_type=MESH)
        copy.start()
        started.append(copy)

    def take(dst, ss, rs):
        pltpu.make_async_remote_copy(dst, dst, ss, rs, device_id=at(d, partner), device_id_type=MESH).wait_recv()

    for copy in loads[:3]:
        copy.wait()
    iota = lax.broadcasted_iota(jnp.int32, (atoms, TILE), 0)
    hots = []
    for q in range(2):
        hot = (iota == m.rows[pl.ds(2 * c + q, 1), :]).astype(F32)
        hots.append(hot.astype(BF16))
        m.sendp[q] = jnp.dot(m.pos[...], hot, precision=lax.Precision.HIGHEST, preferred_element_type=F32)
    for q in range(2):
        m.sendf[q] = tn(hots[q], m.feat[...]).astype(BF16)
    for copy in loads[3:6]:
        copy.wait()
    m.raw[...] = jnp.zeros_like(m.raw)
    for i, src in enumerate((m.home_row, m.kind_row, m.other_row)):
        m.raw[i:i + 1, :pairs] = src[...]
    raw = m.raw[...]
    lanes = lax.broadcasted_iota(jnp.int32, (TILE, TILE), 1)
    subs = lax.broadcasted_iota(jnp.int32, (TILE, TILE), 0)
    real = lanes[0:1] < pairs
    order_f, end_f = order_pairs(jnp.where(real, raw[0:1] * kinds + raw[1:2], TILE), lanes, subs)
    order_b, end_b = order_pairs(jnp.where(real, raw[2:3], TILE), lanes, subs)
    m.plan_v[...] = jnp.concatenate(
        [order_f, order_b, end_f, end_b, jnp.zeros((4, TILE), jnp.int32)], axis=0)
    plan_copy = pltpu.make_async_copy(m.plan_v, m.plan, m.s_plan)
    plan_copy.start()

    def columns(j):
        for x in range(3):
            m.col[j, x] = jnp.transpose(jnp.broadcast_to(m.tiles[j][x:x + 1, :], (TILE, TILE)))

    def table(j):
        pos = m.tiles[j]
        x, yy, z = pos[0:1, :], pos[1:2, :], pos[2:3, :]
        zero = jnp.zeros((2, TILE), F32)
        one_rows = jnp.concatenate([x, yy, z, x, x, yy, zero], axis=0)
        two_rows = jnp.concatenate([x, yy, z, yy, z, z, zero], axis=0)
        m.first[j] = one_rows
        m.second[j] = two_rows
        stack = jnp.concatenate([one_rows * two_rows, one_rows, two_rows], axis=0)
        parts = [v.astype(F32) for v in split3(stack)]
        m.moments[j] = jnp.concatenate(
            [parts[0], jnp.ones((8, TILE), F32), parts[1], parts[2]], axis=0).astype(BF16)

    for j in range(own):
        m.tiles[j] = m.pos[:, j * TILE:(j + 1) * TILE]
        m.ext[j] = m.feat[j * TILE:(j + 1) * TILE, :]
        columns(j)
    pl.semaphore_wait(barrier, 6 + n_rep - 1 + n_dom - 1)
    for q in range(2):
        for i, rep in enumerate((r, partner)):
            push(m.sendp.at[q], m.recvp.at[2 * c + q], m.s_pos.at[q, i], m.r_pos.at[2 * c + q],
                 at(dom_at(mine[q]), rep))
    for q in range(2):
        push(m.sendf.at[q], m.ext.at[own + 2 * c + q], m.s_feat.at[q], m.r_feat.at[2 * c + q],
             at(dom_at(mine[q]), r))

    m.sums[0] = jnp.zeros_like(m.sums[0])
    m.far[0] = jnp.zeros_like(m.far[0])
    m.near[...] = jnp.zeros_like(m.near)
    m.eye[...] = (lax.broadcasted_iota(jnp.int32, m.eye.shape, 0)
                  == lax.broadcasted_iota(jnp.int32, m.eye.shape, 1)).astype(F32).astype(BF16)
    for j in range(own):
        table(j)
    for copy in loads[6:]:
        copy.wait()
    for t in range(4):
        take(m.recvp.at[t], m.s_pos.at[0, 0], m.r_pos.at[t])
        m.tiles[own + t] = m.recvp[t]

    def kernels(g, _):
        for u in range(GROUP):
            p = g * GROUP + u
            h, o, k = m.home[p], m.other[p], m.kind[p]
            row = m.tiles[o]
            d2 = None
            for x in range(3):
                sep = (row[x:x + 1, :] + m.image[x, p].astype(F32) * CELL) - m.col[h, x]
                d2 = sep * sep if d2 is None else d2 + sep * sep
            m.kern_ab[p] = jnp.exp(d2 * (-m.decay[k])).astype(BF16)
        return 0

    def transposed(g, _):
        for u in range(GROUP):
            p = g * GROUP + u
            h, o, k = m.home[p], m.other[p], m.kind[p]
            row = m.tiles[h]
            d2 = None
            for x in range(3):
                sep = m.col[o, x] - (row[x:x + 1, :] - m.image[x, p].astype(F32) * CELL)
                d2 = sep * sep if d2 is None else d2 + sep * sep
            m.kern_ba[p] = jnp.exp(d2 * (-m.decay[k]))
        return 0

    half_steps = pairs // GROUP // 2
    lax.fori_loop(0, half_steps, kernels, 0)
    for q in range(2):
        t = 2 * c + q
        take(m.ext.at[own + t], m.s_feat.at[q], m.r_feat.at[t])
        push(m.ext.at[own + t], m.ext.at[own + t], m.s_relay.at[q], m.r_relay.at[t], at(d, partner))
    lax.fori_loop(half_steps, pairs // GROUP, kernels, 0)
    plan_copy.wait()
    for q in range(2):
        t = 2 * mate + q
        take(m.ext.at[own + t], m.s_relay.at[q], m.r_relay.at[t])

    def pair_at(row, i):
        return jnp.clip(m.plan[row, i], 0, pairs - 1)

    def sum_at(row, i):
        return jnp.clip(m.plan[row, i], 0, pairs)

    def seg_f(p):
        return m.home[p] * kinds + m.kind[p]

    def forward(g, _):
        acc = m.sums[g * FORWARD_GROUP]
        for u in range(FORWARD_GROUP):
            i = g * FORWARD_GROUP + u
            p = pair_at(0, i)
            last = pair_at(0, jnp.maximum(i - 1, 0))
            keep = (seg_f(p) == seg_f(last)).astype(F32)
            acc = acc * keep + mm(m.kern_ab[p], m.ext[m.other[p]])
            m.sums[i + 1] = acc
        return 0

    lax.fori_loop(0, pairs // FORWARD_GROUP, forward, 0)

    def message(h):
        left = [m.sums[sum_at(2, h * kinds + k)].astype(BF16) for k in range(kinds)]
        return mm(jnp.concatenate(left, axis=1), m.radial[...].reshape(kinds * channels, channels))

    m.msg[...] = message(mate).astype(BF16)
    push(m.msg, m.msg_in, m.s_msg.at[0], m.r_msg.at[0], at(d, partner))
    value = message(c)
    for t in range(4):
        columns(own + t)
        table(own + t)
    take(m.msg_in, m.s_msg.at[0], m.r_msg.at[0])
    value = (value + m.msg_in[...].astype(F32)).astype(BF16)
    m.chip[...] = value
    push(m.chip, m.chip_in, m.s_msg.at[1], m.r_msg.at[1], at(d, across))
    lax.fori_loop(0, pairs // GROUP, transposed, 0)
    take(m.chip_in, m.s_msg.at[1], m.r_msg.at[1])
    low = (value.astype(F32) + m.chip_in[...].astype(F32)).astype(BF16)
    mixed = mm(low, m.mixing[...])
    sig = jax.nn.sigmoid(mixed)
    slope = (m.readout[...] * sig * (1.0 + mixed * (1.0 - sig))).astype(BF16)
    adj = nt(slope, m.mixing[...]).astype(BF16)
    m.adjoint[c] = adj
    push(m.adjoint.at[c], m.adjoint.at[c], m.s_adj.at[0], m.r_adj.at[0], at(d, partner))
    m.slope[c] = slope
    push(m.slope.at[c], m.slope.at[c], m.s_adj.at[1], m.r_adj.at[1], at(d, partner))
    m.packed[c] = low
    push(m.packed.at[c], m.packed.at[c], m.s_adj.at[2], m.r_adj.at[2], at(d, partner))

    def spread(h):
        value = m.adjoint[h]
        for k in range(kinds):
            m.weights[h * kinds + k] = nt(value, m.radial[k]).astype(BF16)

    spread(c)
    take(m.adjoint.at[mate], m.s_adj.at[0], m.r_adj.at[0])
    spread(mate)

    sub = lax.broadcasted_iota(jnp.int32, (8, TILE), 0)
    is_x1, is_y1 = (sub == 0) | (sub == 3) | (sub == 4), (sub == 1) | (sub == 5)
    is_x2, is_y2 = (sub == 0), (sub == 1) | (sub == 3)

    def combine(res, a, b):
        quad = res[0:8] + res[32:40] + res[56:64]
        lin1 = res[8:16] + res[40:48] + res[64:72]
        lin2 = res[16:24] + res[48:56] + res[72:80]
        one = res[24:32]
        force = lin1 - a * one
        virial = -0.5 * (quad - a * lin2 - b * lin1 + a * b * one)
        return jnp.concatenate([force, virial], axis=0)

    def pair_b(i):
        p = pair_at(1, i)
        last = pair_at(1, jnp.maximum(i - 1, 0))
        keep = (m.other[p] == m.other[last]).astype(F32)
        return p, m.home[p], m.other[p], m.kind[p], keep

    def spread_back(g, _):
        acc = m.sums[g * SPREAD_GROUP]
        for u in range(SPREAD_GROUP):
            i = g * SPREAD_GROUP + u
            p, h, _, k, keep = pair_b(i)
            acc = acc * keep + mm(m.kern_ba[p].astype(BF16), m.weights[h * kinds + k])
            m.sums[i + 1] = acc
        return 0

    def backward(g, _):
        found = []
        for u in range(BACK_GROUP):
            i = g * BACK_GROUP + u
            p, h, o, k, keep = pair_b(i)
            grad = nt(m.ext[o], m.weights[h * kinds + k])
            found.append((i, p, h, o, keep, ((-2.0 * m.decay[k]) * m.kern_ba[p] * grad).astype(BF16)))
        far = m.far[g * BACK_GROUP]
        near = [m.near[j] for j in range(own)]
        for i, p, h, o, keep, weight in found:
            shift = [m.image[x, p].astype(F32) * CELL for x in range(3)]
            s1 = jnp.where(is_x1, shift[0], jnp.where(is_y1, shift[1], shift[2]))
            s2 = jnp.where(is_x2, shift[0], jnp.where(is_y2, shift[1], shift[2]))
            near_side = combine(mm(m.moments[o], weight), m.first[h] - s1, m.second[h] - s2)
            far_side = combine(nt(m.moments[h], weight), m.first[o] + s1, m.second[o] + s2)
            for j in range(own):
                near[j] = near[j] + near_side * (h == j).astype(F32)
            far = far * keep + far_side
            m.far[i + 1] = far
        for j in range(own):
            m.near[j] = near[j]
        return 0

    lax.fori_loop(0, pairs // SPREAD_GROUP, spread_back, 0)

    share = channels // n_rep
    away = ((1, 2 + 2 * mate), (2, 3 + 2 * mate), (0, mate))
    held = ((1, 2 + 2 * c), (2, 3 + 2 * c), (0, c))

    def settle(slots):
        total = jnp.concatenate([m.sums[sum_at(3, j)].astype(BF16) for _, j in slots], axis=0)
        turned = nt(m.eye[:channels, :channels], total).astype(BF16)
        for i, (_, j) in enumerate(slots):
            m.gfeat[j] = turned[:, i * TILE:(i + 1) * TILE].reshape(n_rep, share, TILE)

    settle(away)
    for slot, j in away:
        push(m.gfeat.at[j], m.gp.at[slot], m.s_gp.at[slot], m.r_gp.at[slot], at(d, partner))
    settle(held)
    half_back = pairs // BACK_GROUP // 2
    lax.fori_loop(0, half_back, backward, 0)
    for slot, j in held:
        take(m.gp.at[slot], m.s_gp.at[slot], m.r_gp.at[slot])
        m.sb[slot] = (m.gfeat[j].astype(F32) + m.gp[slot].astype(F32)).astype(BF16)
        if slot:
            t = 2 * c + slot - 1
            for q in range(n_rep):
                push(m.sb.at[slot, q], m.rf.at[t, y], m.s_rf.at[slot - 1, q], m.r_rf.at[t, y],
                     at(dom_at(-mine[slot - 1]), q))
    for i, q in enumerate(peers):
        push(m.sb.at[0, q], m.ro.at[c, y], m.s_ro.at[i], m.r_ro.at[c, y], at(d, q))
    m.ro[c, y] = m.sb[0, r]
    lax.fori_loop(half_back, pairs // BACK_GROUP, backward, 0)
    def settle_side(slot, j):
        m.side[j] = m.far[sum_at(3, j)] if slot else m.far[sum_at(3, j)] + m.near[j]

    for slot, j in away:
        settle_side(slot, j)
        push(m.side.at[j], m.gs.at[slot], m.s_gs.at[slot], m.r_gs.at[slot], at(d, partner))
    for slot, j in held:
        settle_side(slot, j)
    take(m.slope.at[mate], m.s_adj.at[1], m.r_adj.at[1])
    take(m.packed.at[mate], m.s_adj.at[2], m.r_adj.at[2])
    pick = (lax.broadcasted_iota(jnp.int32, (channels, share), 0)
            == lax.broadcasted_iota(jnp.int32, (channels, share), 1) + r * share).astype(BF16)
    cols = mm(m.slope[...].reshape(atoms, channels), pick).astype(BF16)
    m.mix[...] = tn(m.packed[...].reshape(atoms, channels), cols).reshape(m.mix.shape)
    for slot, j in held:
        take(m.gs.at[slot], m.s_gs.at[slot], m.r_gs.at[slot])
        m.ss[slot] = m.side[j] + m.gs[slot]
        for half in ((0, 1) if slot else (1 - y,)):
            dest = at(dom_at(-mine[slot - 1]) if slot else d, 2 * half + c)
            push(m.ss.at[slot], m.rs.at[slot, y], m.s_rs.at[slot, half], m.r_rs.at[slot, y], dest)

    def mix_copy(i):
        to = lax.rem(d + i, n_dom)
        return pltpu.make_async_remote_copy(m.mix.at[to], m.rm.at[d], m.s_mix.at[i], m.r_mix.at[d],
                                            device_id=at(to, r), device_id_type=MESH)

    lax.fori_loop(1, n_dom, lambda i, _: (mix_copy(i).start(), 0)[1], 0)
    for q in peers:
        take(m.ro.at[lax.rem(q, 2), lax.div(q, 2)], m.s_ro.at[0], m.r_ro.at[lax.rem(q, 2), lax.div(q, 2)])
    total = jnp.concatenate([m.ro[j, 0].astype(F32) + m.ro[j, 1].astype(F32) for j in range(own)], axis=1)
    for t in range(4):
        hot = (iota == m.rows[t:t + 1, :]).astype(F32).astype(BF16)
        for s in range(2):
            take(m.rf.at[t, s], m.s_rf.at[0, 0], m.r_rf.at[t, s])
        both = nt(m.rf[t].reshape(2 * share, TILE), hot)
        total = total + (both[:share] + both[share:])
    m.part[r] = total.astype(BF16)
    for i, q in enumerate(peers):
        push(m.part.at[r], m.part.at[r], m.s_part.at[i], m.r_part.at[r], at(d, q))
    take(m.rs.at[0, 1 - y], m.s_rs.at[0, 0], m.r_rs.at[0, 1 - y])
    side_self = m.ss[0] + m.rs[0, 1 - y]
    is_low = c == 0
    zside = jnp.zeros_like(side_self)
    total_side = jnp.concatenate([jnp.where(is_low, side_self, zside), jnp.where(is_low, zside, side_self)],
                                 axis=1)
    for q in range(2):
        hot = (iota == m.rows[pl.ds(2 * c + q, 1), :]).astype(F32).astype(BF16)
        slot = 1 + q
        for s in range(2):
            take(m.rs.at[slot, s], m.s_rs.at[0, 0], m.r_rs.at[slot, s])
        for v in split3(m.rs[slot, 0] + m.rs[slot, 1]):
            total_side = total_side + nt(v, hot)
    m.pside[...] = total_side
    push(m.pside, m.qside, m.s_side, m.r_side, at(d, partner))

    def mix_add(i, value):
        frm = lax.rem(d + i, n_dom)
        take(m.rm.at[frm], m.s_mix.at[0], m.r_mix.at[frm])
        return value + m.rm[frm]

    m.out_mix[...] = lax.fori_loop(1, n_dom, mix_add, m.mix[d])
    take(m.qside, m.s_side, m.r_side)
    final = total_side + m.qside[...]
    m.out_force[...] = final[0:3]
    m.out_virial[...] = final[8:14]
    for q in peers:
        take(m.part.at[q], m.s_part.at[0], m.r_part.at[q])
    m.out_feat[...] = nt(m.eye[:atoms, :atoms], m.part[...].reshape(channels, atoms)).astype(BF16)
    for copy in started:
        copy.wait_send()
    lax.fori_loop(1, n_dom, lambda i, _: (mix_copy(i).wait_send(), 0)[1], 0)


def copy_out(a, b, c, d, a_h, b_h, c_h, d_h, sem):
    copies = [pltpu.make_async_copy(src, dst, sem.at[i])
              for i, (src, dst) in enumerate(((a, a_h), (b, b_h), (c, c_h), (d, d_h)))]
    for copy in copies:
        copy.start()
    for copy in copies:
        copy.wait()


def on_device(n_dom, n_rep, features, positions, radial, mixing, readout, decay, send_rows, pair_home,
              pair_other, pair_kind, pair_image):
    atoms, channels = features.shape
    own = atoms // TILE
    n_ext = own + len(OFFSETS)
    kinds = radial.shape[0]
    pairs = pair_home.shape[0]
    dma = pltpu.SemaphoreType.DMA
    mix_rows, mix_cols = channels // n_dom, channels // n_rep
    quarters = (n_rep, channels // n_rep, TILE)
    readout_row = readout.reshape(1, channels)
    pair_rows = [a.reshape(1, pairs) for a in (pair_home, pair_other, pair_kind)]

    scratch = {
        "feat": pltpu.VMEM(features.shape, BF16), "pos": pltpu.VMEM(positions.shape, F32),
        "rows": pltpu.VMEM(send_rows.shape, jnp.int32), "radial": pltpu.VMEM(radial.shape, BF16),
        "mixing": pltpu.VMEM(mixing.shape, BF16), "readout": pltpu.VMEM(readout_row.shape, F32),
        "decay": pltpu.SMEM(decay.shape, F32), "home": pltpu.SMEM(pair_home.shape, jnp.int32),
        "other": pltpu.SMEM(pair_other.shape, jnp.int32), "kind": pltpu.SMEM(pair_kind.shape, jnp.int32),
        "image": pltpu.SMEM(pair_image.shape, jnp.int32),
        "home_row": pltpu.VMEM((1, pairs), jnp.int32), "other_row": pltpu.VMEM((1, pairs), jnp.int32),
        "kind_row": pltpu.VMEM((1, pairs), jnp.int32),
        "raw": pltpu.VMEM((8, TILE), jnp.int32), "plan_v": pltpu.VMEM((8, TILE), jnp.int32),
        "plan": pltpu.SMEM((8, TILE), jnp.int32),
        "sendf": pltpu.VMEM((2, TILE, channels), BF16), "sendp": pltpu.VMEM((2, 3, TILE), F32),
        "recvp": pltpu.VMEM((4, 3, TILE), F32), "ext": pltpu.VMEM((n_ext, TILE, channels), BF16),
        "tiles": pltpu.VMEM((n_ext, 3, TILE), F32), "col": pltpu.VMEM((n_ext, 3, TILE, TILE), F32),
        "moments": pltpu.VMEM((n_ext, 80, TILE), BF16),
        "first": pltpu.VMEM((n_ext, 8, TILE), F32), "second": pltpu.VMEM((n_ext, 8, TILE), F32),
        "kern_ab": pltpu.VMEM((pairs, TILE, TILE), BF16), "kern_ba": pltpu.VMEM((pairs, TILE, TILE), F32),
        "sums": pltpu.VMEM((pairs + 1, TILE, channels), F32), "far": pltpu.VMEM((pairs + 1, 16, TILE), F32),
        "near": pltpu.VMEM((own, 16, TILE), F32),
        "msg": pltpu.VMEM((TILE, channels), BF16), "msg_in": pltpu.VMEM((TILE, channels), BF16),
        "chip": pltpu.VMEM((TILE, channels), BF16), "chip_in": pltpu.VMEM((TILE, channels), BF16),
        "adjoint": pltpu.VMEM((own, TILE, channels), BF16), "slope": pltpu.VMEM((own, TILE, channels), BF16),
        "packed": pltpu.VMEM((own, TILE, channels), BF16),
        "weights": pltpu.VMEM((own * kinds, TILE, channels), BF16),
        "gfeat": pltpu.VMEM((n_ext, *quarters), BF16), "side": pltpu.VMEM((n_ext, 16, TILE), F32),
        "gp": pltpu.VMEM((3, *quarters), BF16), "gs": pltpu.VMEM((3, 16, TILE), F32),
        "sb": pltpu.VMEM((3, *quarters), BF16), "ss": pltpu.VMEM((3, 16, TILE), F32),
        "rf": pltpu.VMEM((4, 2, *quarters[1:]), BF16), "ro": pltpu.VMEM((own, 2, *quarters[1:]), BF16), "rs": pltpu.VMEM((3, 2, 16, TILE), F32),
        "mix": pltpu.VMEM((n_dom, mix_rows, mix_cols), F32), "rm": pltpu.VMEM((n_dom, mix_rows, mix_cols), F32),
        "part": pltpu.VMEM((n_rep, channels // n_rep, atoms), BF16),
        "eye": pltpu.VMEM((max(atoms, channels),) * 2, BF16),
        "pside": pltpu.VMEM((16, atoms), F32), "qside": pltpu.VMEM((16, atoms), F32),
        "load": dma((len(INPUTS),)), "s_plan": dma, "s_pos": dma((2, 2)), "r_pos": dma((4,)),
        "s_feat": dma((2,)), "r_feat": dma((4,)), "s_relay": dma((2,)), "r_relay": dma((4,)),
        "s_msg": dma((2,)), "r_msg": dma((2,)), "s_adj": dma((3,)), "r_adj": dma((3,)),
        "s_gp": dma((3,)), "r_gp": dma((3,)), "s_gs": dma((3,)), "r_gs": dma((3,)),
        "s_rf": dma((2, n_rep)), "r_rf": dma((4, 2)),
        "s_ro": dma((n_rep,)), "r_ro": dma((own, 2)), "s_rs": dma((3, 2)), "r_rs": dma((3, 2)),
        "s_mix": dma((n_dom,)), "r_mix": dma((n_dom,)), "s_part": dma((n_rep,)), "r_part": dma((n_rep,)),
        "s_side": dma, "r_side": dma,
    }

    def shape(dims, dtype):
        return jax.ShapeDtypeStruct(dims, dtype)

    results = pl.pallas_call(
        functools.partial(kernel, INPUTS + OUTPUTS + tuple(scratch), n_dom, n_rep),
        out_shape=(shape((atoms, channels), BF16), shape((3, atoms), F32), shape((6, atoms), F32),
                   shape((mix_rows, mix_cols), F32)),
        in_specs=[HBM] * len(INPUTS),
        out_specs=(VMEM,) * 4,
        scratch_shapes=list(scratch.values()),
        compiler_params=pltpu.CompilerParams(collective_id=0, has_side_effects=True, vmem_limit_bytes=48 << 20),
        name="layer",
    )(*[pltpu.with_memory_space_constraint(a, pltpu.HBM) for a in (
        features, positions, send_rows, radial, mixing, readout_row, decay, pair_home, pair_other, pair_kind,
        pair_image, *pair_rows)])
    return pl.pallas_call(
        copy_out,
        out_shape=tuple(shape(a.shape, a.dtype) for a in results),
        in_specs=[VMEM] * 4,
        out_specs=(HBM,) * 4,
        scratch_shapes=[dma((4,))],
        compiler_params=pltpu.CompilerParams(vmem_limit_bytes=4 << 20),
        name="copy_out",
    )(*results)


def solution(mesh):
    in_specs = (
        P("dom", None),
        P(None, "dom"),
        P(),
        P(),
        P(),
        P(),
        P(None, "dom"),
        P(("dom", "rep")),
        P(("dom", "rep")),
        P(("dom", "rep")),
        P(None, ("dom", "rep")),
    )
    out_specs = (P("dom", None), P(None, "dom"), P(None, "dom"), P("dom", "rep"))
    body = functools.partial(on_device, mesh.shape["dom"], mesh.shape["rep"])
    return jax.shard_map(body, mesh=mesh, in_specs=in_specs, out_specs=out_specs, check_vma=False)
```

```python
import functools
import types

import jax
import jax.numpy as jnp
from jax import lax
from jax.experimental import pallas as pl
from jax.experimental.pallas import tpu as pltpu
from jax.sharding import PartitionSpec as P

TILE = 128
OFFSETS = (1, -1, 2, -2)
CELL = 2.0
GROUP = 4
WIDE_GROUP = 24
BACK_GROUP = 12
LOG2E = 1.4426950408889634
F32 = jnp.float32
BF16 = jnp.bfloat16
MESH = pl.DeviceIdType.MESH
VMEM = pl.BlockSpec(memory_space=pltpu.VMEM)
HBM = pl.BlockSpec(memory_space=pltpu.HBM)
INPUTS = ("feat_h", "pos_h", "rows_h", "radial_h", "mixing_h", "readout_h", "decay_h", "home_h", "other_h",
          "kind_h", "image_h", "home_row_h", "other_row_h", "kind_row_h")
OUTPUTS = ("out_feat", "out_force", "out_virial", "out_mix")


def nt(a, b):
    return lax.dot_general(a, b, (((1,), (1,)), ((), ())), preferred_element_type=F32)


def tn(a, b):
    return lax.dot_general(a, b, (((0,), (0,)), ((), ())), preferred_element_type=F32)


def mm(a, b):
    return jnp.dot(a, b, preferred_element_type=F32)


def split3(x):
    hi = x.astype(BF16)
    rest = x - hi.astype(F32)
    mid = rest.astype(BF16)
    low = (rest - mid.astype(F32)).astype(BF16)
    return hi, mid, low


def order_pairs(seg, lanes, subs):
    row = jnp.broadcast_to(seg, (TILE, TILE))
    col = jnp.transpose(row)
    before = (col < row) | ((col == row) & (subs < lanes))
    rank = jnp.sum(before.astype(jnp.int32), axis=0, keepdims=True)
    rank = jnp.transpose(jnp.broadcast_to(rank, (TILE, TILE)))
    order = jnp.sum(jnp.where(rank == lanes, subs, 0), axis=0, keepdims=True)
    upto = jnp.sum((col <= lanes).astype(jnp.int32), axis=0, keepdims=True)
    below = jnp.sum((col < lanes).astype(jnp.int32), axis=0, keepdims=True)
    return order, jnp.where(upto > below, upto, 0)


def kernel(names, n_dom, n_rep, *refs):
    m = types.SimpleNamespace(**dict(zip(names, refs)))
    d = lax.axis_index("dom")
    r = lax.axis_index("rep")
    y = lax.div(r, 2)
    c = lax.rem(r, 2)
    mate = 1 - c
    partner = r + 1 - 2 * c
    across = r + 2 - 4 * y
    atoms, channels = m.feat.shape
    own = atoms // TILE
    late = lax.div(n_dom - 1 - d, n_dom // 2)
    pairs = m.home.shape[0]
    kinds = m.radial.shape[0]
    n_ext = m.tiles.shape[0]

    def dom_at(o):
        return lax.rem(d + o + n_dom, n_dom)

    def at(dom, rep):
        return {"dom": dom, "rep": rep}

    loads = [pltpu.make_async_copy(src, dst, m.load.at[i]) for i, (src, dst) in enumerate((
        (m.rows_h, m.rows), (m.feat_h, m.feat), (m.pos_h, m.pos), (m.home_row_h, m.home_row),
        (m.other_row_h, m.other_row), (m.kind_row_h, m.kind_row), (m.radial_h, m.radial), (m.decay_h, m.decay),
        (m.home_h, m.home), (m.other_h, m.other), (m.kind_h, m.kind), (m.image_h, m.image),
        (m.mixing_h, m.mixing), (m.readout_h, m.readout)))]
    for copy in loads[:3]:
        copy.start()
    barrier = pltpu.get_barrier_semaphore()
    mine = (c + 1, -(c + 1))
    theirs = (2 - c, c - 2)
    peers = [lax.rem(r + i, n_rep) for i in range(1, n_rep)]

    def hello(dom, rep):
        pl.semaphore_signal(barrier, inc=1, device_id=at(dom, rep), device_id_type=MESH)

    def greet(i, _):
        hello(lax.rem(d + i, n_dom), r)
        return 0

    lax.fori_loop(1, n_dom, greet, 0)
    for o in mine:
        hello(dom_at(o), partner)
        hello(dom_at(o), across)
    for o in theirs:
        hello(dom_at(o), partner)
    for q in peers:
        hello(d, q)
    for copy in loads[3:]:
        copy.start()

    started = []

    def push(src, dst, ss, rs, target):
        copy = pltpu.make_async_remote_copy(src, dst, ss, rs, device_id=target, device_id_type=MESH)
        copy.start()
        started.append(copy)

    def take(dst, ss, rs):
        pltpu.make_async_remote_copy(dst, dst, ss, rs, device_id=at(d, partner), device_id_type=MESH).wait_recv()

    for copy in loads[:3]:
        copy.wait()
    iota = lax.broadcasted_iota(jnp.int32, (atoms, TILE), 0)
    hots = []
    for q in range(2):
        hot = (iota == m.rows[pl.ds(2 * c + q, 1), :]).astype(F32)
        hots.append(hot.astype(BF16))
        m.sendp[q] = jnp.dot(m.pos[...], hot, precision=lax.Precision.HIGHEST, preferred_element_type=F32)
    for q in range(2):
        m.sendf[q] = tn(hots[q], m.feat[...]).astype(BF16)
    for copy in loads[3:6]:
        copy.wait()
    m.raw[...] = jnp.zeros_like(m.raw)
    for i, src in enumerate((m.home_row, m.kind_row, m.other_row)):
        m.raw[i:i + 1, :pairs] = src[...]
    raw = m.raw[...]
    lanes = lax.broadcasted_iota(jnp.int32, (TILE, TILE), 1)
    subs = lax.broadcasted_iota(jnp.int32, (TILE, TILE), 0)
    real = lanes[0:1] < pairs
    order_f, end_f = order_pairs(jnp.where(real, raw[0:1] * kinds + raw[1:2], TILE), lanes, subs)
    order_b, end_b = order_pairs(jnp.where(real, raw[2:3], TILE), lanes, subs)
    m.plan_v[...] = jnp.concatenate(
        [order_f, order_b, end_f, end_b, jnp.zeros((4, TILE), jnp.int32)], axis=0)
    plan_copy = pltpu.make_async_copy(m.plan_v, m.plan, m.s_plan)
    plan_copy.start()

    def columns(j):
        for x in range(3):
            m.col[j, x] = jnp.transpose(jnp.broadcast_to(m.tiles[j][x:x + 1, :], (TILE, TILE)))

    def table(j):
        pos = m.tiles[j]
        x, yy, z = pos[0:1, :], pos[1:2, :], pos[2:3, :]
        zero = jnp.zeros((2, TILE), F32)
        one_rows = jnp.concatenate([x, yy, z, x, x, yy, zero], axis=0)
        two_rows = jnp.concatenate([x, yy, z, yy, z, z, zero], axis=0)
        m.first[j] = one_rows
        m.second[j] = two_rows
        stack = jnp.concatenate([one_rows * two_rows, one_rows, two_rows], axis=0)
        parts = [v.astype(F32) for v in split3(stack)]
        stack = jnp.concatenate([parts[0], jnp.ones((8, TILE), F32), parts[1], parts[2]], axis=0).astype(BF16)
        m.moments[j] = stack
        if j < own:
            m.sided[j, 0] = jnp.concatenate([stack, jnp.zeros_like(stack)], axis=1)
            m.sided[j, 1] = jnp.concatenate([jnp.zeros_like(stack), stack], axis=1)

    for j in range(own):
        m.tiles[j] = m.pos[:, j * TILE:(j + 1) * TILE]
        m.ext[j] = m.feat[j * TILE:(j + 1) * TILE, :]
        columns(j)
    pl.semaphore_wait(barrier, 6 + n_rep - 1 + n_dom - 1)
    for q in (late, 1 - late):
        for i, rep in enumerate((r, partner)):
            push(m.sendp.at[q], m.recvp.at[2 * c + q], m.s_pos.at[q, i], m.r_pos.at[2 * c + q],
                 at(dom_at((c + 1) * (1 - 2 * q)), rep))
    for q in (late, 1 - late):
        push(m.sendf.at[q], m.ext.at[own + 2 * c + q], m.s_feat.at[q], m.r_feat.at[2 * c + q],
             at(dom_at((c + 1) * (1 - 2 * q)), r))

    m.sums[0] = jnp.zeros_like(m.sums[0])
    m.carry[...] = jnp.zeros_like(m.carry)
    for t in range(4):
        m.hot[:, t * TILE:(t + 1) * TILE] = (iota == m.rows[t:t + 1, :]).astype(F32).astype(BF16)
    m.far[0] = jnp.zeros_like(m.far[0])
    m.near[...] = jnp.zeros_like(m.near)
    m.eye[...] = (lax.broadcasted_iota(jnp.int32, m.eye.shape, 0)
                  == lax.broadcasted_iota(jnp.int32, m.eye.shape, 1)).astype(F32).astype(BF16)
    for j in range(own):
        table(j)
    for copy in loads[6:]:
        copy.wait()
    for t in range(4):
        take(m.recvp.at[t], m.s_pos.at[0, 0], m.r_pos.at[t])
        m.tiles[own + t] = m.recvp[t]

    def kernels(g, _):
        for u in range(GROUP):
            p = g * GROUP + u
            h, o, k = m.home[p], m.other[p], m.kind[p]
            row = m.tiles[o]
            d2 = None
            for x in range(3):
                sep = (row[x:x + 1, :] + m.image[x, p].astype(F32) * CELL) - m.col[h, x]
                d2 = sep * sep if d2 is None else d2 + sep * sep
            m.kern_ab[p] = jnp.exp2(d2 * (-LOG2E * m.decay[k])).astype(BF16)
        return 0

    def transposed(g, _):
        for u in range(GROUP):
            p = g * GROUP + u
            h, o, k = m.home[p], m.other[p], m.kind[p]
            row = m.tiles[h]
            d2 = None
            for x in range(3):
                sep = m.col[o, x] - (row[x:x + 1, :] - m.image[x, p].astype(F32) * CELL)
                d2 = sep * sep if d2 is None else d2 + sep * sep
            m.kern_ba[p] = jnp.exp2(d2 * (-LOG2E * m.decay[k]))
        return 0

    half_steps = pairs // GROUP // 2
    lax.fori_loop(0, half_steps, kernels, 0)
    for q in range(2):
        t = 2 * c + q
        take(m.ext.at[own + t], m.s_feat.at[q], m.r_feat.at[t])
        push(m.ext.at[own + t], m.ext.at[own + t], m.s_relay.at[q], m.r_relay.at[t], at(d, partner))
    lax.fori_loop(half_steps, pairs // GROUP, kernels, 0)
    plan_copy.wait()
    for q in range(2):
        t = 2 * mate + q
        take(m.ext.at[own + t], m.s_relay.at[q], m.r_relay.at[t])

    def pair_at(row, i):
        return jnp.clip(m.plan[row, i], 0, pairs - 1)

    def sum_at(row, i):
        return jnp.clip(m.plan[row, i], 0, pairs)

    def seg_f(p):
        return m.home[p] * kinds + m.kind[p]

    def forward(g, _):
        acc = m.carry[...]
        for u in range(WIDE_GROUP):
            i = g * WIDE_GROUP + u
            p = pair_at(0, i)
            last = pair_at(0, jnp.maximum(i - 1, 0))
            keep = (seg_f(p) == seg_f(last)).astype(F32)
            acc = acc * keep + mm(m.kern_ab[p], m.ext[m.other[p]])
            m.sums[i + 1] = acc.astype(BF16)
        m.carry[...] = acc
        return 0

    lax.fori_loop(0, pairs // WIDE_GROUP, forward, 0)

    def message(h):
        left = [m.sums[sum_at(2, h * kinds + k)] for k in range(kinds)]
        return mm(jnp.concatenate(left, axis=1), m.radial[...].reshape(kinds * channels, channels))

    m.msg[...] = message(mate).astype(BF16).reshape(m.msg.shape)
    for q in range(2):
        push(m.msg.at[q], m.msg_in.at[q], m.s_msg.at[q], m.r_msg.at[q], at(d, partner))
    value = message(c).reshape(m.msg.shape)
    for t in range(4):
        columns(own + t)
        table(own + t)
    for q in range(2):
        take(m.msg_in.at[q], m.s_msg.at[q], m.r_msg.at[q])
        m.chip[q] = (value[q] + m.msg_in[q].astype(F32)).astype(BF16)
        push(m.chip.at[q], m.chip_in.at[q], m.s_chip.at[q], m.r_chip.at[q], at(d, across))
    lax.fori_loop(0, pairs // GROUP, transposed, 0)
    for q in range(2):
        take(m.chip_in.at[q], m.s_chip.at[q], m.r_chip.at[q])
        low = (m.chip[q].astype(F32) + m.chip_in[q].astype(F32)).astype(BF16)
        mixed = mm(low, m.mixing[...])
        sig = jax.nn.sigmoid(mixed)
        slope = (m.readout[...] * sig * (1.0 + mixed * (1.0 - sig))).astype(BF16)
        m.adjoint[c, q] = nt(slope, m.mixing[...]).astype(BF16)
        push(m.adjoint.at[c, q], m.adjoint.at[c, q], m.s_adj.at[q], m.r_adj.at[q], at(d, partner))
        m.slope[c, q] = slope
        m.packed[c, q] = low
    push(m.slope.at[c], m.slope.at[c], m.s_adj.at[2], m.r_adj.at[2], at(d, partner))
    push(m.packed.at[c], m.packed.at[c], m.s_adj.at[3], m.r_adj.at[3], at(d, partner))

    def spread(h):
        value = m.adjoint[h].reshape(TILE, channels)
        for k in range(kinds):
            m.weights[h * kinds + k] = nt(value, m.radial[k]).astype(BF16)

    spread(c)
    for q in range(2):
        take(m.adjoint.at[mate, q], m.s_adj.at[q], m.r_adj.at[q])
    spread(mate)

    sub = lax.broadcasted_iota(jnp.int32, (8, TILE), 0)
    is_x1, is_y1 = (sub == 0) | (sub == 3) | (sub == 4), (sub == 1) | (sub == 5)
    is_x2, is_y2 = (sub == 0), (sub == 1) | (sub == 3)

    def combine(res, a, b):
        quad = res[0:8] + res[32:40] + res[56:64]
        lin1 = res[8:16] + res[40:48] + res[64:72]
        lin2 = res[16:24] + res[48:56] + res[72:80]
        one = res[24:32]
        force = lin1 - a * one
        virial = -0.5 * (quad - a * lin2 - b * lin1 + a * b * one)
        return jnp.concatenate([force, virial], axis=0)

    def pair_b(i):
        p = pair_at(1, i)
        last = pair_at(1, jnp.maximum(i - 1, 0))
        keep = (m.other[p] == m.other[last]).astype(F32)
        return p, m.home[p], m.other[p], m.kind[p], keep

    def spread_back(g, _):
        acc = m.carry[...]
        for u in range(WIDE_GROUP):
            i = g * WIDE_GROUP + u
            p, h, _, k, keep = pair_b(i)
            acc = acc * keep + mm(m.kern_ba[p].astype(BF16), m.weights[h * kinds + k])
            m.sums[i + 1] = acc.astype(BF16)
        m.carry[...] = acc
        return 0

    def backward(g, _):
        found = []
        for u in range(BACK_GROUP):
            i = g * BACK_GROUP + u
            p, h, o, k, keep = pair_b(i)
            grad = nt(m.ext[o], m.weights[h * kinds + k])
            found.append((i, p, h, o, keep, ((-2.0 * m.decay[k]) * m.kern_ba[p] * grad).astype(BF16)))
        far = m.far[g * BACK_GROUP]
        near = [m.near[j] for j in range(own)]
        results = []
        for one, two in zip(found[::2], found[1::2]):
            weight = jnp.concatenate([one[-1], two[-1]], axis=1)
            close = mm(jnp.concatenate([m.moments[one[3]], m.moments[two[3]]], axis=0), weight)
            beyond = nt(jnp.concatenate([m.sided[one[2], 0], m.sided[two[2], 1]], axis=0), weight)
            size = close.shape[0] // 2
            results += [(close[:size, :TILE], beyond[:size]), (close[size:, TILE:], beyond[size:])]
        for (i, p, h, o, keep, _), (close, beyond) in zip(found, results):
            shift = [m.image[x, p].astype(F32) * CELL for x in range(3)]
            s1 = jnp.where(is_x1, shift[0], jnp.where(is_y1, shift[1], shift[2]))
            s2 = jnp.where(is_x2, shift[0], jnp.where(is_y2, shift[1], shift[2]))
            near_side = combine(close, m.first[h] - s1, m.second[h] - s2)
            far_side = combine(beyond, m.first[o] + s1, m.second[o] + s2)
            for j in range(own):
                near[j] = near[j] + near_side * (h == j).astype(F32)
            far = far * keep + far_side
            m.far[i + 1] = far
        for j in range(own):
            m.near[j] = near[j]
        return 0

    m.carry[...] = jnp.zeros_like(m.carry)
    lax.fori_loop(0, pairs // WIDE_GROUP, spread_back, 0)

    share = channels // n_rep
    slots = (2 - late, 1 + late, 0)
    away = [(slot, own + 2 * mate + slot - 1) for slot in slots[:2]] + [(0, mate)]
    held = [(slot, own + 2 * c + slot - 1) for slot in slots[:2]] + [(0, c)]

    def settle(group):
        total = jnp.concatenate([m.sums[sum_at(3, j)] for _, j in group], axis=0)
        turned = nt(m.eye[:channels, :channels], total).astype(BF16)
        for i, (_, j) in enumerate(group):
            m.gfeat[j] = turned[:, i * TILE:(i + 1) * TILE].reshape(n_rep, share, TILE)

    settle(away)
    for slot, j in away:
        push(m.gfeat.at[j], m.gp.at[slot], m.s_gp.at[slot], m.r_gp.at[slot], at(d, partner))
    settle(held)
    lax.fori_loop(0, 1, backward, 0)
    for place, (slot, j) in enumerate(held):
        take(m.gp.at[slot], m.s_gp.at[slot], m.r_gp.at[slot])
        m.sb[slot] = (m.gfeat[j].astype(F32) + m.gp[slot].astype(F32)).astype(BF16)
        if place < 2:
            t = 2 * c + slot - 1
            for q in range(n_rep):
                push(m.sb.at[slot, q], m.rf.at[t, y], m.s_rf.at[slot - 1, q], m.r_rf.at[t, y],
                     at(dom_at((c + 1) * (2 * slot - 3)), q))
    for i, q in enumerate(peers):
        push(m.sb.at[0, q], m.ro.at[c, y], m.s_ro.at[i], m.r_ro.at[c, y], at(d, q))
    m.ro[c, y] = m.sb[0, r]
    lax.fori_loop(1, pairs // BACK_GROUP, backward, 0)
    for t, o in enumerate(OFFSETS):
        m.side[t] = m.far[sum_at(3, own + t)]
        push(m.side.at[t], m.rs.at[t], m.s_rs.at[t], m.r_rs.at[t], at(dom_at(-o), r))
    take(m.slope.at[mate], m.s_adj.at[2], m.r_adj.at[2])
    take(m.packed.at[mate], m.s_adj.at[3], m.r_adj.at[3])
    pick = (lax.broadcasted_iota(jnp.int32, (channels, share), 0)
            == lax.broadcasted_iota(jnp.int32, (channels, share), 1) + r * share).astype(BF16)
    cols = mm(m.slope[...].reshape(atoms, channels), pick).astype(BF16)
    m.mix[...] = tn(m.packed[...].reshape(atoms, channels), cols).reshape(m.mix.shape)
    def mix_copy(i):
        to = lax.rem(d + i, n_dom)
        return pltpu.make_async_remote_copy(m.mix.at[to], m.rm.at[d], m.s_mix.at[i], m.r_mix.at[d],
                                            device_id=at(to, r), device_id_type=MESH)

    lax.fori_loop(1, n_dom, lambda i, _: (mix_copy(i).start(), 0)[1], 0)
    for q in peers:
        take(m.ro.at[lax.rem(q, 2), lax.div(q, 2)], m.s_ro.at[0], m.r_ro.at[lax.rem(q, 2), lax.div(q, 2)])
    total = jnp.concatenate([m.ro[j, 0].astype(F32) + m.ro[j, 1].astype(F32) for j in range(own)], axis=1)
    for t in range(4):
        for q in range(2):
            take(m.rf.at[t, q], m.s_rf.at[0, 0], m.r_rf.at[t, q])
    both = nt(jnp.concatenate([m.rf[t].reshape(2 * share, TILE) for t in range(4)], axis=1), m.hot[...])
    m.part[r] = (total + (both[:share] + both[share:])).astype(BF16)
    for i, q in enumerate(peers):
        push(m.part.at[r], m.part.at[r], m.s_part.at[i], m.r_part.at[r], at(d, q))
    for t in range(4):
        take(m.rs.at[t], m.s_rs.at[t], m.r_rs.at[t])
    left = jnp.concatenate([jnp.concatenate(split3(m.rs[t]), axis=0) for t in range(4)], axis=1)
    spots = nt(left, m.hot[...])
    m.pside[r] = (jnp.concatenate([m.far[sum_at(3, j)] + m.near[j] for j in range(own)], axis=1)
                  + (spots[0:16] + spots[16:32] + spots[32:48]))
    for i, q in enumerate(peers):
        push(m.pside.at[r], m.pside.at[r], m.s_side.at[i], m.r_side.at[r], at(d, q))

    def mix_add(i, value):
        frm = lax.rem(d + i, n_dom)
        take(m.rm.at[frm], m.s_mix.at[0], m.r_mix.at[frm])
        return value + m.rm[frm]

    m.out_mix[...] = lax.fori_loop(1, n_dom, mix_add, m.mix[d])
    for q in peers:
        take(m.pside.at[q], m.s_side.at[0], m.r_side.at[q])
    final = (m.pside[0] + m.pside[1]) + (m.pside[2] + m.pside[3])
    m.out_force[...] = final[0:3]
    m.out_virial[...] = final[8:14]
    for q in peers:
        take(m.part.at[q], m.s_part.at[0], m.r_part.at[q])
    m.out_feat[...] = nt(m.eye[:atoms, :atoms], m.part[...].reshape(channels, atoms)).astype(BF16)
    for copy in started:
        copy.wait_send()
    lax.fori_loop(1, n_dom, lambda i, _: (mix_copy(i).wait_send(), 0)[1], 0)


def copy_out(a, b, c, d, a_h, b_h, c_h, d_h, sem):
    copies = [pltpu.make_async_copy(src, dst, sem.at[i])
              for i, (src, dst) in enumerate(((a, a_h), (b, b_h), (c, c_h), (d, d_h)))]
    for copy in copies:
        copy.start()
    for copy in copies:
        copy.wait()


def on_device(n_dom, n_rep, features, positions, radial, mixing, readout, decay, send_rows, pair_home,
              pair_other, pair_kind, pair_image):
    atoms, channels = features.shape
    own = atoms // TILE
    n_ext = own + len(OFFSETS)
    kinds = radial.shape[0]
    pairs = pair_home.shape[0]
    dma = pltpu.SemaphoreType.DMA
    mix_rows, mix_cols = channels // n_dom, channels // n_rep
    quarters = (n_rep, channels // n_rep, TILE)
    readout_row = readout.reshape(1, channels)
    pair_rows = [a.reshape(1, pairs) for a in (pair_home, pair_other, pair_kind)]

    scratch = {
        "feat": pltpu.VMEM(features.shape, BF16), "pos": pltpu.VMEM(positions.shape, F32),
        "rows": pltpu.VMEM(send_rows.shape, jnp.int32), "radial": pltpu.VMEM(radial.shape, BF16),
        "mixing": pltpu.VMEM(mixing.shape, BF16), "readout": pltpu.VMEM(readout_row.shape, F32),
        "decay": pltpu.SMEM(decay.shape, F32), "home": pltpu.SMEM(pair_home.shape, jnp.int32),
        "other": pltpu.SMEM(pair_other.shape, jnp.int32), "kind": pltpu.SMEM(pair_kind.shape, jnp.int32),
        "image": pltpu.SMEM(pair_image.shape, jnp.int32),
        "home_row": pltpu.VMEM((1, pairs), jnp.int32), "other_row": pltpu.VMEM((1, pairs), jnp.int32),
        "kind_row": pltpu.VMEM((1, pairs), jnp.int32),
        "raw": pltpu.VMEM((8, TILE), jnp.int32), "plan_v": pltpu.VMEM((8, TILE), jnp.int32),
        "plan": pltpu.SMEM((8, TILE), jnp.int32),
        "sendf": pltpu.VMEM((2, TILE, channels), BF16), "sendp": pltpu.VMEM((2, 3, TILE), F32),
        "recvp": pltpu.VMEM((4, 3, TILE), F32), "ext": pltpu.VMEM((n_ext, TILE, channels), BF16),
        "tiles": pltpu.VMEM((n_ext, 3, TILE), F32), "col": pltpu.VMEM((n_ext, 3, TILE, TILE), F32),
        "moments": pltpu.VMEM((n_ext, 80, TILE), BF16),
        "sided": pltpu.VMEM((own, 2, 80, 2 * TILE), BF16), "hot": pltpu.VMEM((atoms, 4 * TILE), BF16),
        "first": pltpu.VMEM((n_ext, 8, TILE), F32), "second": pltpu.VMEM((n_ext, 8, TILE), F32),
        "kern_ab": pltpu.VMEM((pairs, TILE, TILE), BF16), "kern_ba": pltpu.VMEM((pairs, TILE, TILE), F32),
        "sums": pltpu.VMEM((pairs + 1, TILE, channels), BF16),
        "carry": pltpu.VMEM((TILE, channels), F32), "far": pltpu.VMEM((pairs + 1, 16, TILE), F32),
        "near": pltpu.VMEM((own, 16, TILE), F32),
        "msg": pltpu.VMEM((2, TILE // 2, channels), BF16), "msg_in": pltpu.VMEM((2, TILE // 2, channels), BF16),
        "chip": pltpu.VMEM((2, TILE // 2, channels), BF16), "chip_in": pltpu.VMEM((2, TILE // 2, channels), BF16),
        "adjoint": pltpu.VMEM((own, 2, TILE // 2, channels), BF16), "slope": pltpu.VMEM((own, 2, TILE // 2, channels), BF16),
        "packed": pltpu.VMEM((own, 2, TILE // 2, channels), BF16),
        "weights": pltpu.VMEM((own * kinds, TILE, channels), BF16),
        "gfeat": pltpu.VMEM((n_ext, *quarters), BF16), "side": pltpu.VMEM((4, 16, TILE), F32),
        "gp": pltpu.VMEM((3, *quarters), BF16),
        "sb": pltpu.VMEM((3, *quarters), BF16),
        "rf": pltpu.VMEM((4, 2, *quarters[1:]), BF16), "ro": pltpu.VMEM((own, 2, *quarters[1:]), BF16), "rs": pltpu.VMEM((4, 16, TILE), F32),
        "mix": pltpu.VMEM((n_dom, mix_rows, mix_cols), F32), "rm": pltpu.VMEM((n_dom, mix_rows, mix_cols), F32),
        "part": pltpu.VMEM((n_rep, channels // n_rep, atoms), BF16),
        "eye": pltpu.VMEM((max(atoms, channels),) * 2, BF16),
        "pside": pltpu.VMEM((n_rep, 16, atoms), F32),
        "load": dma((len(INPUTS),)), "s_plan": dma, "s_pos": dma((2, 2)), "r_pos": dma((4,)),
        "s_feat": dma((2,)), "r_feat": dma((4,)), "s_relay": dma((2,)), "r_relay": dma((4,)),
        "s_msg": dma((2,)), "r_msg": dma((2,)), "s_chip": dma((2,)), "r_chip": dma((2,)), "s_adj": dma((4,)), "r_adj": dma((4,)),
        "s_gp": dma((3,)), "r_gp": dma((3,)),
        "s_rf": dma((2, n_rep)), "r_rf": dma((4, 2)),
        "s_ro": dma((n_rep,)), "r_ro": dma((own, 2)), "s_rs": dma((4,)), "r_rs": dma((4,)),
        "s_mix": dma((n_dom,)), "r_mix": dma((n_dom,)), "s_part": dma((n_rep,)), "r_part": dma((n_rep,)),
        "s_side": dma((n_rep,)), "r_side": dma((n_rep,)),
    }

    def shape(dims, dtype):
        return jax.ShapeDtypeStruct(dims, dtype)

    results = pl.pallas_call(
        functools.partial(kernel, INPUTS + OUTPUTS + tuple(scratch), n_dom, n_rep),
        out_shape=(shape((atoms, channels), BF16), shape((3, atoms), F32), shape((6, atoms), F32),
                   shape((mix_rows, mix_cols), F32)),
        in_specs=[HBM] * len(INPUTS),
        out_specs=(VMEM,) * 4,
        scratch_shapes=list(scratch.values()),
        compiler_params=pltpu.CompilerParams(collective_id=0, has_side_effects=True, vmem_limit_bytes=48 << 20),
        name="layer",
    )(*[pltpu.with_memory_space_constraint(a, pltpu.HBM) for a in (
        features, positions, send_rows, radial, mixing, readout_row, decay, pair_home, pair_other, pair_kind,
        pair_image, *pair_rows)])
    return pl.pallas_call(
        copy_out,
        out_shape=tuple(shape(a.shape, a.dtype) for a in results),
        in_specs=[VMEM] * 4,
        out_specs=(HBM,) * 4,
        scratch_shapes=[dma((4,))],
        compiler_params=pltpu.CompilerParams(vmem_limit_bytes=4 << 20),
        name="copy_out",
    )(*results)


def solution(mesh):
    in_specs = (
        P("dom", None),
        P(None, "dom"),
        P(),
        P(),
        P(),
        P(),
        P(None, "dom"),
        P(("dom", "rep")),
        P(("dom", "rep")),
        P(("dom", "rep")),
        P(None, ("dom", "rep")),
    )
    out_specs = (P("dom", None), P(None, "dom"), P(None, "dom"), P("dom", "rep"))
    body = functools.partial(on_device, mesh.shape["dom"], mesh.shape["rep"])
    return jax.shard_map(body, mesh=mesh, in_specs=in_specs, out_specs=out_specs, check_vma=False)
```

```python
import functools
import types

import jax
import jax.numpy as jnp
from jax import lax
from jax.experimental import pallas as pl
from jax.experimental.pallas import tpu as pltpu
from jax.sharding import PartitionSpec as P

TILE = 128
OFFSETS = (1, -1, 2, -2)
CELL = 2.0
GROUP = 4
WIDE_GROUP = 24
BACK_GROUP = 12
LOG2E = 1.4426950408889634
F32 = jnp.float32
BF16 = jnp.bfloat16
MESH = pl.DeviceIdType.MESH
VMEM = pl.BlockSpec(memory_space=pltpu.VMEM)
HBM = pl.BlockSpec(memory_space=pltpu.HBM)
INPUTS = ("feat_h", "pos_h", "rows_h", "radial_h", "mixing_h", "readout_h", "decay_h", "home_h", "other_h",
          "kind_h", "image_h", "home_row_h", "other_row_h", "kind_row_h")
OUTPUTS = ("out_feat", "out_force", "out_virial", "out_mix")


def nt(a, b):
    return lax.dot_general(a, b, (((1,), (1,)), ((), ())), preferred_element_type=F32)


def tn(a, b):
    return lax.dot_general(a, b, (((0,), (0,)), ((), ())), preferred_element_type=F32)


def mm(a, b):
    return jnp.dot(a, b, preferred_element_type=F32)


def split3(x):
    hi = x.astype(BF16)
    rest = x - hi.astype(F32)
    mid = rest.astype(BF16)
    low = (rest - mid.astype(F32)).astype(BF16)
    return hi, mid, low


def order_pairs(seg, lanes, subs):
    row = jnp.broadcast_to(seg, (TILE, TILE))
    col = jnp.transpose(row)
    before = (col < row) | ((col == row) & (subs < lanes))
    rank = jnp.sum(before.astype(jnp.int32), axis=0, keepdims=True)
    rank = jnp.transpose(jnp.broadcast_to(rank, (TILE, TILE)))
    order = jnp.sum(jnp.where(rank == lanes, subs, 0), axis=0, keepdims=True)
    upto = jnp.sum((col <= lanes).astype(jnp.int32), axis=0, keepdims=True)
    below = jnp.sum((col < lanes).astype(jnp.int32), axis=0, keepdims=True)
    return order, jnp.where(upto > below, upto, 0)


def kernel(names, n_dom, n_rep, *refs):
    m = types.SimpleNamespace(**dict(zip(names, refs)))
    d = lax.axis_index("dom")
    r = lax.axis_index("rep")
    y = lax.div(r, 2)
    c = lax.rem(r, 2)
    mate = 1 - c
    partner = r + 1 - 2 * c
    across = r + 2 - 4 * y
    atoms, channels = m.feat.shape
    own = atoms // TILE
    late = lax.div(n_dom - 1 - d, n_dom // 2)
    pairs = m.home.shape[0]
    kinds = m.radial.shape[0]
    n_ext = m.tiles.shape[0]

    def dom_at(o):
        return lax.rem(d + o + n_dom, n_dom)

    def at(dom, rep):
        return {"dom": dom, "rep": rep}

    groups = ((m.rows_h, m.rows), (m.feat_h, m.feat), (m.pos_h, m.pos)), (
        (m.home_row_h, m.home_row), (m.other_row_h, m.other_row), (m.kind_row_h, m.kind_row)), (
        (m.radial_h, m.radial), (m.decay_h, m.decay), (m.home_h, m.home), (m.other_h, m.other),
        (m.kind_h, m.kind), (m.image_h, m.image), (m.mixing_h, m.mixing), (m.readout_h, m.readout))
    loads = [[pltpu.make_async_copy(src, dst, m.load.at[i]) for src, dst in group]
             for i, group in enumerate(groups)]
    for copy in loads[0]:
        copy.start()
    barrier = pltpu.get_barrier_semaphore()
    mine = (c + 1, -(c + 1))
    theirs = (2 - c, c - 2)
    peers = [lax.rem(r + i, n_rep) for i in range(1, n_rep)]

    def hello(dom, rep):
        pl.semaphore_signal(barrier, inc=1, device_id=at(dom, rep), device_id_type=MESH)

    def greet(i, _):
        hello(lax.rem(d + i, n_dom), r)
        return 0

    lax.fori_loop(1, n_dom, greet, 0)
    for o in mine:
        hello(dom_at(o), partner)
    for o in theirs:
        hello(dom_at(o), partner)
    for q in peers:
        hello(d, q)
    for copy in loads[1] + loads[2]:
        copy.start()

    started = []

    def push(src, dst, rs, target):
        copy = pltpu.make_async_remote_copy(src, dst, m.sent, rs, device_id=target, device_id_type=MESH)
        copy.start()
        started.append(copy)

    def take(dst, rs):
        pltpu.make_async_remote_copy(dst, dst, m.sent, rs, device_id=at(d, partner), device_id_type=MESH).wait_recv()

    for copy in loads[0]:
        copy.wait()
    iota = lax.broadcasted_iota(jnp.int32, (atoms, TILE), 0)
    hots = []
    for q in range(2):
        hot = (iota == m.rows[pl.ds(2 * c + q, 1), :]).astype(F32)
        hots.append(hot.astype(BF16))
        m.sendp[q] = jnp.dot(m.pos[...], hot, precision=lax.Precision.HIGHEST, preferred_element_type=F32)
    for q in range(2):
        m.sendf[q] = tn(hots[q], m.feat[...]).astype(BF16)
    for copy in loads[1]:
        copy.wait()
    m.raw[...] = jnp.zeros_like(m.raw)
    for i, src in enumerate((m.home_row, m.kind_row, m.other_row)):
        m.raw[i:i + 1, :pairs] = src[...]
    raw = m.raw[...]
    lanes = lax.broadcasted_iota(jnp.int32, (TILE, TILE), 1)
    subs = lax.broadcasted_iota(jnp.int32, (TILE, TILE), 0)
    real = lanes[0:1] < pairs
    order_f, end_f = order_pairs(jnp.where(real, raw[0:1] * kinds + raw[1:2], TILE), lanes, subs)
    order_b, end_b = order_pairs(jnp.where(real, raw[2:3], TILE), lanes, subs)
    m.plan_v[...] = jnp.concatenate(
        [order_f, order_b, end_f, end_b, jnp.zeros((4, TILE), jnp.int32)], axis=0)
    plan_copy = pltpu.make_async_copy(m.plan_v, m.plan, m.s_plan)
    plan_copy.start()

    def columns(j):
        for x in range(3):
            m.col[j, x] = jnp.transpose(jnp.broadcast_to(m.tiles[j][x:x + 1, :], (TILE, TILE)))

    def table(j):
        pos = m.tiles[j]
        x, yy, z = pos[0:1, :], pos[1:2, :], pos[2:3, :]
        zero = jnp.zeros((2, TILE), F32)
        one_rows = jnp.concatenate([x, yy, z, x, x, yy, zero], axis=0)
        two_rows = jnp.concatenate([x, yy, z, yy, z, z, zero], axis=0)
        m.first[j] = one_rows
        m.second[j] = two_rows
        stack = jnp.concatenate([one_rows * two_rows, one_rows, two_rows], axis=0)
        parts = [v.astype(F32) for v in split3(stack)]
        stack = jnp.concatenate([parts[0], jnp.ones((8, TILE), F32), parts[1], parts[2]], axis=0).astype(BF16)
        m.moments[j] = stack
        if j < own:
            m.sided[j, 0] = jnp.concatenate([stack, jnp.zeros_like(stack)], axis=1)
            m.sided[j, 1] = jnp.concatenate([jnp.zeros_like(stack), stack], axis=1)

    for j in range(own):
        m.tiles[j] = m.pos[:, j * TILE:(j + 1) * TILE]
        m.ext[j] = m.feat[j * TILE:(j + 1) * TILE, :]
        columns(j)
    pl.semaphore_wait(barrier, 4 + n_rep - 1 + n_dom - 1)
    for q in (late, 1 - late):
        for i, rep in enumerate((r, partner)):
            push(m.sendp.at[q], m.recvp.at[2 * c + q], m.r_pos,
                 at(dom_at((c + 1) * (1 - 2 * q)), rep))
    for q in (late, 1 - late):
        push(m.sendf.at[q], m.ext.at[own + 2 * c + q], m.r_feat.at[q],
             at(dom_at((c + 1) * (1 - 2 * q)), r))

    for q in peers:
        pl.semaphore_signal(m.passed, inc=1, device_id=at(d, q), device_id_type=MESH)
    m.sums[0] = jnp.zeros_like(m.sums[0])
    m.carry[...] = jnp.zeros_like(m.carry)
    for t in range(4):
        m.hot[:, t * TILE:(t + 1) * TILE] = (iota == m.rows[t:t + 1, :]).astype(F32).astype(BF16)
    m.far[0] = jnp.zeros_like(m.far[0])
    m.near[...] = jnp.zeros_like(m.near)
    m.eye[...] = (lax.broadcasted_iota(jnp.int32, m.eye.shape, 0)
                  == lax.broadcasted_iota(jnp.int32, m.eye.shape, 1)).astype(F32).astype(BF16)
    for j in range(own):
        table(j)
    for copy in loads[2]:
        copy.wait()
    take(m.recvp, m.r_pos)
    for t in range(4):
        m.tiles[own + t] = m.recvp[t]

    def kernels(g, _):
        for u in range(GROUP):
            p = g * GROUP + u
            h, o, k = m.home[p], m.other[p], m.kind[p]
            row = m.tiles[o]
            d2 = None
            for x in range(3):
                sep = (row[x:x + 1, :] + m.image[x, p].astype(F32) * CELL) - m.col[h, x]
                d2 = sep * sep if d2 is None else d2 + sep * sep
            m.kern_ab[p] = jnp.exp2(d2 * (-LOG2E * m.decay[k])).astype(BF16)
        return 0

    def transposed(g, _):
        for u in range(GROUP):
            p = g * GROUP + u
            h, o, k = m.home[p], m.other[p], m.kind[p]
            row = m.tiles[h]
            d2 = None
            for x in range(3):
                sep = m.col[o, x] - (row[x:x + 1, :] - m.image[x, p].astype(F32) * CELL)
                d2 = sep * sep if d2 is None else d2 + sep * sep
            m.kern_ba[p] = jnp.exp2(d2 * (-LOG2E * m.decay[k]))
        return 0

    half_steps = pairs // GROUP // 2
    lax.fori_loop(0, half_steps, kernels, 0)
    for q in range(2):
        t = 2 * c + q
        take(m.ext.at[own + t], m.r_feat.at[q])
        push(m.ext.at[own + t], m.ext.at[own + t], m.r_relay, at(d, partner))
    lax.fori_loop(half_steps, pairs // GROUP, kernels, 0)
    plan_copy.wait()
    take(m.ext.at[pl.ds(own + 2 * mate, 2)], m.r_relay)

    def pair_at(row, i):
        return jnp.clip(m.plan[row, i], 0, pairs - 1)

    def sum_at(row, i):
        return jnp.clip(m.plan[row, i], 0, pairs)

    def seg_f(p):
        return m.home[p] * kinds + m.kind[p]

    def forward(g, _):
        acc = m.carry[...]
        for u in range(WIDE_GROUP):
            i = g * WIDE_GROUP + u
            p = pair_at(0, i)
            last = pair_at(0, jnp.maximum(i - 1, 0))
            keep = (seg_f(p) == seg_f(last)).astype(F32)
            acc = acc * keep + mm(m.kern_ab[p], m.ext[m.other[p]])
            m.sums[i + 1] = acc.astype(BF16)
        m.carry[...] = acc
        return 0

    lax.fori_loop(0, pairs // WIDE_GROUP, forward, 0)

    def message(h):
        left = [m.sums[sum_at(2, h * kinds + k)] for k in range(kinds)]
        return mm(jnp.concatenate(left, axis=1), m.radial[...].reshape(kinds * channels, channels))

    m.msg[...] = message(mate).astype(BF16).reshape(m.msg.shape)
    for q in range(2):
        push(m.msg.at[q], m.msg_in.at[q], m.r_msg.at[q], at(d, partner))
    value = message(c).reshape(m.msg.shape)
    for t in range(4):
        columns(own + t)
        table(own + t)
    for q in range(2):
        take(m.msg_in.at[q], m.r_msg.at[q])
        m.chip[q] = (value[q] + m.msg_in[q].astype(F32)).astype(BF16)
        push(m.chip.at[q], m.chip_in.at[q], m.r_chip.at[q], at(d, across))
    lax.fori_loop(0, pairs // GROUP, transposed, 0)
    for q in range(2):
        take(m.chip_in.at[q], m.r_chip.at[q])
        low = (m.chip[q].astype(F32) + m.chip_in[q].astype(F32)).astype(BF16)
        mixed = mm(low, m.mixing[...])
        sig = jax.nn.sigmoid(mixed)
        slope = (m.readout[...] * sig * (1.0 + mixed * (1.0 - sig))).astype(BF16)
        m.adjoint[c, q] = nt(slope, m.mixing[...]).astype(BF16)
        push(m.adjoint.at[c, q], m.adjoint.at[c, q], m.r_adj, at(d, partner))
        m.state[0, c, q] = slope
        m.state[1, c, q] = low
    push(m.state.at[0, c], m.state.at[0, c], m.r_state, at(d, partner))
    push(m.state.at[1, c], m.state.at[1, c], m.r_state, at(d, partner))

    take(m.adjoint.at[mate], m.r_adj)
    adjoint = m.adjoint[...].reshape(atoms, channels)
    for k in range(kinds):
        wide = nt(adjoint, m.radial[k]).astype(BF16)
        for j in range(own):
            m.weights[j * kinds + k] = wide[j * TILE:(j + 1) * TILE]

    sub = lax.broadcasted_iota(jnp.int32, (8, TILE), 0)
    is_x1, is_y1 = (sub == 0) | (sub == 3) | (sub == 4), (sub == 1) | (sub == 5)
    is_x2, is_y2 = (sub == 0), (sub == 1) | (sub == 3)

    def combine(res, a, b):
        quad = res[0:8] + res[32:40] + res[56:64]
        lin1 = res[8:16] + res[40:48] + res[64:72]
        lin2 = res[16:24] + res[48:56] + res[72:80]
        one = res[24:32]
        force = lin1 - a * one
        virial = -0.5 * (quad - a * lin2 - b * lin1 + a * b * one)
        return jnp.concatenate([force, virial], axis=0)

    def pair_b(i):
        p = pair_at(1, i)
        last = pair_at(1, jnp.maximum(i - 1, 0))
        keep = (m.other[p] == m.other[last]).astype(F32)
        return p, m.home[p], m.other[p], m.kind[p], keep

    def spread_back(g, _):
        acc = m.carry[...]
        for u in range(WIDE_GROUP):
            i = g * WIDE_GROUP + u
            p, h, _, k, keep = pair_b(i)
            acc = acc * keep + mm(m.kern_ba[p].astype(BF16), m.weights[h * kinds + k])
            m.sums[i + 1] = acc.astype(BF16)
        m.carry[...] = acc
        return 0

    def backward(g, _):
        found = []
        for u in range(BACK_GROUP):
            i = g * BACK_GROUP + u
            p, h, o, k, keep = pair_b(i)
            grad = nt(m.ext[o], m.weights[h * kinds + k])
            found.append((i, p, h, o, keep, ((-2.0 * m.decay[k]) * m.kern_ba[p] * grad).astype(BF16)))
        far = m.far[g * BACK_GROUP]
        near = [m.near[j] for j in range(own)]
        results = []
        for one, two in zip(found[::2], found[1::2]):
            weight = jnp.concatenate([one[-1], two[-1]], axis=1)
            close = mm(jnp.concatenate([m.moments[one[3]], m.moments[two[3]]], axis=0), weight)
            beyond = nt(jnp.concatenate([m.sided[one[2], 0], m.sided[two[2], 1]], axis=0), weight)
            size = close.shape[0] // 2
            results += [(close[:size, :TILE], beyond[:size]), (close[size:, TILE:], beyond[size:])]
        for (i, p, h, o, keep, _), (close, beyond) in zip(found, results):
            shift = [m.image[x, p].astype(F32) * CELL for x in range(3)]
            s1 = jnp.where(is_x1, shift[0], jnp.where(is_y1, shift[1], shift[2]))
            s2 = jnp.where(is_x2, shift[0], jnp.where(is_y2, shift[1], shift[2]))
            near_side = combine(close, m.first[h] - s1, m.second[h] - s2)
            far_side = combine(beyond, m.first[o] + s1, m.second[o] + s2)
            for j in range(own):
                near[j] = near[j] + near_side * (h == j).astype(F32)
            far = far * keep + far_side
            m.far[i + 1] = far
        for j in range(own):
            m.near[j] = near[j]
        return 0

    m.carry[...] = jnp.zeros_like(m.carry)
    lax.fori_loop(0, pairs // WIDE_GROUP, spread_back, 0)

    share = channels // n_rep
    slots = (2 - late, 1 + late, 0)
    away = [(slot, own + 2 * mate + slot - 1) for slot in slots[:2]] + [(0, mate)]
    held = [(slot, own + 2 * c + slot - 1) for slot in slots[:2]] + [(0, c)]

    def settle(group):
        total = jnp.concatenate([m.sums[sum_at(3, j)] for _, j in group], axis=0)
        turned = nt(m.eye[:channels, :channels], total).astype(BF16)
        for i, (_, j) in enumerate(group):
            m.gfeat[j] = turned[:, i * TILE:(i + 1) * TILE].reshape(n_rep, share, TILE)

    settle(away)
    for slot, j in away:
        push(m.gfeat.at[j], m.gp.at[slot], m.r_gp.at[slot], at(d, partner))
    settle(held)
    lax.fori_loop(0, 1, backward, 0)
    pl.semaphore_wait(m.passed, n_rep - 1)
    for place, (slot, j) in enumerate(held):
        take(m.gp.at[slot], m.r_gp.at[slot])
        m.sb[slot] = (m.gfeat[j].astype(F32) + m.gp[slot].astype(F32)).astype(BF16)
        if place < 2:
            t = 2 * c + slot - 1
            for q in range(n_rep):
                push(m.sb.at[slot, q], m.rf.at[t, y], m.r_rf,
                     at(dom_at((c + 1) * (2 * slot - 3)), q))
    for i, q in enumerate(peers):
        push(m.sb.at[0, q], m.ro.at[r], m.r_ro, at(d, q))
    m.ro[r] = m.sb[0, r]
    lax.fori_loop(1, pairs // BACK_GROUP, backward, 0)
    for t, o in enumerate(OFFSETS):
        m.side[t] = m.far[sum_at(3, own + t)]
        push(m.side.at[t], m.rs.at[t], m.r_rs, at(dom_at(-o), r))
    take(m.state.at[0], m.r_state)
    pick = (lax.broadcasted_iota(jnp.int32, (channels, share), 0)
            == lax.broadcasted_iota(jnp.int32, (channels, share), 1) + r * share).astype(BF16)
    cols = mm(m.state[0].reshape(atoms, channels), pick).astype(BF16)
    m.mix[...] = tn(m.state[1].reshape(atoms, channels), cols).reshape(m.mix.shape)
    def mix_copy(i):
        to = lax.rem(d + i, n_dom)
        return pltpu.make_async_remote_copy(m.mix.at[to], m.rm.at[d], m.sent, m.r_mix,
                                            device_id=at(to, r), device_id_type=MESH)

    lax.fori_loop(1, n_dom, lambda i, _: (mix_copy(i).start(), 0)[1], 0)
    take(m.ro.at[:n_rep - 1], m.r_ro)
    total = jnp.concatenate([m.ro[j].astype(F32) + m.ro[own + j].astype(F32) for j in range(own)], axis=1)
    take(m.rf, m.r_rf)
    both = nt(jnp.concatenate([m.rf[t].reshape(2 * share, TILE) for t in range(4)], axis=1), m.hot[...])
    m.part[r] = (total + (both[:share] + both[share:])).astype(BF16)
    push(m.part.at[r], m.part.at[r], m.r_part.at[0], at(d, across))
    push(m.part.at[r], m.part.at[r], m.r_part.at[1], at(d, partner))
    take(m.rs, m.r_rs)
    left = jnp.concatenate([jnp.concatenate(split3(m.rs[t]), axis=0) for t in range(4)], axis=1)
    spots = nt(left, m.hot[...])
    m.pside[r] = (jnp.concatenate([m.far[sum_at(3, j)] + m.near[j] for j in range(own)], axis=1)
                  + (spots[0:16] + spots[16:32] + spots[32:48]))
    for i, q in enumerate(peers):
        push(m.pside.at[r], m.pside.at[r], m.r_side, at(d, q))
    take(m.part.at[across], m.r_part.at[0])
    push(m.part.at[across], m.part.at[across], m.r_part.at[2], at(d, partner))

    take(m.rm.at[:n_dom - 1], m.r_mix)
    m.out_mix[...] = lax.fori_loop(1, n_dom, lambda i, v: v + m.rm[lax.rem(d + i, n_dom)], m.mix[d])
    take(m.pside.at[:n_rep - 1], m.r_side)
    final = (m.pside[0] + m.pside[1]) + (m.pside[2] + m.pside[3])
    m.out_force[...] = final[0:3]
    m.out_virial[...] = final[8:14]
    take(m.part.at[partner], m.r_part.at[1])
    take(m.part.at[partner], m.r_part.at[2])
    m.out_feat[...] = nt(m.eye[:atoms, :atoms], m.part[...].reshape(channels, atoms)).astype(BF16)
    for copy in started:
        copy.wait_send()
    lax.fori_loop(1, n_dom, lambda i, _: (mix_copy(i).wait_send(), 0)[1], 0)


def copy_out(a, b, c, d, a_h, b_h, c_h, d_h, sem):
    copies = [pltpu.make_async_copy(src, dst, sem.at[i])
              for i, (src, dst) in enumerate(((a, a_h), (b, b_h), (c, c_h), (d, d_h)))]
    for copy in copies:
        copy.start()
    for copy in copies:
        copy.wait()


def on_device(n_dom, n_rep, features, positions, radial, mixing, readout, decay, send_rows, pair_home,
              pair_other, pair_kind, pair_image):
    atoms, channels = features.shape
    own = atoms // TILE
    n_ext = own + len(OFFSETS)
    kinds = radial.shape[0]
    pairs = pair_home.shape[0]
    dma = pltpu.SemaphoreType.DMA
    mix_rows, mix_cols = channels // n_dom, channels // n_rep
    quarters = (n_rep, channels // n_rep, TILE)
    readout_row = readout.reshape(1, channels)
    pair_rows = [a.reshape(1, pairs) for a in (pair_home, pair_other, pair_kind)]

    scratch = {
        "feat": pltpu.VMEM(features.shape, BF16), "pos": pltpu.VMEM(positions.shape, F32),
        "rows": pltpu.VMEM(send_rows.shape, jnp.int32), "radial": pltpu.VMEM(radial.shape, BF16),
        "mixing": pltpu.VMEM(mixing.shape, BF16), "readout": pltpu.VMEM(readout_row.shape, F32),
        "decay": pltpu.SMEM(decay.shape, F32), "home": pltpu.SMEM(pair_home.shape, jnp.int32),
        "other": pltpu.SMEM(pair_other.shape, jnp.int32), "kind": pltpu.SMEM(pair_kind.shape, jnp.int32),
        "image": pltpu.SMEM(pair_image.shape, jnp.int32),
        "home_row": pltpu.VMEM((1, pairs), jnp.int32), "other_row": pltpu.VMEM((1, pairs), jnp.int32),
        "kind_row": pltpu.VMEM((1, pairs), jnp.int32),
        "raw": pltpu.VMEM((8, TILE), jnp.int32), "plan_v": pltpu.VMEM((8, TILE), jnp.int32),
        "plan": pltpu.SMEM((8, TILE), jnp.int32),
        "sendf": pltpu.VMEM((2, TILE, channels), BF16), "sendp": pltpu.VMEM((2, 3, TILE), F32),
        "recvp": pltpu.VMEM((4, 3, TILE), F32), "ext": pltpu.VMEM((n_ext, TILE, channels), BF16),
        "tiles": pltpu.VMEM((n_ext, 3, TILE), F32), "col": pltpu.VMEM((n_ext, 3, TILE, TILE), F32),
        "moments": pltpu.VMEM((n_ext, 80, TILE), BF16),
        "sided": pltpu.VMEM((own, 2, 80, 2 * TILE), BF16), "hot": pltpu.VMEM((atoms, 4 * TILE), BF16),
        "first": pltpu.VMEM((n_ext, 8, TILE), F32), "second": pltpu.VMEM((n_ext, 8, TILE), F32),
        "kern_ab": pltpu.VMEM((pairs, TILE, TILE), BF16), "kern_ba": pltpu.VMEM((pairs, TILE, TILE), F32),
        "sums": pltpu.VMEM((pairs + 1, TILE, channels), BF16),
        "carry": pltpu.VMEM((TILE, channels), F32), "far": pltpu.VMEM((pairs + 1, 16, TILE), F32),
        "near": pltpu.VMEM((own, 16, TILE), F32),
        "msg": pltpu.VMEM((2, TILE // 2, channels), BF16), "msg_in": pltpu.VMEM((2, TILE // 2, channels), BF16),
        "chip": pltpu.VMEM((2, TILE // 2, channels), BF16), "chip_in": pltpu.VMEM((2, TILE // 2, channels), BF16),
        "adjoint": pltpu.VMEM((own, 2, TILE // 2, channels), BF16), "state": pltpu.VMEM((2, own, 2, TILE // 2, channels), BF16),
        "weights": pltpu.VMEM((own * kinds, TILE, channels), BF16),
        "gfeat": pltpu.VMEM((n_ext, *quarters), BF16), "side": pltpu.VMEM((4, 16, TILE), F32),
        "gp": pltpu.VMEM((3, *quarters), BF16),
        "sb": pltpu.VMEM((3, *quarters), BF16),
        "rf": pltpu.VMEM((4, 2, *quarters[1:]), BF16), "ro": pltpu.VMEM(quarters, BF16), "rs": pltpu.VMEM((4, 16, TILE), F32),
        "mix": pltpu.VMEM((n_dom, mix_rows, mix_cols), F32), "rm": pltpu.VMEM((n_dom, mix_rows, mix_cols), F32),
        "part": pltpu.VMEM((n_rep, channels // n_rep, atoms), BF16),
        "eye": pltpu.VMEM((max(atoms, channels),) * 2, BF16),
        "pside": pltpu.VMEM((n_rep, 16, atoms), F32),
        "load": dma((3,)), "s_plan": dma, "sent": dma, "passed": pltpu.SemaphoreType.REGULAR, "r_pos": dma,
        "r_feat": dma((2,)), "r_relay": dma, "r_msg": dma((2,)), "r_chip": dma((2,)), "r_adj": dma,
        "r_state": dma, "r_gp": dma((3,)), "r_rf": dma, "r_ro": dma, "r_rs": dma, "r_mix": dma,
        "r_part": dma((3,)), "r_side": dma,
    }

    def shape(dims, dtype):
        return jax.ShapeDtypeStruct(dims, dtype)

    results = pl.pallas_call(
        functools.partial(kernel, INPUTS + OUTPUTS + tuple(scratch), n_dom, n_rep),
        out_shape=(shape((atoms, channels), BF16), shape((3, atoms), F32), shape((6, atoms), F32),
                   shape((mix_rows, mix_cols), F32)),
        in_specs=[HBM] * len(INPUTS),
        out_specs=(VMEM,) * 4,
        scratch_shapes=list(scratch.values()),
        compiler_params=pltpu.CompilerParams(collective_id=0, has_side_effects=True, vmem_limit_bytes=48 << 20),
        name="layer",
    )(*[pltpu.with_memory_space_constraint(a, pltpu.HBM) for a in (
        features, positions, send_rows, radial, mixing, readout_row, decay, pair_home, pair_other, pair_kind,
        pair_image, *pair_rows)])
    return pl.pallas_call(
        copy_out,
        out_shape=tuple(shape(a.shape, a.dtype) for a in results),
        in_specs=[VMEM] * 4,
        out_specs=(HBM,) * 4,
        scratch_shapes=[dma((4,))],
        compiler_params=pltpu.CompilerParams(vmem_limit_bytes=4 << 20),
        name="copy_out",
    )(*results)


def solution(mesh):
    in_specs = (
        P("dom", None),
        P(None, "dom"),
        P(),
        P(),
        P(),
        P(),
        P(None, "dom"),
        P(("dom", "rep")),
        P(("dom", "rep")),
        P(("dom", "rep")),
        P(None, ("dom", "rep")),
    )
    out_specs = (P("dom", None), P(None, "dom"), P(None, "dom"), P("dom", "rep"))
    body = functools.partial(on_device, mesh.shape["dom"], mesh.shape["rep"])
    return jax.shard_map(body, mesh=mesh, in_specs=in_specs, out_specs=out_specs, check_vma=False)
```

```python
import functools
import types

import jax
import jax.numpy as jnp
from jax import lax
from jax.experimental import pallas as pl
from jax.experimental.pallas import tpu as pltpu
from jax.sharding import PartitionSpec as P

TILE = 128
OFFSETS = (1, -1, 2, -2)
CELL = 2.0
GROUP = 4
WIDE_GROUP = 24
BACK_GROUP = 12
LOG2E = 1.4426950408889634
F32 = jnp.float32
BF16 = jnp.bfloat16
MESH = pl.DeviceIdType.MESH
VMEM = pl.BlockSpec(memory_space=pltpu.VMEM)
HBM = pl.BlockSpec(memory_space=pltpu.HBM)
INPUTS = ("feat_h", "pos_h", "rows_h", "radial_h", "mixing_h", "readout_h", "decay_h", "home_h", "other_h",
          "kind_h", "image_h", "home_row_h", "other_row_h", "kind_row_h")
OUTPUTS = ("out_feat", "out_force", "out_virial", "out_mix")


def nt(a, b):
    return lax.dot_general(a, b, (((1,), (1,)), ((), ())), preferred_element_type=F32)


def tn(a, b):
    return lax.dot_general(a, b, (((0,), (0,)), ((), ())), preferred_element_type=F32)


def mm(a, b):
    return jnp.dot(a, b, preferred_element_type=F32)


def split3(x):
    hi = x.astype(BF16)
    rest = x - hi.astype(F32)
    mid = rest.astype(BF16)
    low = (rest - mid.astype(F32)).astype(BF16)
    return hi, mid, low


def order_pairs(seg, lanes, subs):
    row = jnp.broadcast_to(seg, (TILE, TILE))
    col = jnp.transpose(row)
    before = (col < row) | ((col == row) & (subs < lanes))
    rank = jnp.sum(before.astype(jnp.int32), axis=0, keepdims=True)
    rank = jnp.transpose(jnp.broadcast_to(rank, (TILE, TILE)))
    order = jnp.sum(jnp.where(rank == lanes, subs, 0), axis=0, keepdims=True)
    upto = jnp.sum((col <= lanes).astype(jnp.int32), axis=0, keepdims=True)
    below = jnp.sum((col < lanes).astype(jnp.int32), axis=0, keepdims=True)
    return order, jnp.where(upto > below, upto, 0)


def kernel(names, n_dom, n_rep, *refs):
    m = types.SimpleNamespace(**dict(zip(names, refs)))
    d = lax.axis_index("dom")
    r = lax.axis_index("rep")
    y = lax.div(r, 2)
    c = lax.rem(r, 2)
    mate = 1 - c
    partner = r + 1 - 2 * c
    across = r + 2 - 4 * y
    cross = across + 1 - 2 * c
    atoms, channels = m.feat.shape
    own = atoms // TILE
    late = lax.div(n_dom - 1 - d, n_dom // 2)
    pairs = m.home.shape[0]
    kinds = m.radial.shape[0]
    n_ext = m.tiles.shape[0]

    def dom_at(o):
        return lax.rem(d + o + n_dom, n_dom)

    def at(dom, rep):
        return {"dom": dom, "rep": rep}

    groups = ((m.rows_h, m.rows), (m.feat_h, m.feat), (m.pos_h, m.pos)), (
        (m.home_row_h, m.home_row), (m.other_row_h, m.other_row), (m.kind_row_h, m.kind_row)), (
        (m.radial_h, m.radial), (m.decay_h, m.decay), (m.home_h, m.home), (m.other_h, m.other),
        (m.kind_h, m.kind), (m.image_h, m.image), (m.mixing_h, m.mixing), (m.readout_h, m.readout))
    loads = [[pltpu.make_async_copy(src, dst, m.load.at[i]) for src, dst in group]
             for i, group in enumerate(groups)]
    for copy in loads[0]:
        copy.start()
    barrier = pltpu.get_barrier_semaphore()
    mine = (c + 1, -(c + 1))
    theirs = (2 - c, c - 2)
    peers = [lax.rem(r + i, n_rep) for i in range(1, n_rep)]

    def hello(dom, rep):
        pl.semaphore_signal(barrier, inc=1, device_id=at(dom, rep), device_id_type=MESH)

    def greet(i, _):
        hello(lax.rem(d + i, n_dom), r)
        return 0

    lax.fori_loop(1, n_dom, greet, 0)
    for o in mine:
        hello(dom_at(o), partner)
    for o in theirs:
        hello(dom_at(o), partner)
    for q in peers:
        hello(d, q)
    for copy in loads[1] + loads[2]:
        copy.start()

    started = []

    def push(src, dst, rs, target):
        copy = pltpu.make_async_remote_copy(src, dst, m.sent, rs, device_id=target, device_id_type=MESH)
        copy.start()
        started.append(copy)

    def take(dst, rs):
        pltpu.make_async_remote_copy(dst, dst, m.sent, rs, device_id=at(d, partner), device_id_type=MESH).wait_recv()

    for copy in loads[0]:
        copy.wait()
    iota = lax.broadcasted_iota(jnp.int32, (atoms, TILE), 0)
    hots = []
    for q in range(2):
        hot = (iota == m.rows[pl.ds(2 * c + q, 1), :]).astype(F32)
        hots.append(hot.astype(BF16))
        m.sendp[q] = jnp.dot(m.pos[...], hot, precision=lax.Precision.HIGHEST, preferred_element_type=F32)
    for q in range(2):
        m.sendf[q] = tn(hots[q], m.feat[...]).astype(BF16)
    pl.semaphore_wait(barrier, 4 + n_rep - 1 + n_dom - 1)
    for q in (late, 1 - late):
        for i, rep in enumerate((r, partner)):
            push(m.sendp.at[q], m.recvp.at[2 * c + q], m.r_pos,
                 at(dom_at((c + 1) * (1 - 2 * q)), rep))
    for q in (late, 1 - late):
        push(m.sendf.at[q], m.ext.at[own + 2 * c + q], m.r_feat.at[q],
             at(dom_at((c + 1) * (1 - 2 * q)), r))

    for copy in loads[1]:
        copy.wait()
    m.raw[...] = jnp.zeros_like(m.raw)
    for i, src in enumerate((m.home_row, m.kind_row, m.other_row)):
        m.raw[i:i + 1, :pairs] = src[...]
    raw = m.raw[...]
    lanes = lax.broadcasted_iota(jnp.int32, (TILE, TILE), 1)
    subs = lax.broadcasted_iota(jnp.int32, (TILE, TILE), 0)
    real = lanes[0:1] < pairs
    order_f, end_f = order_pairs(jnp.where(real, raw[0:1] * kinds + raw[1:2], TILE), lanes, subs)
    order_b, end_b = order_pairs(jnp.where(real, raw[2:3], TILE), lanes, subs)
    m.plan_v[...] = jnp.concatenate(
        [order_f, order_b, end_f, end_b, jnp.zeros((4, TILE), jnp.int32)], axis=0)
    plan_copy = pltpu.make_async_copy(m.plan_v, m.plan, m.s_plan)
    plan_copy.start()

    def columns(j):
        for x in range(3):
            m.col[j, x] = jnp.transpose(jnp.broadcast_to(m.tiles[j][x:x + 1, :], (TILE, TILE)))

    def table(j):
        pos = m.tiles[j]
        x, yy, z = pos[0:1, :], pos[1:2, :], pos[2:3, :]
        zero = jnp.zeros((2, TILE), F32)
        one_rows = jnp.concatenate([x, yy, z, x, x, yy, zero], axis=0)
        two_rows = jnp.concatenate([x, yy, z, yy, z, z, zero], axis=0)
        m.first[j] = one_rows
        m.second[j] = two_rows
        stack = jnp.concatenate([one_rows * two_rows, one_rows, two_rows], axis=0)
        parts = [v.astype(F32) for v in split3(stack)]
        stack = jnp.concatenate([parts[0], jnp.ones((8, TILE), F32), parts[1], parts[2]], axis=0).astype(BF16)
        m.moments[j] = stack
        if j < own:
            m.sided[j, 0] = jnp.concatenate([stack, jnp.zeros_like(stack)], axis=1)
            m.sided[j, 1] = jnp.concatenate([jnp.zeros_like(stack), stack], axis=1)

    for j in range(own):
        m.tiles[j] = m.pos[:, j * TILE:(j + 1) * TILE]
        m.ext[j] = m.feat[j * TILE:(j + 1) * TILE, :]
        columns(j)
    for q in peers:
        pl.semaphore_signal(m.passed, inc=1, device_id=at(d, q), device_id_type=MESH)
    m.sums[0] = jnp.zeros_like(m.sums[0])
    m.carry[...] = jnp.zeros_like(m.carry)
    for t in range(4):
        m.hot[:, t * TILE:(t + 1) * TILE] = (iota == m.rows[t:t + 1, :]).astype(F32).astype(BF16)
    m.far[0] = jnp.zeros_like(m.far[0])
    m.near[...] = jnp.zeros_like(m.near)
    m.eye[...] = (lax.broadcasted_iota(jnp.int32, m.eye.shape, 0)
                  == lax.broadcasted_iota(jnp.int32, m.eye.shape, 1)).astype(F32).astype(BF16)
    for j in range(own):
        table(j)
    for copy in loads[2]:
        copy.wait()
    for k in range(kinds):
        m.radmix[k] = mm(m.radial[k], m.mixing[...]).astype(BF16)
    take(m.recvp, m.r_pos)
    for t in range(4):
        m.tiles[own + t] = m.recvp[t]

    def kernels(g, _):
        for u in range(GROUP):
            p = g * GROUP + u
            h, o, k = m.home[p], m.other[p], m.kind[p]
            row = m.tiles[o]
            d2 = None
            for x in range(3):
                sep = (row[x:x + 1, :] + m.image[x, p].astype(F32) * CELL) - m.col[h, x]
                d2 = sep * sep if d2 is None else d2 + sep * sep
            m.kern_ab[p] = jnp.exp2(d2 * (-LOG2E * m.decay[k])).astype(BF16)
        return 0

    def transposed(g, _):
        for u in range(GROUP):
            p = g * GROUP + u
            h, o, k = m.home[p], m.other[p], m.kind[p]
            row = m.tiles[h]
            d2 = None
            for x in range(3):
                sep = m.col[o, x] - (row[x:x + 1, :] - m.image[x, p].astype(F32) * CELL)
                d2 = sep * sep if d2 is None else d2 + sep * sep
            m.kern_ba[p] = jnp.exp2(d2 * (-LOG2E * m.decay[k]))
        return 0

    half_steps = pairs // GROUP // 2
    lax.fori_loop(0, half_steps, kernels, 0)
    for q in range(2):
        t = 2 * c + q
        take(m.ext.at[own + t], m.r_feat.at[q])
        push(m.ext.at[own + t], m.ext.at[own + t], m.r_relay, at(d, partner))
    lax.fori_loop(half_steps, pairs // GROUP, kernels, 0)
    plan_copy.wait()
    take(m.ext.at[pl.ds(own + 2 * mate, 2)], m.r_relay)

    def pair_at(row, i):
        return jnp.clip(m.plan[row, i], 0, pairs - 1)

    def sum_at(row, i):
        return jnp.clip(m.plan[row, i], 0, pairs)

    def seg_f(p):
        return m.home[p] * kinds + m.kind[p]

    def forward(g, _):
        acc = m.carry[...]
        for u in range(WIDE_GROUP):
            i = g * WIDE_GROUP + u
            p = pair_at(0, i)
            last = pair_at(0, jnp.maximum(i - 1, 0))
            keep = (seg_f(p) == seg_f(last)).astype(F32)
            acc = acc * keep + mm(m.kern_ab[p], m.ext[m.other[p]])
            m.sums[i + 1] = acc.astype(BF16)
        m.carry[...] = acc
        return 0

    lax.fori_loop(0, pairs // WIDE_GROUP, forward, 0)

    def message(h):
        left = [m.sums[sum_at(2, h * kinds + k)] for k in range(kinds)]
        return mm(jnp.concatenate(left, axis=1), m.radial[...].reshape(kinds * channels, channels))

    m.msg[...] = message(mate).astype(BF16).reshape(m.msg.shape)
    for q in range(2):
        push(m.msg.at[q], m.msg_in.at[q], m.r_msg.at[q], at(d, partner))
    value = message(c).reshape(m.msg.shape)
    for q in range(2):
        take(m.msg_in.at[q], m.r_msg.at[q])
        m.chip[q] = (value[q] + m.msg_in[q].astype(F32)).astype(BF16)
        push(m.chip.at[q], m.chip_in.at[q], m.r_chip.at[q], at(d, across))
    for t in range(4):
        columns(own + t)
        table(own + t)
    lax.fori_loop(0, pairs // GROUP, transposed, 0)
    for q in range(2):
        take(m.chip_in.at[q], m.r_chip.at[q])
        low = (m.chip[q].astype(F32) + m.chip_in[q].astype(F32)).astype(BF16)
        mixed = mm(low, m.mixing[...])
        sig = jax.nn.sigmoid(mixed)
        slope = (m.readout[...] * sig * (1.0 + mixed * (1.0 - sig))).astype(BF16)
        m.slope[c, q] = slope
        push(m.slope.at[c, q], m.slope.at[c, q], m.r_slope, at(d, partner))
        m.packed[c, q] = low
    push(m.packed.at[c], m.packed.at[c], m.r_packed, at(d, partner))

    take(m.slope.at[mate], m.r_slope)
    slope = m.slope[...].reshape(atoms, channels)
    for k in range(kinds):
        wide = nt(slope, m.radmix[k]).astype(BF16)
        for j in range(own):
            m.weights[j * kinds + k] = wide[j * TILE:(j + 1) * TILE]

    sub = lax.broadcasted_iota(jnp.int32, (8, TILE), 0)
    is_x1, is_y1 = (sub == 0) | (sub == 3) | (sub == 4), (sub == 1) | (sub == 5)
    is_x2, is_y2 = (sub == 0), (sub == 1) | (sub == 3)

    def combine(res, a, b):
        quad = res[0:8] + res[32:40] + res[56:64]
        lin1 = res[8:16] + res[40:48] + res[64:72]
        lin2 = res[16:24] + res[48:56] + res[72:80]
        one = res[24:32]
        force = lin1 - a * one
        virial = -0.5 * (quad - a * lin2 - b * lin1 + a * b * one)
        return jnp.concatenate([force, virial], axis=0)

    def pair_b(i):
        p = pair_at(1, i)
        last = pair_at(1, jnp.maximum(i - 1, 0))
        keep = (m.other[p] == m.other[last]).astype(F32)
        return p, m.home[p], m.other[p], m.kind[p], keep

    def spread_back(g, _):
        acc = m.carry[...]
        for u in range(WIDE_GROUP):
            i = g * WIDE_GROUP + u
            p, h, _, k, keep = pair_b(i)
            acc = acc * keep + mm(m.kern_ba[p].astype(BF16), m.weights[h * kinds + k])
            m.sums[i + 1] = acc.astype(BF16)
        m.carry[...] = acc
        return 0

    def backward(g, _):
        found = []
        for u in range(BACK_GROUP):
            i = g * BACK_GROUP + u
            p, h, o, k, keep = pair_b(i)
            grad = nt(m.ext[o], m.weights[h * kinds + k])
            found.append((i, p, h, o, keep, ((-2.0 * m.decay[k]) * m.kern_ba[p] * grad).astype(BF16)))
        far = m.far[g * BACK_GROUP]
        near = [m.near[j] for j in range(own)]
        results = []
        for one, two in zip(found[::2], found[1::2]):
            weight = jnp.concatenate([one[-1], two[-1]], axis=1)
            close = mm(jnp.concatenate([m.moments[one[3]], m.moments[two[3]]], axis=0), weight)
            beyond = nt(jnp.concatenate([m.sided[one[2], 0], m.sided[two[2], 1]], axis=0), weight)
            size = close.shape[0] // 2
            results += [(close[:size, :TILE], beyond[:size]), (close[size:, TILE:], beyond[size:])]
        for (i, p, h, o, keep, _), (close, beyond) in zip(found, results):
            shift = [m.image[x, p].astype(F32) * CELL for x in range(3)]
            s1 = jnp.where(is_x1, shift[0], jnp.where(is_y1, shift[1], shift[2]))
            s2 = jnp.where(is_x2, shift[0], jnp.where(is_y2, shift[1], shift[2]))
            near_side = combine(close, m.first[h] - s1, m.second[h] - s2)
            far_side = combine(beyond, m.first[o] + s1, m.second[o] + s2)
            for j in range(own):
                near[j] = near[j] + near_side * (h == j).astype(F32)
            far = far * keep + far_side
            m.far[i + 1] = far
        for j in range(own):
            m.near[j] = near[j]
        return 0

    m.carry[...] = jnp.zeros_like(m.carry)
    lax.fori_loop(0, pairs // WIDE_GROUP, spread_back, 0)

    share = channels // n_rep
    slots = (2 - late, 1 + late, 0)
    away = [(slot, own + 2 * mate + slot - 1) for slot in slots[:2]] + [(0, mate)]
    held = [(slot, own + 2 * c + slot - 1) for slot in slots[:2]] + [(0, c)]

    def settle(group):
        total = jnp.concatenate([m.sums[sum_at(3, j)] for _, j in group], axis=0)
        turned = nt(m.eye[:channels, :channels], total).astype(BF16)
        for i, (_, j) in enumerate(group):
            m.gfeat[j] = turned[:, i * TILE:(i + 1) * TILE].reshape(n_rep, share, TILE)

    settle(away)
    for slot, j in away:
        push(m.gfeat.at[j], m.gp.at[slot], m.r_gp.at[slot], at(d, partner))
    settle(held)
    lax.fori_loop(0, 1, backward, 0)
    pl.semaphore_wait(m.passed, n_rep - 1)
    for place, (slot, j) in enumerate(held):
        take(m.gp.at[slot], m.r_gp.at[slot])
        m.sb[slot] = (m.gfeat[j].astype(F32) + m.gp[slot].astype(F32)).astype(BF16)
        if place < 2:
            t = 2 * c + slot - 1
            for q in (across, cross, r, partner):
                push(m.sb.at[slot, q], m.rf.at[t, y], m.r_rf,
                     at(dom_at((c + 1) * (2 * slot - 3)), q))
    for q in (across, cross, partner):
        push(m.sb.at[0, q], m.ro.at[r], m.r_ro, at(d, q))
    m.ro[r] = m.sb[0, r]
    lax.fori_loop(1, pairs // BACK_GROUP, backward, 0)
    for t, o in enumerate(OFFSETS):
        m.side[t] = m.far[sum_at(3, own + t)].astype(BF16)
        push(m.side.at[t], m.rs.at[t], m.r_rs, at(dom_at(-o), r))
    take(m.packed.at[mate], m.r_packed)
    pick = (lax.broadcasted_iota(jnp.int32, (channels, share), 0)
            == lax.broadcasted_iota(jnp.int32, (channels, share), 1) + r * share).astype(BF16)
    cols = mm(m.slope[...].reshape(atoms, channels), pick).astype(BF16)
    m.mix[...] = tn(m.packed[...].reshape(atoms, channels), cols).reshape(m.mix.shape)
    def mix_copy(i):
        to = lax.rem(d + i, n_dom)
        return pltpu.make_async_remote_copy(m.mix.at[to], m.rm.at[d], m.sent, m.r_mix,
                                            device_id=at(to, r), device_id_type=MESH)

    lax.fori_loop(1, n_dom, lambda i, _: (mix_copy(i).start(), 0)[1], 0)
    take(m.ro.at[:n_rep - 1], m.r_ro)
    total = jnp.concatenate([m.ro[j].astype(F32) + m.ro[own + j].astype(F32) for j in range(own)], axis=1)
    take(m.rf, m.r_rf)
    both = nt(jnp.concatenate([m.rf[t].reshape(2 * share, TILE) for t in range(4)], axis=1), m.hot[...])
    m.part[r] = (total + (both[:share] + both[share:])).astype(BF16)
    for q in (across, cross, partner):
        push(m.part.at[r], m.part.at[r], m.r_part, at(d, q))
    take(m.rs, m.r_rs)
    spots = nt(jnp.concatenate([m.rs[t] for t in range(4)], axis=1), m.hot[...])
    here = jnp.concatenate([m.far[sum_at(3, j)] + m.near[j] for j in range(own)], axis=1)
    m.pside[r] = (here + spots).astype(BF16)
    for q in (across, cross, partner):
        push(m.pside.at[r], m.pside.at[r], m.r_side, at(d, q))
    take(m.rm.at[:n_dom - 1], m.r_mix)
    m.out_mix[...] = lax.fori_loop(1, n_dom, lambda i, v: v + m.rm[lax.rem(d + i, n_dom)], m.mix[d])
    take(m.pside.at[:n_rep - 1], m.r_side)
    final = sum(m.pside[q].astype(F32) for q in range(n_rep))
    m.out_force[...] = final[0:3]
    m.out_virial[...] = final[8:14]
    take(m.part.at[:n_rep - 1], m.r_part)
    m.out_feat[...] = nt(m.eye[:atoms, :atoms], m.part[...].reshape(channels, atoms)).astype(BF16)
    for copy in started:
        copy.wait_send()
    lax.fori_loop(1, n_dom, lambda i, _: (mix_copy(i).wait_send(), 0)[1], 0)


def copy_out(a, b, c, d, a_h, b_h, c_h, d_h, sem):
    copies = [pltpu.make_async_copy(src, dst, sem)
              for src, dst in ((a, a_h), (b, b_h), (c, c_h), (d, d_h))]
    for copy in copies:
        copy.start()
    for copy in copies:
        copy.wait()


def on_device(n_dom, n_rep, features, positions, radial, mixing, readout, decay, send_rows, pair_home,
              pair_other, pair_kind, pair_image):
    atoms, channels = features.shape
    own = atoms // TILE
    n_ext = own + len(OFFSETS)
    kinds = radial.shape[0]
    pairs = pair_home.shape[0]
    dma = pltpu.SemaphoreType.DMA
    mix_rows, mix_cols = channels // n_dom, channels // n_rep
    quarters = (n_rep, channels // n_rep, TILE)
    readout_row = readout.reshape(1, channels)
    pair_rows = [a.reshape(1, pairs) for a in (pair_home, pair_other, pair_kind)]

    scratch = {
        "feat": pltpu.VMEM(features.shape, BF16), "pos": pltpu.VMEM(positions.shape, F32),
        "rows": pltpu.VMEM(send_rows.shape, jnp.int32), "radial": pltpu.VMEM(radial.shape, BF16),
        "mixing": pltpu.VMEM(mixing.shape, BF16), "readout": pltpu.VMEM(readout_row.shape, F32),
        "decay": pltpu.SMEM(decay.shape, F32), "home": pltpu.SMEM(pair_home.shape, jnp.int32),
        "other": pltpu.SMEM(pair_other.shape, jnp.int32), "kind": pltpu.SMEM(pair_kind.shape, jnp.int32),
        "image": pltpu.SMEM(pair_image.shape, jnp.int32),
        "home_row": pltpu.VMEM((1, pairs), jnp.int32), "other_row": pltpu.VMEM((1, pairs), jnp.int32),
        "kind_row": pltpu.VMEM((1, pairs), jnp.int32),
        "raw": pltpu.VMEM((8, TILE), jnp.int32), "plan_v": pltpu.VMEM((8, TILE), jnp.int32),
        "plan": pltpu.SMEM((8, TILE), jnp.int32),
        "sendf": pltpu.VMEM((2, TILE, channels), BF16), "sendp": pltpu.VMEM((2, 3, TILE), F32),
        "recvp": pltpu.VMEM((4, 3, TILE), F32), "ext": pltpu.VMEM((n_ext, TILE, channels), BF16),
        "tiles": pltpu.VMEM((n_ext, 3, TILE), F32), "col": pltpu.VMEM((n_ext, 3, TILE, TILE), F32),
        "moments": pltpu.VMEM((n_ext, 80, TILE), BF16),
        "sided": pltpu.VMEM((own, 2, 80, 2 * TILE), BF16), "hot": pltpu.VMEM((atoms, 4 * TILE), BF16),
        "first": pltpu.VMEM((n_ext, 8, TILE), F32), "second": pltpu.VMEM((n_ext, 8, TILE), F32),
        "kern_ab": pltpu.VMEM((pairs, TILE, TILE), BF16), "kern_ba": pltpu.VMEM((pairs, TILE, TILE), F32),
        "sums": pltpu.VMEM((pairs + 1, TILE, channels), BF16),
        "carry": pltpu.VMEM((TILE, channels), F32), "far": pltpu.VMEM((pairs + 1, 16, TILE), F32),
        "near": pltpu.VMEM((own, 16, TILE), F32),
        "msg": pltpu.VMEM((2, TILE // 2, channels), BF16), "msg_in": pltpu.VMEM((2, TILE // 2, channels), BF16),
        "chip": pltpu.VMEM((2, TILE // 2, channels), BF16), "chip_in": pltpu.VMEM((2, TILE // 2, channels), BF16),
        "slope": pltpu.VMEM((own, 2, TILE // 2, channels), BF16),
        "packed": pltpu.VMEM((own, 2, TILE // 2, channels), BF16), "radmix": pltpu.VMEM(radial.shape, BF16),
        "weights": pltpu.VMEM((own * kinds, TILE, channels), BF16),
        "gfeat": pltpu.VMEM((n_ext, *quarters), BF16), "side": pltpu.VMEM((4, 16, TILE), BF16),
        "gp": pltpu.VMEM((3, *quarters), BF16),
        "sb": pltpu.VMEM((3, *quarters), BF16),
        "rf": pltpu.VMEM((4, 2, *quarters[1:]), BF16), "ro": pltpu.VMEM(quarters, BF16), "rs": pltpu.VMEM((4, 16, TILE), BF16),
        "mix": pltpu.VMEM((n_dom, mix_rows, mix_cols), F32), "rm": pltpu.VMEM((n_dom, mix_rows, mix_cols), F32),
        "part": pltpu.VMEM((n_rep, channels // n_rep, atoms), BF16),
        "eye": pltpu.VMEM((max(atoms, channels),) * 2, BF16),
        "pside": pltpu.VMEM((n_rep, 16, atoms), BF16),
        "load": dma((3,)), "s_plan": dma, "sent": dma, "passed": pltpu.SemaphoreType.REGULAR, "r_pos": dma,
        "r_feat": dma((2,)), "r_relay": dma, "r_msg": dma((2,)), "r_chip": dma((2,)), "r_slope": dma,
        "r_packed": dma, "r_gp": dma((3,)), "r_rf": dma, "r_ro": dma, "r_rs": dma, "r_mix": dma,
        "r_part": dma, "r_side": dma,
    }

    def shape(dims, dtype):
        return jax.ShapeDtypeStruct(dims, dtype)

    results = pl.pallas_call(
        functools.partial(kernel, INPUTS + OUTPUTS + tuple(scratch), n_dom, n_rep),
        out_shape=(shape((atoms, channels), BF16), shape((3, atoms), F32), shape((6, atoms), F32),
                   shape((mix_rows, mix_cols), F32)),
        in_specs=[HBM] * len(INPUTS),
        out_specs=(VMEM,) * 4,
        scratch_shapes=list(scratch.values()),
        compiler_params=pltpu.CompilerParams(collective_id=0, has_side_effects=True, vmem_limit_bytes=48 << 20),
        name="layer",
    )(*[pltpu.with_memory_space_constraint(a, pltpu.HBM) for a in (
        features, positions, send_rows, radial, mixing, readout_row, decay, pair_home, pair_other, pair_kind,
        pair_image, *pair_rows)])
    return pl.pallas_call(
        copy_out,
        out_shape=tuple(shape(a.shape, a.dtype) for a in results),
        in_specs=[VMEM] * 4,
        out_specs=(HBM,) * 4,
        scratch_shapes=[dma],
        compiler_params=pltpu.CompilerParams(vmem_limit_bytes=4 << 20),
        name="copy_out",
    )(*results)


def solution(mesh):
    in_specs = (
        P("dom", None),
        P(None, "dom"),
        P(),
        P(),
        P(),
        P(),
        P(None, "dom"),
        P(("dom", "rep")),
        P(("dom", "rep")),
        P(("dom", "rep")),
        P(None, ("dom", "rep")),
    )
    out_specs = (P("dom", None), P(None, "dom"), P(None, "dom"), P("dom", "rep"))
    body = functools.partial(on_device, mesh.shape["dom"], mesh.shape["rep"])
    return jax.shard_map(body, mesh=mesh, in_specs=in_specs, out_specs=out_specs, check_vma=False)
```

```python
import functools
import types

import jax
import jax.numpy as jnp
from jax import lax
from jax.experimental import pallas as pl
from jax.experimental.pallas import tpu as pltpu
from jax.sharding import PartitionSpec as P

TILE = 128
OFFSETS = (1, -1, 2, -2)
CELL = 2.0
GROUP = 4
WIDE_GROUP = 48
BACK_GROUP = 12
LOG2E = 1.4426950408889634
F32 = jnp.float32
BF16 = jnp.bfloat16
MESH = pl.DeviceIdType.MESH
VMEM = pl.BlockSpec(memory_space=pltpu.VMEM)
HBM = pl.BlockSpec(memory_space=pltpu.HBM)
INPUTS = ("feat_h", "pos_h", "rows_h", "radial_h", "mixing_h", "readout_h", "decay_h", "home_h", "other_h",
          "kind_h", "image_h", "home_row_h", "other_row_h", "kind_row_h")
OUTPUTS = ("out_feat", "out_force", "out_virial", "out_mix")


def nt(a, b):
    return lax.dot_general(a, b, (((1,), (1,)), ((), ())), preferred_element_type=F32)


def tn(a, b):
    return lax.dot_general(a, b, (((0,), (0,)), ((), ())), preferred_element_type=F32)


def mm(a, b):
    return jnp.dot(a, b, preferred_element_type=F32)


def split3(x):
    hi = x.astype(BF16)
    rest = x - hi.astype(F32)
    mid = rest.astype(BF16)
    low = (rest - mid.astype(F32)).astype(BF16)
    return hi, mid, low


def order_pairs(seg, lanes, subs):
    row = jnp.broadcast_to(seg, (TILE, TILE))
    col = jnp.transpose(row)
    before = (col < row) | ((col == row) & (subs < lanes))
    rank = jnp.sum(before.astype(jnp.int32), axis=0, keepdims=True)
    rank = jnp.transpose(jnp.broadcast_to(rank, (TILE, TILE)))
    order = jnp.sum(jnp.where(rank == lanes, subs, 0), axis=0, keepdims=True)
    upto = jnp.sum((col <= lanes).astype(jnp.int32), axis=0, keepdims=True)
    below = jnp.sum((col < lanes).astype(jnp.int32), axis=0, keepdims=True)
    return order, jnp.where(upto > below, upto, 0)


def kernel(names, n_dom, n_rep, *refs):
    m = types.SimpleNamespace(**dict(zip(names, refs)))
    d = lax.axis_index("dom")
    r = lax.axis_index("rep")
    y = lax.div(r, 2)
    c = lax.rem(r, 2)
    mate = 1 - c
    partner = r + 1 - 2 * c
    across = r + 2 - 4 * y
    cross = across + 1 - 2 * c
    atoms, channels = m.feat.shape
    own = atoms // TILE
    late = lax.div(n_dom - 1 - d, n_dom // 2)
    pairs = m.home.shape[0]
    kinds = m.radial.shape[0]
    n_ext = m.tiles.shape[0]
    size = TILE // 2
    halves = [pl.ds(i * size, size) for i in range(2)]

    def dom_at(o):
        return lax.rem(d + o + n_dom, n_dom)

    def at(dom, rep):
        return {"dom": dom, "rep": rep}

    groups = ((m.rows_h, m.rows), (m.feat_h, m.feat), (m.pos_h, m.pos)), (
        (m.home_row_h, m.home_row), (m.other_row_h, m.other_row), (m.kind_row_h, m.kind_row)), (
        (m.radial_h, m.radial), (m.decay_h, m.decay), (m.home_h, m.home), (m.other_h, m.other),
        (m.kind_h, m.kind), (m.image_h, m.image), (m.mixing_h, m.mixing), (m.readout_h, m.readout))
    loads = [[pltpu.make_async_copy(src, dst, m.load.at[i]) for src, dst in group]
             for i, group in enumerate(groups)]
    for copy in loads[0]:
        copy.start()
    barrier = pltpu.get_barrier_semaphore()
    mine = (c + 1, -(c + 1))
    theirs = (2 - c, c - 2)
    peers = [lax.rem(r + i, n_rep) for i in range(1, n_rep)]

    def hello(dom, rep):
        pl.semaphore_signal(barrier, inc=1, device_id=at(dom, rep), device_id_type=MESH)

    def greet(i, _):
        hello(lax.rem(d + i, n_dom), r)
        return 0

    lax.fori_loop(1, n_dom, greet, 0)
    for o in mine:
        hello(dom_at(o), partner)
    for o in theirs:
        hello(dom_at(o), partner)
    for q in peers:
        hello(d, q)
    for copy in loads[1] + loads[2]:
        copy.start()

    started = []

    def push(src, dst, rs, target):
        copy = pltpu.make_async_remote_copy(src, dst, m.sent, rs, device_id=target, device_id_type=MESH)
        copy.start()
        started.append(copy)

    def take(dst, rs):
        pltpu.make_async_remote_copy(dst, dst, m.sent, rs, device_id=at(d, partner), device_id_type=MESH).wait_recv()

    for copy in loads[0]:
        copy.wait()
    iota = lax.broadcasted_iota(jnp.int32, (atoms, TILE), 0)
    hots = []
    for q in range(2):
        hot = (iota == m.rows[pl.ds(2 * c + q, 1), :]).astype(F32)
        hots.append(hot.astype(BF16))
        m.sendp[q] = jnp.dot(m.pos[...], hot, precision=lax.Precision.HIGHEST, preferred_element_type=F32)
    for q in range(2):
        m.sendf[q] = tn(hots[q], m.feat[...]).astype(BF16)
    pl.semaphore_wait(barrier, 4 + n_rep - 1 + n_dom - 1)
    for q in (late, 1 - late):
        for i, rep in enumerate((r, partner)):
            push(m.sendp.at[q], m.recvp.at[2 * c + q], m.r_pos,
                 at(dom_at((c + 1) * (1 - 2 * q)), rep))
    for q in (late, 1 - late):
        for rows in halves:
            push(m.sendf.at[q, rows], m.ext.at[own + 2 * c + q, rows], m.r_feat.at[q, rows.start // size],
                 at(dom_at((c + 1) * (1 - 2 * q)), r))

    for copy in loads[1]:
        copy.wait()
    m.raw[...] = jnp.zeros_like(m.raw)
    for i, src in enumerate((m.home_row, m.kind_row, m.other_row)):
        m.raw[i:i + 1, :pairs] = src[...]
    raw = m.raw[...]
    lanes = lax.broadcasted_iota(jnp.int32, (TILE, TILE), 1)
    subs = lax.broadcasted_iota(jnp.int32, (TILE, TILE), 0)
    real = lanes[0:1] < pairs
    order_f, end_f = order_pairs(jnp.where(real, raw[0:1] * kinds + raw[1:2], TILE), lanes, subs)
    order_b, end_b = order_pairs(jnp.where(real, raw[2:3], TILE), lanes, subs)
    m.plan_v[...] = jnp.concatenate(
        [order_f, order_b, end_f, end_b, jnp.zeros((4, TILE), jnp.int32)], axis=0)
    plan_copy = pltpu.make_async_copy(m.plan_v, m.plan, m.s_plan)
    plan_copy.start()

    def columns(j):
        for x in range(3):
            m.col[j, x] = jnp.transpose(jnp.broadcast_to(m.tiles[j][x:x + 1, :], (TILE, TILE)))

    def table(j):
        pos = m.tiles[j]
        x, yy, z = pos[0:1, :], pos[1:2, :], pos[2:3, :]
        zero = jnp.zeros((2, TILE), F32)
        one_rows = jnp.concatenate([x, yy, z, x, x, yy, zero], axis=0)
        two_rows = jnp.concatenate([x, yy, z, yy, z, z, zero], axis=0)
        m.first[j] = one_rows
        m.second[j] = two_rows
        stack = jnp.concatenate([one_rows * two_rows, one_rows, two_rows], axis=0)
        parts = [v.astype(F32) for v in split3(stack)]
        stack = jnp.concatenate([parts[0], jnp.ones((8, TILE), F32), parts[1], parts[2]], axis=0).astype(BF16)
        m.moments[j] = stack
        if j < own:
            m.sided[j, 0] = jnp.concatenate([stack, jnp.zeros_like(stack)], axis=1)
            m.sided[j, 1] = jnp.concatenate([jnp.zeros_like(stack), stack], axis=1)

    for j in range(own):
        m.tiles[j] = m.pos[:, j * TILE:(j + 1) * TILE]
        m.ext[j] = m.feat[j * TILE:(j + 1) * TILE, :]
        columns(j)
    for q in peers:
        pl.semaphore_signal(m.passed, inc=1, device_id=at(d, q), device_id_type=MESH)
    m.sums[0] = jnp.zeros_like(m.sums[0])
    m.carry[...] = jnp.zeros_like(m.carry)
    for t in range(4):
        m.hot[t % 2, :, t // 2 * TILE:(t // 2 + 1) * TILE] = (iota == m.rows[t:t + 1, :]).astype(F32).astype(BF16)
    m.far[0] = jnp.zeros_like(m.far[0])
    m.near[...] = jnp.zeros_like(m.near)
    m.eye[...] = (lax.broadcasted_iota(jnp.int32, m.eye.shape, 0)
                  == lax.broadcasted_iota(jnp.int32, m.eye.shape, 1)).astype(F32).astype(BF16)
    for j in range(own):
        table(j)
    for copy in loads[2]:
        copy.wait()
    for k in range(kinds):
        m.radmix[k] = mm(m.radial[k], m.mixing[...]).astype(BF16)
    take(m.recvp, m.r_pos)
    for t in range(4):
        m.tiles[own + t] = m.recvp[t]

    def kernels(g, _):
        for u in range(GROUP):
            p = g * GROUP + u
            h, o, k = m.home[p], m.other[p], m.kind[p]
            row = m.tiles[o]
            d2 = None
            for x in range(3):
                sep = (row[x:x + 1, :] + m.image[x, p].astype(F32) * CELL) - m.col[h, x]
                d2 = sep * sep if d2 is None else d2 + sep * sep
            m.kern_ab[p] = jnp.exp2(d2 * (-LOG2E * m.decay[k])).astype(BF16)
        return 0

    def transposed(g, _):
        for u in range(GROUP):
            p = g * GROUP + u
            h, o, k = m.home[p], m.other[p], m.kind[p]
            row = m.tiles[h]
            d2 = None
            for x in range(3):
                sep = m.col[o, x] - (row[x:x + 1, :] - m.image[x, p].astype(F32) * CELL)
                d2 = sep * sep if d2 is None else d2 + sep * sep
            m.kern_ba[p] = jnp.exp2(d2 * (-LOG2E * m.decay[k]))
        return 0

    half_steps = pairs // GROUP // 2
    lax.fori_loop(0, half_steps, kernels, 0)
    for q in (late, 1 - late):
        t = own + 2 * c + q
        for rows in halves:
            take(m.ext.at[t, rows], m.r_feat.at[q, rows.start // size])
            push(m.ext.at[t, rows], m.ext.at[t, rows], m.r_relay, at(d, partner))
    lax.fori_loop(half_steps, pairs // GROUP, kernels, 0)
    plan_copy.wait()
    take(m.ext.at[pl.ds(own + 2 * mate, 2)], m.r_relay)

    def pair_at(row, i):
        return jnp.clip(m.plan[row, i], 0, pairs - 1)

    def sum_at(row, i):
        return jnp.clip(m.plan[row, i], 0, pairs)

    def seg_f(p):
        return m.home[p] * kinds + m.kind[p]

    def forward(g, _):
        acc = m.carry[...]
        for u in range(WIDE_GROUP):
            i = g * WIDE_GROUP + u
            p = pair_at(0, i)
            last = pair_at(0, jnp.maximum(i - 1, 0))
            keep = (seg_f(p) == seg_f(last)).astype(F32)
            acc = acc * keep + mm(m.kern_ab[p], m.ext[m.other[p]])
            m.sums[i + 1] = acc.astype(BF16)
        m.carry[...] = acc
        return 0

    lax.fori_loop(0, pairs // WIDE_GROUP, forward, 0)

    def message(h):
        left = [m.sums[sum_at(2, h * kinds + k)] for k in range(kinds)]
        return mm(jnp.concatenate(left, axis=1), m.radial[...].reshape(kinds * channels, channels))

    m.msg[...] = message(mate).astype(BF16).reshape(m.msg.shape)
    for q in range(2):
        push(m.msg.at[q], m.msg_in.at[q], m.r_msg.at[q], at(d, partner))
    value = message(c).reshape(m.msg.shape)
    for q in range(2):
        take(m.msg_in.at[q], m.r_msg.at[q])
        m.chip[q] = (value[q] + m.msg_in[q].astype(F32)).astype(BF16)
        push(m.chip.at[q], m.chip_in.at[q], m.r_chip.at[q], at(d, across))
    for t in range(4):
        columns(own + t)
        table(own + t)
    lax.fori_loop(0, pairs // GROUP, transposed, 0)
    for q in range(2):
        take(m.chip_in.at[q], m.r_chip.at[q])
        low = (m.chip[q].astype(F32) + m.chip_in[q].astype(F32)).astype(BF16)
        mixed = mm(low, m.mixing[...])
        sig = jax.nn.sigmoid(mixed)
        slope = (m.readout[...] * sig * (1.0 + mixed * (1.0 - sig))).astype(BF16)
        m.slope[c, q] = slope
        push(m.slope.at[c, q], m.slope.at[c, q], m.r_slope, at(d, partner))
        m.packed[c, q] = low
    push(m.packed.at[c], m.packed.at[c], m.r_packed, at(d, partner))

    take(m.slope.at[mate], m.r_slope)
    slope = m.slope[...].reshape(atoms, channels)
    for k in range(kinds):
        wide = nt(slope, m.radmix[k]).astype(BF16)
        for j in range(own):
            m.weights[j * kinds + k] = wide[j * TILE:(j + 1) * TILE]

    sub = lax.broadcasted_iota(jnp.int32, (8, TILE), 0)
    is_x1, is_y1 = (sub == 0) | (sub == 3) | (sub == 4), (sub == 1) | (sub == 5)
    is_x2, is_y2 = (sub == 0), (sub == 1) | (sub == 3)

    def combine(res, a, b):
        quad = res[0:8] + res[32:40] + res[56:64]
        lin1 = res[8:16] + res[40:48] + res[64:72]
        lin2 = res[16:24] + res[48:56] + res[72:80]
        one = res[24:32]
        force = lin1 - a * one
        virial = -0.5 * (quad - a * lin2 - b * lin1 + a * b * one)
        return jnp.concatenate([force, virial], axis=0)

    def pair_b(i):
        p = pair_at(1, i)
        last = pair_at(1, jnp.maximum(i - 1, 0))
        keep = (m.other[p] == m.other[last]).astype(F32)
        return p, m.home[p], m.other[p], m.kind[p], keep

    def spread_back(g, _):
        acc = m.carry[...]
        for u in range(WIDE_GROUP):
            i = g * WIDE_GROUP + u
            p, h, _, k, keep = pair_b(i)
            acc = acc * keep + mm(m.kern_ba[p].astype(BF16), m.weights[h * kinds + k])
            m.sums[i + 1] = acc.astype(BF16)
        m.carry[...] = acc
        return 0

    def backward(g, _):
        found = []
        for u in range(BACK_GROUP):
            i = g * BACK_GROUP + u
            p, h, o, k, keep = pair_b(i)
            grad = nt(m.ext[o], m.weights[h * kinds + k])
            found.append((i, p, h, o, keep, ((-2.0 * m.decay[k]) * m.kern_ba[p] * grad).astype(BF16)))
        far = m.far[g * BACK_GROUP]
        near = [m.near[j] for j in range(own)]
        results = []
        for one, two in zip(found[::2], found[1::2]):
            weight = jnp.concatenate([one[-1], two[-1]], axis=1)
            close = mm(jnp.concatenate([m.moments[one[3]], m.moments[two[3]]], axis=0), weight)
            beyond = nt(jnp.concatenate([m.sided[one[2], 0], m.sided[two[2], 1]], axis=0), weight)
            size = close.shape[0] // 2
            results += [(close[:size, :TILE], beyond[:size]), (close[size:, TILE:], beyond[size:])]
        for (i, p, h, o, keep, _), (close, beyond) in zip(found, results):
            shift = [m.image[x, p].astype(F32) * CELL for x in range(3)]
            s1 = jnp.where(is_x1, shift[0], jnp.where(is_y1, shift[1], shift[2]))
            s2 = jnp.where(is_x2, shift[0], jnp.where(is_y2, shift[1], shift[2]))
            near_side = combine(close, m.first[h] - s1, m.second[h] - s2)
            far_side = combine(beyond, m.first[o] + s1, m.second[o] + s2)
            for j in range(own):
                near[j] = near[j] + near_side * (h == j).astype(F32)
            far = far * keep + far_side
            m.far[i + 1] = far
        for j in range(own):
            m.near[j] = near[j]
        return 0

    m.carry[...] = jnp.zeros_like(m.carry)
    lax.fori_loop(0, pairs // WIDE_GROUP, spread_back, 0)

    share = channels // n_rep
    slots = (2 - late, 1 + late, 0)
    away = [(slot, own + 2 * mate + slot - 1) for slot in slots[:2]] + [(0, mate)]
    held = [(slot, own + 2 * c + slot - 1) for slot in slots[:2]] + [(0, c)]

    def settle(group):
        total = jnp.concatenate([m.sums[sum_at(3, j)] for _, j in group], axis=0)
        turned = nt(m.eye[:channels, :channels], total).astype(BF16)
        for i, (_, j) in enumerate(group):
            m.gfeat[j] = turned[:, i * TILE:(i + 1) * TILE].reshape(n_rep, share, TILE)

    settle(away)
    for slot, j in away:
        push(m.gfeat.at[j], m.gp.at[slot], m.r_gp.at[slot], at(d, partner))
    settle(held)
    lax.fori_loop(0, 2 - c, backward, 0)
    pl.semaphore_wait(m.passed, n_rep - 1)
    for place, (slot, j) in enumerate(held):
        take(m.gp.at[slot], m.r_gp.at[slot])
        m.sb[slot] = (m.gfeat[j].astype(F32) + m.gp[slot].astype(F32)).astype(BF16)
        if place < 2:
            for q in (across, cross, r, partner):
                push(m.sb.at[slot, q], m.rf.at[slot - 1, c, y], m.r_rf.at[slot - 1],
                     at(dom_at((c + 1) * (2 * slot - 3)), q))
    for q in (across, cross, partner):
        push(m.sb.at[0, q], m.ro.at[r], m.r_ro, at(d, q))
    m.ro[r] = m.sb[0, r]
    lax.fori_loop(2 - c, pairs // BACK_GROUP, backward, 0)
    for t, o in enumerate(OFFSETS):
        m.side[t] = m.far[sum_at(3, own + t)].astype(BF16)
        push(m.side.at[t], m.rs.at[t], m.r_rs, at(dom_at(-o), r))
    take(m.packed.at[mate], m.r_packed)
    pick = (lax.broadcasted_iota(jnp.int32, (channels, share), 0)
            == lax.broadcasted_iota(jnp.int32, (channels, share), 1) + r * share).astype(BF16)
    cols = mm(m.slope[...].reshape(atoms, channels), pick).astype(BF16)
    m.mix[...] = tn(m.packed[...].reshape(atoms, channels), cols).reshape(m.mix.shape)
    def mix_copy(i):
        to = lax.rem(d + i, n_dom)
        return pltpu.make_async_remote_copy(m.mix.at[to], m.rm.at[d], m.sent, m.r_mix,
                                            device_id=at(to, r), device_id_type=MESH)

    lax.fori_loop(1, n_dom, lambda i, _: (mix_copy(i).start(), 0)[1], 0)
    take(m.ro.at[:n_rep - 1], m.r_ro)
    total = jnp.concatenate([m.ro[j].astype(F32) + m.ro[own + j].astype(F32) for j in range(own)], axis=1)
    def gather(group):
        take(m.rf.at[group], m.r_rf.at[group])
        both = nt(jnp.concatenate([m.rf[group, i].reshape(2 * share, TILE) for i in range(2)], axis=1), m.hot[group])
        return both[:share] + both[share:]

    total = total + gather(1 - late)
    m.part[r] = (total + gather(late)).astype(BF16)
    low, high = [pl.ds(i * share // 2, share // 2) for i in range(2)]
    push(m.part.at[r, high], m.part.at[r, high], m.r_part.at[0], at(d, across))
    push(m.part.at[r, low], m.part.at[r, low], m.r_part.at[1], at(d, across))
    push(m.part.at[r, low], m.part.at[r, low], m.r_part.at[1], at(d, cross))
    push(m.part.at[r], m.part.at[r], m.r_part.at[2], at(d, partner))
    take(m.rs, m.r_rs)
    spots = sum(nt(jnp.concatenate([m.rs[i], m.rs[i + 2]], axis=1), m.hot[i]) for i in range(2))
    here = jnp.concatenate([m.far[sum_at(3, j)] + m.near[j] for j in range(own)], axis=1)
    m.pside[r] = (here + spots).astype(BF16)
    for q in (across, cross, partner):
        push(m.pside.at[r], m.pside.at[r], m.r_side, at(d, q))
    def finish(half):
        width = channels // 2
        turned = nt(m.eye[:atoms, :atoms], m.part[pl.ds(2 * half, 2)].reshape(width, atoms))
        m.out_feat[:, pl.ds(pl.multiple_of(half * width, TILE), width)] = turned.astype(BF16)

    take(m.part.at[partner], m.r_part.at[2])
    finish(y)
    take(m.part.at[across, high], m.r_part.at[0])
    push(m.part.at[across, high], m.part.at[across, high], m.r_part.at[3], at(d, partner))
    take(m.rm.at[:n_dom - 1], m.r_mix)
    m.out_mix[...] = lax.fori_loop(1, n_dom, lambda i, v: v + m.rm[lax.rem(d + i, n_dom)], m.mix[d])
    take(m.pside.at[:n_rep - 1], m.r_side)
    final = sum(m.pside[q].astype(F32) for q in range(n_rep))
    m.out_force[...] = final[0:3]
    m.out_virial[...] = final[8:14]
    take(m.part.at[across], m.r_part.at[1])
    take(m.part.at[cross, high], m.r_part.at[3])
    finish(1 - y)
    for copy in started:
        copy.wait_send()
    lax.fori_loop(1, n_dom, lambda i, _: (mix_copy(i).wait_send(), 0)[1], 0)


def copy_out(a, b, c, d, a_h, b_h, c_h, d_h, sem):
    copies = [pltpu.make_async_copy(src, dst, sem)
              for src, dst in ((a, a_h), (b, b_h), (c, c_h), (d, d_h))]
    for copy in copies:
        copy.start()
    for copy in copies:
        copy.wait()


def on_device(n_dom, n_rep, features, positions, radial, mixing, readout, decay, send_rows, pair_home,
              pair_other, pair_kind, pair_image):
    atoms, channels = features.shape
    own = atoms // TILE
    n_ext = own + len(OFFSETS)
    kinds = radial.shape[0]
    pairs = pair_home.shape[0]
    dma = pltpu.SemaphoreType.DMA
    mix_rows, mix_cols = channels // n_dom, channels // n_rep
    quarters = (n_rep, channels // n_rep, TILE)
    readout_row = readout.reshape(1, channels)
    pair_rows = [a.reshape(1, pairs) for a in (pair_home, pair_other, pair_kind)]

    scratch = {
        "feat": pltpu.VMEM(features.shape, BF16), "pos": pltpu.VMEM(positions.shape, F32),
        "rows": pltpu.VMEM(send_rows.shape, jnp.int32), "radial": pltpu.VMEM(radial.shape, BF16),
        "mixing": pltpu.VMEM(mixing.shape, BF16), "readout": pltpu.VMEM(readout_row.shape, F32),
        "decay": pltpu.SMEM(decay.shape, F32), "home": pltpu.SMEM(pair_home.shape, jnp.int32),
        "other": pltpu.SMEM(pair_other.shape, jnp.int32), "kind": pltpu.SMEM(pair_kind.shape, jnp.int32),
        "image": pltpu.SMEM(pair_image.shape, jnp.int32),
        "home_row": pltpu.VMEM((1, pairs), jnp.int32), "other_row": pltpu.VMEM((1, pairs), jnp.int32),
        "kind_row": pltpu.VMEM((1, pairs), jnp.int32),
        "raw": pltpu.VMEM((8, TILE), jnp.int32), "plan_v": pltpu.VMEM((8, TILE), jnp.int32),
        "plan": pltpu.SMEM((8, TILE), jnp.int32),
        "sendf": pltpu.VMEM((2, TILE, channels), BF16), "sendp": pltpu.VMEM((2, 3, TILE), F32),
        "recvp": pltpu.VMEM((4, 3, TILE), F32), "ext": pltpu.VMEM((n_ext, TILE, channels), BF16),
        "tiles": pltpu.VMEM((n_ext, 3, TILE), F32), "col": pltpu.VMEM((n_ext, 3, TILE, TILE), F32),
        "moments": pltpu.VMEM((n_ext, 80, TILE), BF16),
        "sided": pltpu.VMEM((own, 2, 80, 2 * TILE), BF16), "hot": pltpu.VMEM((2, atoms, 2 * TILE), BF16),
        "first": pltpu.VMEM((n_ext, 8, TILE), F32), "second": pltpu.VMEM((n_ext, 8, TILE), F32),
        "kern_ab": pltpu.VMEM((pairs, TILE, TILE), BF16), "kern_ba": pltpu.VMEM((pairs, TILE, TILE), F32),
        "sums": pltpu.VMEM((pairs + 1, TILE, channels), BF16),
        "carry": pltpu.VMEM((TILE, channels), F32), "far": pltpu.VMEM((pairs + 1, 16, TILE), F32),
        "near": pltpu.VMEM((own, 16, TILE), F32),
        "msg": pltpu.VMEM((2, TILE // 2, channels), BF16), "msg_in": pltpu.VMEM((2, TILE // 2, channels), BF16),
        "chip": pltpu.VMEM((2, TILE // 2, channels), BF16), "chip_in": pltpu.VMEM((2, TILE // 2, channels), BF16),
        "slope": pltpu.VMEM((own, 2, TILE // 2, channels), BF16),
        "packed": pltpu.VMEM((own, 2, TILE // 2, channels), BF16), "radmix": pltpu.VMEM(radial.shape, BF16),
        "weights": pltpu.VMEM((own * kinds, TILE, channels), BF16),
        "gfeat": pltpu.VMEM((n_ext, *quarters), BF16), "side": pltpu.VMEM((4, 16, TILE), BF16),
        "gp": pltpu.VMEM((3, *quarters), BF16),
        "sb": pltpu.VMEM((3, *quarters), BF16),
        "rf": pltpu.VMEM((2, 2, 2, *quarters[1:]), BF16), "ro": pltpu.VMEM(quarters, BF16), "rs": pltpu.VMEM((4, 16, TILE), BF16),
        "mix": pltpu.VMEM((n_dom, mix_rows, mix_cols), F32), "rm": pltpu.VMEM((n_dom, mix_rows, mix_cols), F32),
        "part": pltpu.VMEM((n_rep, channels // n_rep, atoms), BF16),
        "eye": pltpu.VMEM((max(atoms, channels),) * 2, BF16),
        "pside": pltpu.VMEM((n_rep, 16, atoms), BF16),
        "load": dma((3,)), "s_plan": dma, "sent": dma, "passed": pltpu.SemaphoreType.REGULAR, "r_pos": dma,
        "r_feat": dma((2, 2)), "r_relay": dma, "r_msg": dma((2,)), "r_chip": dma((2,)), "r_slope": dma,
        "r_packed": dma, "r_gp": dma((3,)), "r_rf": dma((2,)), "r_ro": dma, "r_rs": dma, "r_mix": dma,
        "r_part": dma((4,)), "r_side": dma,
    }

    def shape(dims, dtype):
        return jax.ShapeDtypeStruct(dims, dtype)

    results = pl.pallas_call(
        functools.partial(kernel, INPUTS + OUTPUTS + tuple(scratch), n_dom, n_rep),
        out_shape=(shape((atoms, channels), BF16), shape((3, atoms), F32), shape((6, atoms), F32),
                   shape((mix_rows, mix_cols), F32)),
        in_specs=[HBM] * len(INPUTS),
        out_specs=(VMEM,) * 4,
        scratch_shapes=list(scratch.values()),
        compiler_params=pltpu.CompilerParams(collective_id=0, has_side_effects=True, vmem_limit_bytes=48 << 20),
        name="layer",
    )(*[pltpu.with_memory_space_constraint(a, pltpu.HBM) for a in (
        features, positions, send_rows, radial, mixing, readout_row, decay, pair_home, pair_other, pair_kind,
        pair_image, *pair_rows)])
    return pl.pallas_call(
        copy_out,
        out_shape=tuple(shape(a.shape, a.dtype) for a in results),
        in_specs=[VMEM] * 4,
        out_specs=(HBM,) * 4,
        scratch_shapes=[dma],
        compiler_params=pltpu.CompilerParams(vmem_limit_bytes=4 << 20),
        name="copy_out",
    )(*results)


def solution(mesh):
    in_specs = (
        P("dom", None),
        P(None, "dom"),
        P(),
        P(),
        P(),
        P(),
        P(None, "dom"),
        P(("dom", "rep")),
        P(("dom", "rep")),
        P(("dom", "rep")),
        P(None, ("dom", "rep")),
    )
    out_specs = (P("dom", None), P(None, "dom"), P(None, "dom"), P("dom", "rep"))
    body = functools.partial(on_device, mesh.shape["dom"], mesh.shape["rep"])
    return jax.shard_map(body, mesh=mesh, in_specs=in_specs, out_specs=out_specs, check_vma=False)
```

```python
import functools
import types

import jax
import jax.numpy as jnp
from jax import lax
from jax.experimental import pallas as pl
from jax.experimental.pallas import tpu as pltpu
from jax.sharding import PartitionSpec as P

TILE = 128
OFFSETS = (1, -1, 2, -2)
CELL = 2.0
GROUP = 4
WIDE_GROUP = 48
BACK_GROUP = 12
LOG2E = 1.4426950408889634
F32 = jnp.float32
BF16 = jnp.bfloat16
MESH = pl.DeviceIdType.MESH
VMEM = pl.BlockSpec(memory_space=pltpu.VMEM)
HBM = pl.BlockSpec(memory_space=pltpu.HBM)
INPUTS = ("feat_h", "pos_h", "rows_h", "radial_h", "mixing_h", "readout_h", "decay_h", "home_h", "other_h",
          "kind_h", "image_h", "home_row_h", "other_row_h", "kind_row_h")
OUTPUTS = ("out_feat", "out_force", "out_virial", "out_mix")


def nt(a, b):
    return lax.dot_general(a, b, (((1,), (1,)), ((), ())), preferred_element_type=F32)


def tn(a, b):
    return lax.dot_general(a, b, (((0,), (0,)), ((), ())), preferred_element_type=F32)


def mm(a, b):
    return jnp.dot(a, b, preferred_element_type=F32)


def split3(x):
    hi = x.astype(BF16)
    rest = x - hi.astype(F32)
    mid = rest.astype(BF16)
    low = (rest - mid.astype(F32)).astype(BF16)
    return hi, mid, low


def order_pairs(seg, lanes, subs):
    row = jnp.broadcast_to(seg, (TILE, TILE))
    col = jnp.transpose(row)
    before = (col < row) | ((col == row) & (subs < lanes))
    rank = jnp.sum(before.astype(jnp.int32), axis=0, keepdims=True)
    rank = jnp.transpose(jnp.broadcast_to(rank, (TILE, TILE)))
    order = jnp.sum(jnp.where(rank == lanes, subs, 0), axis=0, keepdims=True)
    upto = jnp.sum((col <= lanes).astype(jnp.int32), axis=0, keepdims=True)
    below = jnp.sum((col < lanes).astype(jnp.int32), axis=0, keepdims=True)
    return order, jnp.where(upto > below, upto, 0)


def kernel(names, n_dom, n_rep, *refs):
    m = types.SimpleNamespace(**dict(zip(names, refs)))
    d = lax.axis_index("dom")
    r = lax.axis_index("rep")
    y = lax.div(r, 2)
    c = lax.rem(r, 2)
    mate = 1 - c
    partner = r + 1 - 2 * c
    across = r + 2 - 4 * y
    cross = across + 1 - 2 * c
    atoms, channels = m.feat.shape
    own = atoms // TILE
    late = lax.div(n_dom - 1 - d, n_dom // 2)
    pairs = m.home.shape[0]
    kinds = m.radial.shape[0]
    n_ext = m.tiles.shape[0]
    size = TILE // 2
    halves = [pl.ds(i * size, size) for i in range(2)]

    def dom_at(o):
        return lax.rem(d + o + n_dom, n_dom)

    def at(dom, rep):
        return {"dom": dom, "rep": rep}

    groups = ((m.rows_h, m.rows), (m.feat_h, m.feat), (m.pos_h, m.pos)), (
        (m.home_row_h, m.home_row), (m.other_row_h, m.other_row), (m.kind_row_h, m.kind_row)), (
        (m.radial_h, m.radial), (m.decay_h, m.decay), (m.home_h, m.home), (m.other_h, m.other),
        (m.kind_h, m.kind), (m.image_h, m.image), (m.mixing_h, m.mixing), (m.readout_h, m.readout))
    loads = [[pltpu.make_async_copy(src, dst, m.load.at[i]) for src, dst in group]
             for i, group in enumerate(groups)]
    for copy in loads[0]:
        copy.start()
    barrier = pltpu.get_barrier_semaphore()
    mine = (c + 1, -(c + 1))
    theirs = (2 - c, c - 2)
    peers = [lax.rem(r + i, n_rep) for i in range(1, n_rep)]

    def hello(dom, rep):
        pl.semaphore_signal(barrier, inc=1, device_id=at(dom, rep), device_id_type=MESH)

    def greet(i, _):
        hello(lax.rem(d + i, n_dom), r)
        return 0

    lax.fori_loop(1, n_dom, greet, 0)
    for o in mine:
        hello(dom_at(o), partner)
    for o in theirs:
        hello(dom_at(o), partner)
    for q in peers:
        hello(d, q)
    for copy in loads[1] + loads[2]:
        copy.start()

    started = []

    def push(src, dst, rs, target):
        copy = pltpu.make_async_remote_copy(src, dst, m.sent, rs, device_id=target, device_id_type=MESH)
        copy.start()
        started.append(copy)

    def take(dst, rs):
        pltpu.make_async_remote_copy(dst, dst, m.sent, rs, device_id=at(d, partner), device_id_type=MESH).wait_recv()

    for copy in loads[0]:
        copy.wait()
    iota = lax.broadcasted_iota(jnp.int32, (atoms, TILE), 0)
    hots = []
    for q in range(2):
        hot = (iota == m.rows[pl.ds(2 * c + q, 1), :]).astype(F32)
        hots.append(hot.astype(BF16))
        m.sendp[q] = jnp.dot(m.pos[...], hot, precision=lax.Precision.HIGHEST, preferred_element_type=F32)
    for q in range(2):
        m.sendf[q] = tn(hots[q], m.feat[...]).astype(BF16)
    pl.semaphore_wait(barrier, 4 + n_rep - 1 + n_dom - 1)
    for q in (late, 1 - late):
        for i, rep in enumerate((r, partner)):
            push(m.sendp.at[q], m.recvp.at[2 * c + q], m.r_pos,
                 at(dom_at((c + 1) * (1 - 2 * q)), rep))
    for q in (late, 1 - late):
        for rows in halves:
            push(m.sendf.at[q, rows], m.ext.at[own + 2 * c + q, rows], m.r_feat.at[q, rows.start // size],
                 at(dom_at((c + 1) * (1 - 2 * q)), r))

    for copy in loads[1]:
        copy.wait()
    m.raw[...] = jnp.zeros_like(m.raw)
    for i, src in enumerate((m.home_row, m.kind_row, m.other_row)):
        m.raw[i:i + 1, :pairs] = src[...]
    raw = m.raw[...]
    lanes = lax.broadcasted_iota(jnp.int32, (TILE, TILE), 1)
    subs = lax.broadcasted_iota(jnp.int32, (TILE, TILE), 0)
    real = lanes[0:1] < pairs
    order_f, end_f = order_pairs(jnp.where(real, raw[0:1] * kinds + raw[1:2], TILE), lanes, subs)
    order_b, end_b = order_pairs(jnp.where(real, raw[2:3], TILE), lanes, subs)
    m.plan_v[...] = jnp.concatenate(
        [order_f, order_b, end_f, end_b, jnp.zeros((4, TILE), jnp.int32)], axis=0)
    plan_copy = pltpu.make_async_copy(m.plan_v, m.plan, m.load.at[0])
    plan_copy.start()

    def columns(j):
        for x in range(3):
            m.col[j, x] = jnp.transpose(jnp.broadcast_to(m.tiles[j][x:x + 1, :], (TILE, TILE)))

    def table(j):
        pos = m.tiles[j]
        x, yy, z = pos[0:1, :], pos[1:2, :], pos[2:3, :]
        zero = jnp.zeros((2, TILE), F32)
        one_rows = jnp.concatenate([x, yy, z, x, x, yy, zero], axis=0)
        two_rows = jnp.concatenate([x, yy, z, yy, z, z, zero], axis=0)
        m.first[j] = one_rows
        m.second[j] = two_rows
        stack = jnp.concatenate([one_rows * two_rows, one_rows, two_rows], axis=0)
        parts = [v.astype(F32) for v in split3(stack)]
        stack = jnp.concatenate([parts[0], jnp.ones((8, TILE), F32), parts[1], parts[2]], axis=0).astype(BF16)
        m.moments[j] = stack
        if j < own:
            m.sided[j, 0] = jnp.concatenate([stack, jnp.zeros_like(stack)], axis=1)
            m.sided[j, 1] = jnp.concatenate([jnp.zeros_like(stack), stack], axis=1)

    for j in range(own):
        m.tiles[j] = m.pos[:, j * TILE:(j + 1) * TILE]
        m.ext[j] = m.feat[j * TILE:(j + 1) * TILE, :]
        columns(j)
    for q in peers:
        pl.semaphore_signal(m.passed, inc=1, device_id=at(d, q), device_id_type=MESH)
    m.sums[0] = jnp.zeros_like(m.sums[0])
    m.carry[...] = jnp.zeros_like(m.carry)
    for t in range(4):
        m.hot[t % 2, :, t // 2 * TILE:(t // 2 + 1) * TILE] = (iota == m.rows[t:t + 1, :]).astype(F32).astype(BF16)
    m.far[0] = jnp.zeros_like(m.far[0])
    m.near[...] = jnp.zeros_like(m.near)
    m.eye[...] = (lax.broadcasted_iota(jnp.int32, m.eye.shape, 0)
                  == lax.broadcasted_iota(jnp.int32, m.eye.shape, 1)).astype(F32).astype(BF16)
    for j in range(own):
        table(j)
    for copy in loads[2]:
        copy.wait()
    for k in range(kinds):
        m.radmix[k] = mm(m.radial[k], m.mixing[...]).astype(BF16)
    take(m.recvp, m.r_pos)
    for t in range(4):
        m.tiles[own + t] = m.recvp[t]

    def kernels(g, _):
        for u in range(GROUP):
            p = g * GROUP + u
            h, o, k = m.home[p], m.other[p], m.kind[p]
            row = m.tiles[o]
            d2 = None
            for x in range(3):
                sep = (row[x:x + 1, :] + m.image[x, p].astype(F32) * CELL) - m.col[h, x]
                d2 = sep * sep if d2 is None else d2 + sep * sep
            m.kern_ab[p] = jnp.exp2(d2 * (-LOG2E * m.decay[k])).astype(BF16)
        return 0

    def transposed(g, _):
        for u in range(GROUP):
            p = g * GROUP + u
            h, o, k = m.home[p], m.other[p], m.kind[p]
            row = m.tiles[h]
            d2 = None
            for x in range(3):
                sep = m.col[o, x] - (row[x:x + 1, :] - m.image[x, p].astype(F32) * CELL)
                d2 = sep * sep if d2 is None else d2 + sep * sep
            m.kern_ba[p] = jnp.exp2(d2 * (-LOG2E * m.decay[k]))
        return 0

    half_steps = pairs // GROUP // 2
    lax.fori_loop(0, half_steps, kernels, 0)
    for q in (late, 1 - late):
        t = own + 2 * c + q
        for rows in halves:
            take(m.ext.at[t, rows], m.r_feat.at[q, rows.start // size])
            push(m.ext.at[t, rows], m.ext.at[t, rows], m.near_sem.at[2], at(d, partner))
    lax.fori_loop(half_steps, pairs // GROUP, kernels, 0)
    plan_copy.wait()
    take(m.ext.at[pl.ds(own + 2 * mate, 2)], m.near_sem.at[2])

    def pair_at(row, i):
        return jnp.clip(m.plan[row, i], 0, pairs - 1)

    def sum_at(row, i):
        return jnp.clip(m.plan[row, i], 0, pairs)

    def seg_f(p):
        return m.home[p] * kinds + m.kind[p]

    def forward(g, _):
        acc = m.carry[...]
        for u in range(WIDE_GROUP):
            i = g * WIDE_GROUP + u
            p = pair_at(0, i)
            last = pair_at(0, jnp.maximum(i - 1, 0))
            keep = (seg_f(p) == seg_f(last)).astype(F32)
            acc = acc * keep + mm(m.kern_ab[p], m.ext[m.other[p]])
            m.sums[i + 1] = acc.astype(BF16)
        m.carry[...] = acc
        return 0

    lax.fori_loop(0, pairs // WIDE_GROUP, forward, 0)

    def message(h):
        left = [m.sums[sum_at(2, h * kinds + k)] for k in range(kinds)]
        return mm(jnp.concatenate(left, axis=1), m.radial[...].reshape(kinds * channels, channels))

    m.msg[...] = message(mate).astype(BF16).reshape(m.msg.shape)
    for q in range(2):
        push(m.msg.at[q], m.msg_in.at[q], m.near_sem.at[q], at(d, partner))
    value = message(c).reshape(m.msg.shape)
    for q in range(2):
        take(m.msg_in.at[q], m.near_sem.at[q])
        m.chip[q] = (value[q] + m.msg_in[q].astype(F32)).astype(BF16)
        push(m.chip.at[q], m.chip_in.at[q], m.r_chip.at[q], at(d, across))
    for t in range(4):
        columns(own + t)
        table(own + t)
    lax.fori_loop(0, pairs // GROUP, transposed, 0)
    for q in range(2):
        take(m.chip_in.at[q], m.r_chip.at[q])
        low = (m.chip[q].astype(F32) + m.chip_in[q].astype(F32)).astype(BF16)
        mixed = mm(low, m.mixing[...])
        sig = jax.nn.sigmoid(mixed)
        slope = (m.readout[...] * sig * (1.0 + mixed * (1.0 - sig))).astype(BF16)
        m.slope[c, q] = slope
        push(m.slope.at[c, q], m.slope.at[c, q], m.near_sem.at[3], at(d, partner))
        m.packed[c, q] = low
    push(m.packed.at[c], m.packed.at[c], m.near_sem.at[4], at(d, partner))

    take(m.slope.at[mate], m.near_sem.at[3])
    slope = m.slope[...].reshape(atoms, channels)
    for k in range(kinds):
        wide = nt(slope, m.radmix[k]).astype(BF16)
        for j in range(own):
            m.weights[j * kinds + k] = wide[j * TILE:(j + 1) * TILE]

    sub = lax.broadcasted_iota(jnp.int32, (8, TILE), 0)
    is_x1, is_y1 = (sub == 0) | (sub == 3) | (sub == 4), (sub == 1) | (sub == 5)
    is_x2, is_y2 = (sub == 0), (sub == 1) | (sub == 3)

    def combine(res, a, b):
        quad = res[0:8] + res[32:40] + res[56:64]
        lin1 = res[8:16] + res[40:48] + res[64:72]
        lin2 = res[16:24] + res[48:56] + res[72:80]
        one = res[24:32]
        force = lin1 - a * one
        virial = -0.5 * (quad - a * lin2 - b * lin1 + a * b * one)
        return jnp.concatenate([force, virial], axis=0)

    def pair_b(i):
        p = pair_at(1, i)
        last = pair_at(1, jnp.maximum(i - 1, 0))
        keep = (m.other[p] == m.other[last]).astype(F32)
        return p, m.home[p], m.other[p], m.kind[p], keep

    def spread_back(g, _):
        acc = m.carry[...]
        for u in range(WIDE_GROUP):
            i = g * WIDE_GROUP + u
            p, h, _, k, keep = pair_b(i)
            acc = acc * keep + mm(m.kern_ba[p].astype(BF16), m.weights[h * kinds + k])
            m.sums[i + 1] = acc.astype(BF16)
        m.carry[...] = acc
        return 0

    def backward(g, _):
        found = []
        for u in range(BACK_GROUP):
            i = g * BACK_GROUP + u
            p, h, o, k, keep = pair_b(i)
            grad = nt(m.ext[o], m.weights[h * kinds + k])
            found.append((i, p, h, o, keep, ((-2.0 * m.decay[k]) * m.kern_ba[p] * grad).astype(BF16)))
        far = m.far[g * BACK_GROUP]
        near = [m.near[j] for j in range(own)]
        results = []
        for one, two in zip(found[::2], found[1::2]):
            weight = jnp.concatenate([one[-1], two[-1]], axis=1)
            close = mm(jnp.concatenate([m.moments[one[3]], m.moments[two[3]]], axis=0), weight)
            beyond = nt(jnp.concatenate([m.sided[one[2], 0], m.sided[two[2], 1]], axis=0), weight)
            size = close.shape[0] // 2
            results += [(close[:size, :TILE], beyond[:size]), (close[size:, TILE:], beyond[size:])]
        for (i, p, h, o, keep, _), (close, beyond) in zip(found, results):
            shift = [m.image[x, p].astype(F32) * CELL for x in range(3)]
            s1 = jnp.where(is_x1, shift[0], jnp.where(is_y1, shift[1], shift[2]))
            s2 = jnp.where(is_x2, shift[0], jnp.where(is_y2, shift[1], shift[2]))
            near_side = combine(close, m.first[h] - s1, m.second[h] - s2)
            far_side = combine(beyond, m.first[o] + s1, m.second[o] + s2)
            for j in range(own):
                near[j] = near[j] + near_side * (h == j).astype(F32)
            far = far * keep + far_side
            m.far[i + 1] = far
        for j in range(own):
            m.near[j] = near[j]
        return 0

    m.carry[...] = jnp.zeros_like(m.carry)
    lax.fori_loop(0, pairs // WIDE_GROUP, spread_back, 0)

    share = channels // n_rep
    slots = (2 - late, 1 + late, 0)
    away = [(slot, own + 2 * mate + slot - 1) for slot in slots[:2]] + [(0, mate)]
    held = [(slot, own + 2 * c + slot - 1) for slot in slots[:2]] + [(0, c)]

    def settle(group):
        total = jnp.concatenate([m.sums[sum_at(3, j)] for _, j in group], axis=0)
        turned = nt(m.eye[:channels, :channels], total).astype(BF16)
        for i, (_, j) in enumerate(group):
            m.gfeat[j] = turned[:, i * TILE:(i + 1) * TILE].reshape(n_rep, share, TILE)

    for group in (away[:1], away[1:]):
        settle(group)
        for slot, j in group:
            push(m.gfeat.at[j], m.gp.at[slot], m.near_sem.at[slot], at(d, partner))
    settle(held)
    lax.fori_loop(0, 2 - 2 * c, backward, 0)
    pl.semaphore_wait(m.passed, n_rep - 1)
    for place, (slot, j) in enumerate(held):
        take(m.gp.at[slot], m.near_sem.at[slot])
        m.sb[slot] = (m.gfeat[j].astype(F32) + m.gp[slot].astype(F32)).astype(BF16)
        if place < 2:
            for q in (across, cross, r, partner):
                push(m.sb.at[slot, q], m.rf.at[slot - 1, c, y], m.r_rf.at[slot - 1],
                     at(dom_at((c + 1) * (2 * slot - 3)), q))
    for q in (across, cross, partner):
        push(m.sb.at[0, q], m.ro.at[r], m.r_ro, at(d, q))
    m.ro[r] = m.sb[0, r]
    lax.fori_loop(2 - 2 * c, pairs // BACK_GROUP, backward, 0)
    for t, o in enumerate(OFFSETS):
        m.side[t] = m.far[sum_at(3, own + t)].astype(BF16)
        push(m.side.at[t], m.rs.at[t], m.r_rs, at(dom_at(-o), r))
    take(m.packed.at[mate], m.near_sem.at[4])
    pick = (lax.broadcasted_iota(jnp.int32, (channels, share), 0)
            == lax.broadcasted_iota(jnp.int32, (channels, share), 1) + r * share).astype(BF16)
    cols = mm(m.slope[...].reshape(atoms, channels), pick).astype(BF16)
    m.mix[...] = tn(m.packed[...].reshape(atoms, channels), cols).reshape(m.mix.shape)
    def mix_copy(i):
        to = lax.rem(d + i, n_dom)
        return pltpu.make_async_remote_copy(m.mix.at[to], m.rm.at[d], m.sent, m.r_mix,
                                            device_id=at(to, r), device_id_type=MESH)

    lax.fori_loop(1, n_dom, lambda i, _: (mix_copy(i).start(), 0)[1], 0)
    take(m.ro.at[:n_rep - 1], m.r_ro)
    total = jnp.concatenate([m.ro[j].astype(F32) + m.ro[own + j].astype(F32) for j in range(own)], axis=1)
    def gather(group):
        take(m.rf.at[group], m.r_rf.at[group])
        both = nt(jnp.concatenate([m.rf[group, i].reshape(2 * share, TILE) for i in range(2)], axis=1), m.hot[group])
        return both[:share] + both[share:]

    total = total + gather(1 - late)
    m.part[r] = (total + gather(late)).astype(BF16)
    low, high = pl.ds(0, share - share // 4), pl.ds(share - share // 4, share // 4)
    push(m.part.at[r, high], m.part.at[r, high], m.r_chip.at[0], at(d, across))
    push(m.part.at[r, low], m.part.at[r, low], m.r_chip.at[1], at(d, across))
    push(m.part.at[r, low], m.part.at[r, low], m.r_chip.at[1], at(d, cross))
    push(m.part.at[r], m.part.at[r], m.near_sem.at[3], at(d, partner))
    take(m.rs, m.r_rs)
    spots = sum(nt(jnp.concatenate([m.rs[i], m.rs[i + 2]], axis=1), m.hot[i]) for i in range(2))
    here = jnp.concatenate([m.far[sum_at(3, j)] + m.near[j] for j in range(own)], axis=1)
    m.pside[r] = (here + spots).astype(BF16)
    for q in (across, cross, partner):
        push(m.pside.at[r], m.pside.at[r], m.r_pos, at(d, q))
    def finish(half):
        width = channels // 2
        turned = nt(m.eye[:atoms, :atoms], m.part[pl.ds(2 * half, 2)].reshape(width, atoms))
        m.out_feat[:, pl.ds(pl.multiple_of(half * width, TILE), width)] = turned.astype(BF16)

    take(m.part.at[partner], m.near_sem.at[3])
    finish(y)
    take(m.part.at[across, high], m.r_chip.at[0])
    push(m.part.at[across, high], m.part.at[across, high], m.near_sem.at[4], at(d, partner))
    take(m.rm.at[:n_dom - 1], m.r_mix)
    m.out_mix[...] = lax.fori_loop(1, n_dom, lambda i, v: v + m.rm[lax.rem(d + i, n_dom)], m.mix[d])
    take(m.pside.at[:n_rep - 1], m.r_pos)
    final = sum(m.pside[q].astype(F32) for q in range(n_rep))
    m.out_force[...] = final[0:3]
    m.out_virial[...] = final[8:14]
    take(m.part.at[pl.ds(2 * (1 - y), 2), low], m.r_chip.at[1])
    take(m.part.at[cross, high], m.near_sem.at[4])
    finish(1 - y)
    for copy in started:
        copy.wait_send()
    lax.fori_loop(1, n_dom, lambda i, _: (mix_copy(i).wait_send(), 0)[1], 0)


def copy_out(a, b, c, d, a_h, b_h, c_h, d_h, sem):
    copies = [pltpu.make_async_copy(src, dst, sem)
              for src, dst in ((a, a_h), (b, b_h), (c, c_h), (d, d_h))]
    for copy in copies:
        copy.start()
    for copy in copies:
        copy.wait()


def on_device(n_dom, n_rep, features, positions, radial, mixing, readout, decay, send_rows, pair_home,
              pair_other, pair_kind, pair_image):
    atoms, channels = features.shape
    own = atoms // TILE
    n_ext = own + len(OFFSETS)
    kinds = radial.shape[0]
    pairs = pair_home.shape[0]
    dma = pltpu.SemaphoreType.DMA
    mix_rows, mix_cols = channels // n_dom, channels // n_rep
    quarters = (n_rep, channels // n_rep, TILE)
    readout_row = readout.reshape(1, channels)
    pair_rows = [a.reshape(1, pairs) for a in (pair_home, pair_other, pair_kind)]

    scratch = {
        "feat": pltpu.VMEM(features.shape, BF16), "pos": pltpu.VMEM(positions.shape, F32),
        "rows": pltpu.VMEM(send_rows.shape, jnp.int32), "radial": pltpu.VMEM(radial.shape, BF16),
        "mixing": pltpu.VMEM(mixing.shape, BF16), "readout": pltpu.VMEM(readout_row.shape, F32),
        "decay": pltpu.SMEM(decay.shape, F32), "home": pltpu.SMEM(pair_home.shape, jnp.int32),
        "other": pltpu.SMEM(pair_other.shape, jnp.int32), "kind": pltpu.SMEM(pair_kind.shape, jnp.int32),
        "image": pltpu.SMEM(pair_image.shape, jnp.int32),
        "home_row": pltpu.VMEM((1, pairs), jnp.int32), "other_row": pltpu.VMEM((1, pairs), jnp.int32),
        "kind_row": pltpu.VMEM((1, pairs), jnp.int32),
        "raw": pltpu.VMEM((8, TILE), jnp.int32), "plan_v": pltpu.VMEM((8, TILE), jnp.int32),
        "plan": pltpu.SMEM((8, TILE), jnp.int32),
        "sendf": pltpu.VMEM((2, TILE, channels), BF16), "sendp": pltpu.VMEM((2, 3, TILE), F32),
        "recvp": pltpu.VMEM((4, 3, TILE), F32), "ext": pltpu.VMEM((n_ext, TILE, channels), BF16),
        "tiles": pltpu.VMEM((n_ext, 3, TILE), F32), "col": pltpu.VMEM((n_ext, 3, TILE, TILE), F32),
        "moments": pltpu.VMEM((n_ext, 80, TILE), BF16),
        "sided": pltpu.VMEM((own, 2, 80, 2 * TILE), BF16), "hot": pltpu.VMEM((2, atoms, 2 * TILE), BF16),
        "first": pltpu.VMEM((n_ext, 8, TILE), F32), "second": pltpu.VMEM((n_ext, 8, TILE), F32),
        "kern_ab": pltpu.VMEM((pairs, TILE, TILE), BF16), "kern_ba": pltpu.VMEM((pairs, TILE, TILE), F32),
        "sums": pltpu.VMEM((pairs + 1, TILE, channels), BF16),
        "carry": pltpu.VMEM((TILE, channels), F32), "far": pltpu.VMEM((pairs + 1, 16, TILE), F32),
        "near": pltpu.VMEM((own, 16, TILE), F32),
        "msg": pltpu.VMEM((2, TILE // 2, channels), BF16), "msg_in": pltpu.VMEM((2, TILE // 2, channels), BF16),
        "chip": pltpu.VMEM((2, TILE // 2, channels), BF16), "chip_in": pltpu.VMEM((2, TILE // 2, channels), BF16),
        "slope": pltpu.VMEM((own, 2, TILE // 2, channels), BF16),
        "packed": pltpu.VMEM((own, 2, TILE // 2, channels), BF16), "radmix": pltpu.VMEM(radial.shape, BF16),
        "weights": pltpu.VMEM((own * kinds, TILE, channels), BF16),
        "gfeat": pltpu.VMEM((n_ext, *quarters), BF16), "side": pltpu.VMEM((4, 16, TILE), BF16),
        "gp": pltpu.VMEM((3, *quarters), BF16),
        "sb": pltpu.VMEM((3, *quarters), BF16),
        "rf": pltpu.VMEM((2, 2, 2, *quarters[1:]), BF16), "ro": pltpu.VMEM(quarters, BF16), "rs": pltpu.VMEM((4, 16, TILE), BF16),
        "mix": pltpu.VMEM((n_dom, mix_rows, mix_cols), F32), "rm": pltpu.VMEM((n_dom, mix_rows, mix_cols), F32),
        "part": pltpu.VMEM((n_rep, channels // n_rep, atoms), BF16),
        "eye": pltpu.VMEM((max(atoms, channels),) * 2, BF16),
        "pside": pltpu.VMEM((n_rep, 16, atoms), BF16),
        "load": dma((3,)), "sent": dma, "passed": pltpu.SemaphoreType.REGULAR, "r_pos": dma,
        "r_feat": dma((2, 2)), "near_sem": dma((5,)), "r_chip": dma((2,)),
        "r_rf": dma((2,)), "r_ro": dma, "r_rs": dma, "r_mix": dma,
    }

    def shape(dims, dtype):
        return jax.ShapeDtypeStruct(dims, dtype)

    results = pl.pallas_call(
        functools.partial(kernel, INPUTS + OUTPUTS + tuple(scratch), n_dom, n_rep),
        out_shape=(shape((atoms, channels), BF16), shape((3, atoms), F32), shape((6, atoms), F32),
                   shape((mix_rows, mix_cols), F32)),
        in_specs=[HBM] * len(INPUTS),
        out_specs=(VMEM,) * 4,
        scratch_shapes=list(scratch.values()),
        compiler_params=pltpu.CompilerParams(collective_id=0, has_side_effects=True, vmem_limit_bytes=48 << 20),
        name="layer",
    )(*[pltpu.with_memory_space_constraint(a, pltpu.HBM) for a in (
        features, positions, send_rows, radial, mixing, readout_row, decay, pair_home, pair_other, pair_kind,
        pair_image, *pair_rows)])
    return pl.pallas_call(
        copy_out,
        out_shape=tuple(shape(a.shape, a.dtype) for a in results),
        in_specs=[VMEM] * 4,
        out_specs=(HBM,) * 4,
        scratch_shapes=[dma],
        compiler_params=pltpu.CompilerParams(vmem_limit_bytes=4 << 20),
        name="copy_out",
    )(*results)


def solution(mesh):
    in_specs = (
        P("dom", None),
        P(None, "dom"),
        P(),
        P(),
        P(),
        P(),
        P(None, "dom"),
        P(("dom", "rep")),
        P(("dom", "rep")),
        P(("dom", "rep")),
        P(None, ("dom", "rep")),
    )
    out_specs = (P("dom", None), P(None, "dom"), P(None, "dom"), P("dom", "rep"))
    body = functools.partial(on_device, mesh.shape["dom"], mesh.shape["rep"])
    return jax.shard_map(body, mesh=mesh, in_specs=in_specs, out_specs=out_specs, check_vma=False)
```

```python
import functools
import types

import jax
import jax.numpy as jnp
from jax import lax
from jax.experimental import pallas as pl
from jax.experimental.pallas import tpu as pltpu
from jax.sharding import PartitionSpec as P

TILE = 128
OFFSETS = (1, -1, 2, -2)
CELL = 2.0
GROUP = 4
WIDE_GROUP = 48
BACK_GROUP = 24
LOG2E = 1.4426950408889634
F32 = jnp.float32
BF16 = jnp.bfloat16
MESH = pl.DeviceIdType.MESH
VMEM = pl.BlockSpec(memory_space=pltpu.VMEM)
HBM = pl.BlockSpec(memory_space=pltpu.HBM)
INPUTS = ("feat_h", "pos_h", "rows_h", "radial_h", "mixing_h", "readout_h", "decay_h", "home_h", "other_h",
          "kind_h", "image_h", "home_row_h", "other_row_h", "kind_row_h")
OUTPUTS = ("out_feat", "out_force", "out_virial", "out_mix")


def nt(a, b):
    return lax.dot_general(a, b, (((1,), (1,)), ((), ())), preferred_element_type=F32)


def tn(a, b):
    return lax.dot_general(a, b, (((0,), (0,)), ((), ())), preferred_element_type=F32)


def mm(a, b):
    return jnp.dot(a, b, preferred_element_type=F32)


def split3(x):
    hi = x.astype(BF16)
    rest = x - hi.astype(F32)
    mid = rest.astype(BF16)
    low = (rest - mid.astype(F32)).astype(BF16)
    return hi, mid, low


def order_pairs(seg, lanes, subs):
    row = jnp.broadcast_to(seg, (TILE, TILE))
    col = jnp.transpose(row)
    before = (col < row) | ((col == row) & (subs < lanes))
    rank = jnp.sum(before.astype(jnp.int32), axis=0, keepdims=True)
    rank = jnp.transpose(jnp.broadcast_to(rank, (TILE, TILE)))
    order = jnp.sum(jnp.where(rank == lanes, subs, 0), axis=0, keepdims=True)
    upto = jnp.sum((col <= lanes).astype(jnp.int32), axis=0, keepdims=True)
    below = jnp.sum((col < lanes).astype(jnp.int32), axis=0, keepdims=True)
    return order, jnp.where(upto > below, upto, 0)


def kernel(names, n_dom, n_rep, *refs):
    m = types.SimpleNamespace(**dict(zip(names, refs)))
    d = lax.axis_index("dom")
    r = lax.axis_index("rep")
    y = lax.div(r, 2)
    c = lax.rem(r, 2)
    mate = 1 - c
    partner = r + 1 - 2 * c
    across = r + 2 - 4 * y
    cross = across + 1 - 2 * c
    atoms, channels = m.feat.shape
    own = atoms // TILE
    late = lax.div(n_dom - 1 - d, n_dom // 2)
    pairs = m.home.shape[0]
    kinds = m.radial.shape[0]
    n_ext = m.tiles.shape[0]
    size = TILE // 2
    halves = [pl.ds(i * size, size) for i in range(2)]

    def dom_at(o):
        return lax.rem(d + o + n_dom, n_dom)

    def at(dom, rep):
        return {"dom": dom, "rep": rep}

    groups = ((m.rows_h, m.rows), (m.feat_h, m.feat), (m.pos_h, m.pos)), (
        (m.home_row_h, m.home_row), (m.other_row_h, m.other_row), (m.kind_row_h, m.kind_row)), (
        (m.radial_h, m.radial), (m.decay_h, m.decay), (m.home_h, m.home), (m.other_h, m.other),
        (m.kind_h, m.kind), (m.image_h, m.image), (m.mixing_h, m.mixing), (m.readout_h, m.readout))
    loads = [[pltpu.make_async_copy(src, dst, m.load.at[i]) for src, dst in group]
             for i, group in enumerate(groups)]
    for copy in loads[0]:
        copy.start()
    barrier = pltpu.get_barrier_semaphore()
    mine = (c + 1, -(c + 1))
    theirs = (2 - c, c - 2)
    peers = [lax.rem(r + i, n_rep) for i in range(1, n_rep)]

    def hello(dom, rep):
        pl.semaphore_signal(barrier, inc=1, device_id=at(dom, rep), device_id_type=MESH)

    def greet(i, _):
        hello(lax.rem(d + i, n_dom), r)
        return 0

    lax.fori_loop(1, n_dom, greet, 0)
    for o in mine:
        hello(dom_at(o), partner)
    for o in theirs:
        hello(dom_at(o), partner)
    for q in peers:
        hello(d, q)
    for copy in loads[1] + loads[2]:
        copy.start()

    started = []

    def push(src, dst, rs, target):
        copy = pltpu.make_async_remote_copy(src, dst, m.sent, rs, device_id=target, device_id_type=MESH)
        copy.start()
        started.append(copy)

    def take(dst, rs):
        pltpu.make_async_remote_copy(dst, dst, m.sent, rs, device_id=at(d, partner), device_id_type=MESH).wait_recv()

    for copy in loads[0]:
        copy.wait()
    iota = lax.broadcasted_iota(jnp.int32, (atoms, TILE), 0)
    hots = []
    for q in range(2):
        hot = (iota == m.rows[pl.ds(2 * c + q, 1), :]).astype(F32)
        hots.append(hot.astype(BF16))
        m.sendp[q] = jnp.dot(m.pos[...], hot, precision=lax.Precision.HIGHEST, preferred_element_type=F32)
    for q in range(2):
        m.sendf[q] = tn(hots[q], m.feat[...]).astype(BF16)
    pl.semaphore_wait(barrier, 4 + n_rep - 1 + n_dom - 1)
    for q in (late, 1 - late):
        for i, rep in enumerate((r, partner)):
            push(m.sendp.at[q], m.recvp.at[2 * c + q], m.r_pos,
                 at(dom_at((c + 1) * (1 - 2 * q)), rep))
    for q in (late, 1 - late):
        for rows in halves:
            push(m.sendf.at[q, rows], m.ext.at[own + 2 * c + q, rows], m.r_feat.at[q, rows.start // size],
                 at(dom_at((c + 1) * (1 - 2 * q)), r))

    for copy in loads[1]:
        copy.wait()
    m.raw[...] = jnp.zeros_like(m.raw)
    for i, src in enumerate((m.home_row, m.kind_row, m.other_row)):
        m.raw[i:i + 1, :pairs] = src[...]
    raw = m.raw[...]
    lanes = lax.broadcasted_iota(jnp.int32, (TILE, TILE), 1)
    subs = lax.broadcasted_iota(jnp.int32, (TILE, TILE), 0)
    real = lanes[0:1] < pairs
    order_f, end_f = order_pairs(jnp.where(real, raw[0:1] * kinds + raw[1:2], TILE), lanes, subs)
    order_b, end_b = order_pairs(jnp.where(real, raw[2:3], TILE), lanes, subs)
    m.plan_v[...] = jnp.concatenate(
        [order_f, order_b, end_f, end_b, jnp.zeros((4, TILE), jnp.int32)], axis=0)
    plan_copy = pltpu.make_async_copy(m.plan_v, m.plan, m.load.at[0])
    plan_copy.start()

    def columns(j):
        for x in range(3):
            m.col[j, x] = jnp.transpose(jnp.broadcast_to(m.tiles[j][x:x + 1, :], (TILE, TILE)))

    def table(j):
        pos = m.tiles[j]
        x, yy, z = pos[0:1, :], pos[1:2, :], pos[2:3, :]
        zero = jnp.zeros((2, TILE), F32)
        one_rows = jnp.concatenate([x, yy, z, x, x, yy, zero], axis=0)
        two_rows = jnp.concatenate([x, yy, z, yy, z, z, zero], axis=0)
        m.first[j] = one_rows
        m.second[j] = two_rows
        stack = jnp.concatenate([one_rows * two_rows, one_rows, two_rows], axis=0)
        parts = [v.astype(F32) for v in split3(stack)]
        stack = jnp.concatenate([parts[0], jnp.ones((8, TILE), F32), parts[1], parts[2]], axis=0).astype(BF16)
        m.moments[j] = stack
        if j < own:
            m.sided[j, 0] = jnp.concatenate([stack, jnp.zeros_like(stack)], axis=1)
            m.sided[j, 1] = jnp.concatenate([jnp.zeros_like(stack), stack], axis=1)

    for j in range(own):
        m.tiles[j] = m.pos[:, j * TILE:(j + 1) * TILE]
        m.ext[j] = m.feat[j * TILE:(j + 1) * TILE, :]
        columns(j)
    for q in peers:
        pl.semaphore_signal(m.passed, inc=1, device_id=at(d, q), device_id_type=MESH)
    m.sums[0] = jnp.zeros_like(m.sums[0])
    m.carry[...] = jnp.zeros_like(m.carry)
    for t in range(4):
        m.hot[t % 2, :, t // 2 * TILE:(t // 2 + 1) * TILE] = (iota == m.rows[t:t + 1, :]).astype(F32).astype(BF16)
    m.far[0] = jnp.zeros_like(m.far[0])
    m.near[...] = jnp.zeros_like(m.near)
    m.eye[...] = (lax.broadcasted_iota(jnp.int32, m.eye.shape, 0)
                  == lax.broadcasted_iota(jnp.int32, m.eye.shape, 1)).astype(F32).astype(BF16)
    for j in range(own):
        table(j)
    for copy in loads[2]:
        copy.wait()
    for k in range(kinds):
        m.radmix[k] = mm(m.radial[k], m.mixing[...]).astype(BF16)
    take(m.recvp, m.r_pos)
    for t in range(4):
        m.tiles[own + t] = m.recvp[t]

    def kernels(g, _):
        for u in range(GROUP):
            p = g * GROUP + u
            h, o, k = m.home[p], m.other[p], m.kind[p]
            row = m.tiles[o]
            d2 = None
            for x in range(3):
                sep = (row[x:x + 1, :] + m.image[x, p].astype(F32) * CELL) - m.col[h, x]
                d2 = sep * sep if d2 is None else d2 + sep * sep
            m.kern_ab[p] = jnp.exp2(d2 * (-LOG2E * m.decay[k])).astype(BF16)
        return 0

    def transposed(g, _):
        for u in range(GROUP):
            p = g * GROUP + u
            h, o, k = m.home[p], m.other[p], m.kind[p]
            row = m.tiles[h]
            d2 = None
            for x in range(3):
                sep = m.col[o, x] - (row[x:x + 1, :] - m.image[x, p].astype(F32) * CELL)
                d2 = sep * sep if d2 is None else d2 + sep * sep
            m.kern_ba[p] = jnp.exp2(d2 * (-LOG2E * m.decay[k]))
        return 0

    half_steps = pairs // GROUP // 2
    lax.fori_loop(0, half_steps, kernels, 0)
    for q in (late, 1 - late):
        t = own + 2 * c + q
        for rows in halves:
            take(m.ext.at[t, rows], m.r_feat.at[q, rows.start // size])
            push(m.ext.at[t, rows], m.ext.at[t, rows], m.near_sem.at[2], at(d, partner))
    lax.fori_loop(half_steps, pairs // GROUP, kernels, 0)
    plan_copy.wait()
    take(m.ext.at[pl.ds(own + 2 * mate, 2)], m.near_sem.at[2])

    def pair_at(row, i):
        return jnp.clip(m.plan[row, i], 0, pairs - 1)

    def sum_at(row, i):
        return jnp.clip(m.plan[row, i], 0, pairs)

    def seg_f(p):
        return m.home[p] * kinds + m.kind[p]

    def forward(g, _):
        acc = m.carry[...]
        for u in range(WIDE_GROUP):
            i = g * WIDE_GROUP + u
            p = pair_at(0, i)
            last = pair_at(0, jnp.maximum(i - 1, 0))
            keep = (seg_f(p) == seg_f(last)).astype(F32)
            acc = acc * keep + mm(m.kern_ab[p], m.ext[m.other[p]])
            m.sums[i + 1] = acc.astype(BF16)
        m.carry[...] = acc
        return 0

    lax.fori_loop(0, pairs // WIDE_GROUP, forward, 0)

    def message(h):
        left = [m.sums[sum_at(2, h * kinds + k)] for k in range(kinds)]
        return mm(jnp.concatenate(left, axis=1), m.radial[...].reshape(kinds * channels, channels))

    m.msg[...] = message(mate).astype(BF16).reshape(m.msg.shape)
    for q in range(2):
        push(m.msg.at[q], m.msg_in.at[q], m.near_sem.at[q], at(d, partner))
    value = message(c).reshape(m.msg.shape)
    for q in range(2):
        take(m.msg_in.at[q], m.near_sem.at[q])
        m.chip[q] = (value[q] + m.msg_in[q].astype(F32)).astype(BF16)
        push(m.chip.at[q], m.chip_in.at[q], m.r_chip.at[q], at(d, across))
    def twin(near):
        return pltpu.make_async_remote_copy(
            m.chip.at[1], m.twin.at[1 - near], m.sent, m.near_sem.at[5] if near else m.r_chip.at[2],
            device_id=at(d, partner if near else cross), device_id_type=MESH)

    @pl.when(c == 0)
    def _():
        twin(0).start()
        twin(1).start()

    for t in range(4):
        columns(own + t)
        table(own + t)
    lax.fori_loop(0, pairs // GROUP, transposed, 0)
    def activate(one, two):
        low = (one.astype(F32) + two.astype(F32)).astype(BF16)
        mixed = mm(low, m.mixing[...])
        sig = jax.nn.sigmoid(mixed)
        return low, (m.readout[...] * sig * (1.0 + mixed * (1.0 - sig))).astype(BF16)

    def slope_copy(q):
        return pltpu.make_async_remote_copy(m.slope.at[c, q], m.slope.at[c, q], m.sent, m.near_sem.at[3],
                                            device_id=at(d, partner), device_id_type=MESH)

    for q in range(2):
        take(m.chip_in.at[q], m.r_chip.at[q])
        low, slope = activate(m.chip[q], m.chip_in[q])
        m.slope[c, q] = slope
        m.packed[c, q] = low
        if q == 0:
            slope_copy(q).start()
        else:
            @pl.when(c == 1)
            def _():
                slope_copy(q).start()
    push(m.packed.at[c], m.packed.at[c], m.near_sem.at[4], at(d, partner))

    @pl.when(c == 0)
    def _():
        take(m.slope.at[mate], m.near_sem.at[3])

    @pl.when(c == 1)
    def _():
        take(m.slope.at[mate, 0], m.near_sem.at[3])
        take(m.twin.at[0], m.near_sem.at[5])
        take(m.twin.at[1], m.r_chip.at[2])
        m.slope[mate, 1] = activate(m.twin[0], m.twin[1])[1]
    slope = m.slope[...].reshape(atoms, channels)
    for k in range(kinds):
        wide = nt(slope, m.radmix[k]).astype(BF16)
        for j in range(own):
            m.weights[j * kinds + k] = wide[j * TILE:(j + 1) * TILE]

    sub = lax.broadcasted_iota(jnp.int32, (8, TILE), 0)
    is_x1, is_y1 = (sub == 0) | (sub == 3) | (sub == 4), (sub == 1) | (sub == 5)
    is_x2, is_y2 = (sub == 0), (sub == 1) | (sub == 3)

    def combine(res, a, b):
        quad = res[0:8] + res[32:40] + res[56:64]
        lin1 = res[8:16] + res[40:48] + res[64:72]
        lin2 = res[16:24] + res[48:56] + res[72:80]
        one = res[24:32]
        force = lin1 - a * one
        virial = -0.5 * (quad - a * lin2 - b * lin1 + a * b * one)
        return jnp.concatenate([force, virial], axis=0)

    def pair_b(i):
        p = pair_at(1, i)
        last = pair_at(1, jnp.maximum(i - 1, 0))
        keep = (m.other[p] == m.other[last]).astype(F32)
        return p, m.home[p], m.other[p], m.kind[p], keep

    def spread_back(g, _):
        acc = m.carry[...]
        for u in range(WIDE_GROUP):
            i = g * WIDE_GROUP + u
            p, h, _, k, keep = pair_b(i)
            acc = acc * keep + mm(m.kern_ba[p].astype(BF16), m.weights[h * kinds + k])
            m.sums[i + 1] = acc.astype(BF16)
        m.carry[...] = acc
        return 0

    def backward(g, _):
        found = []
        for u in range(BACK_GROUP):
            i = g * BACK_GROUP + u
            p, h, o, k, keep = pair_b(i)
            grad = nt(m.ext[o], m.weights[h * kinds + k])
            found.append((i, p, h, o, keep, ((-2.0 * m.decay[k]) * m.kern_ba[p] * grad).astype(BF16)))
        far = m.far[g * BACK_GROUP]
        near = [m.near[j] for j in range(own)]
        results = []
        for one, two in zip(found[::2], found[1::2]):
            weight = jnp.concatenate([one[-1], two[-1]], axis=1)
            close = mm(jnp.concatenate([m.moments[one[3]], m.moments[two[3]]], axis=0), weight)
            beyond = nt(jnp.concatenate([m.sided[one[2], 0], m.sided[two[2], 1]], axis=0), weight)
            size = close.shape[0] // 2
            results += [(close[:size, :TILE], beyond[:size]), (close[size:, TILE:], beyond[size:])]
        for (i, p, h, o, keep, _), (close, beyond) in zip(found, results):
            shift = [m.image[x, p].astype(F32) * CELL for x in range(3)]
            s1 = jnp.where(is_x1, shift[0], jnp.where(is_y1, shift[1], shift[2]))
            s2 = jnp.where(is_x2, shift[0], jnp.where(is_y2, shift[1], shift[2]))
            near_side = combine(close, m.first[h] - s1, m.second[h] - s2)
            far_side = combine(beyond, m.first[o] + s1, m.second[o] + s2)
            for j in range(own):
                near[j] = near[j] + near_side * (h == j).astype(F32)
            far = far * keep + far_side
            m.far[i + 1] = far
        for j in range(own):
            m.near[j] = near[j]
        return 0

    m.carry[...] = jnp.zeros_like(m.carry)
    lax.fori_loop(0, pairs // WIDE_GROUP, spread_back, 0)

    share = channels // n_rep
    slots = (2 - late, 1 + late, 0)
    away = [(slot, own + 2 * mate + slot - 1) for slot in slots[:2]] + [(0, mate)]
    held = [(slot, own + 2 * c + slot - 1) for slot in slots[:2]] + [(0, c)]

    def settle(group):
        total = jnp.concatenate([m.sums[sum_at(3, j)] for _, j in group], axis=0)
        turned = nt(m.eye[:channels, :channels], total).astype(BF16)
        for i, (_, j) in enumerate(group):
            m.gfeat[j] = turned[:, i * TILE:(i + 1) * TILE].reshape(n_rep, share, TILE)

    for group in (away[:1], away[1:]):
        settle(group)
        for slot, j in group:
            push(m.gfeat.at[j], m.gp.at[slot], m.near_sem.at[slot], at(d, partner))
    settle(held)
    lax.fori_loop(0, 1 - c, backward, 0)
    pl.semaphore_wait(m.passed, n_rep - 1)
    for place, (slot, j) in enumerate(held):
        take(m.gp.at[slot], m.near_sem.at[slot])
        m.sb[slot] = (m.gfeat[j].astype(F32) + m.gp[slot].astype(F32)).astype(BF16)
        if place < 2:
            for q in (across, cross, r, partner):
                push(m.sb.at[slot, q], m.rf.at[slot - 1, c, y], m.r_rf.at[slot - 1],
                     at(dom_at((c + 1) * (2 * slot - 3)), q))
    for q in (across, cross, partner):
        push(m.sb.at[0, q], m.ro.at[r], m.r_ro, at(d, q))
    m.ro[r] = m.sb[0, r]
    lax.fori_loop(1 - c, pairs // BACK_GROUP, backward, 0)
    for t, o in enumerate(OFFSETS):
        m.side[t] = m.far[sum_at(3, own + t)].astype(BF16)
        push(m.side.at[t], m.rs.at[t], m.r_rs, at(dom_at(-o), r))
    take(m.packed.at[mate], m.near_sem.at[4])
    pick = (lax.broadcasted_iota(jnp.int32, (channels, share), 0)
            == lax.broadcasted_iota(jnp.int32, (channels, share), 1) + r * share).astype(BF16)
    cols = mm(m.slope[...].reshape(atoms, channels), pick).astype(BF16)
    m.mix[...] = tn(m.packed[...].reshape(atoms, channels), cols).reshape(m.mix.shape)
    def mix_copy(i):
        to = lax.rem(d + i, n_dom)
        return pltpu.make_async_remote_copy(m.mix.at[to], m.rm.at[d], m.sent, m.r_mix,
                                            device_id=at(to, r), device_id_type=MESH)

    lax.fori_loop(1, n_dom, lambda i, _: (mix_copy(i).start(), 0)[1], 0)
    take(m.ro.at[:n_rep - 1], m.r_ro)
    total = jnp.concatenate([m.ro[j].astype(F32) + m.ro[own + j].astype(F32) for j in range(own)], axis=1)
    def gather(group):
        take(m.rf.at[group], m.r_rf.at[group])
        both = nt(jnp.concatenate([m.rf[group, i].reshape(2 * share, TILE) for i in range(2)], axis=1), m.hot[group])
        return both[:share] + both[share:]

    total = total + gather(1 - late)
    m.part[r] = (total + gather(late)).astype(BF16)
    low, high = pl.ds(0, share - share // 4), pl.ds(share - share // 4, share // 4)
    push(m.part.at[r, high], m.part.at[r, high], m.r_chip.at[0], at(d, across))
    push(m.part.at[r, low], m.part.at[r, low], m.r_chip.at[1], at(d, across))
    push(m.part.at[r, low], m.part.at[r, low], m.r_chip.at[1], at(d, cross))
    push(m.part.at[r], m.part.at[r], m.near_sem.at[3], at(d, partner))
    take(m.rs, m.r_rs)
    spots = sum(nt(jnp.concatenate([m.rs[i], m.rs[i + 2]], axis=1), m.hot[i]) for i in range(2))
    here = jnp.concatenate([m.far[sum_at(3, j)] + m.near[j] for j in range(own)], axis=1)
    m.pside[r] = (here + spots).astype(BF16)
    for q in (across, cross, partner):
        push(m.pside.at[r], m.pside.at[r], m.r_pos, at(d, q))
    def finish(half):
        width = channels // 2
        turned = nt(m.eye[:atoms, :atoms], m.part[pl.ds(2 * half, 2)].reshape(width, atoms))
        m.out_feat[:, pl.ds(pl.multiple_of(half * width, TILE), width)] = turned.astype(BF16)

    take(m.part.at[partner], m.near_sem.at[3])
    finish(y)
    take(m.part.at[across, high], m.r_chip.at[0])
    push(m.part.at[across, high], m.part.at[across, high], m.near_sem.at[4], at(d, partner))
    take(m.rm.at[:n_dom - 1], m.r_mix)
    m.out_mix[...] = lax.fori_loop(1, n_dom, lambda i, v: v + m.rm[lax.rem(d + i, n_dom)], m.mix[d])
    take(m.pside.at[:n_rep - 1], m.r_pos)
    final = sum(m.pside[q].astype(F32) for q in range(n_rep))
    m.out_force[...] = final[0:3]
    m.out_virial[...] = final[8:14]
    take(m.part.at[pl.ds(2 * (1 - y), 2), low], m.r_chip.at[1])
    take(m.part.at[cross, high], m.near_sem.at[4])
    finish(1 - y)
    for copy in started + [slope_copy(0)]:
        copy.wait_send()

    @pl.when(c == 0)
    def _():
        twin(0).wait_send()
        twin(1).wait_send()

    @pl.when(c == 1)
    def _():
        slope_copy(1).wait_send()

    lax.fori_loop(1, n_dom, lambda i, _: (mix_copy(i).wait_send(), 0)[1], 0)


def copy_out(a, b, c, d, a_h, b_h, c_h, d_h, sem):
    copies = [pltpu.make_async_copy(src, dst, sem)
              for src, dst in ((a, a_h), (b, b_h), (c, c_h), (d, d_h))]
    for copy in copies:
        copy.start()
    for copy in copies:
        copy.wait()


def on_device(n_dom, n_rep, features, positions, radial, mixing, readout, decay, send_rows, pair_home,
              pair_other, pair_kind, pair_image):
    atoms, channels = features.shape
    own = atoms // TILE
    n_ext = own + len(OFFSETS)
    kinds = radial.shape[0]
    pairs = pair_home.shape[0]
    dma = pltpu.SemaphoreType.DMA
    mix_rows, mix_cols = channels // n_dom, channels // n_rep
    quarters = (n_rep, channels // n_rep, TILE)
    readout_row = readout.reshape(1, channels)
    pair_rows = [a.reshape(1, pairs) for a in (pair_home, pair_other, pair_kind)]

    scratch = {
        "feat": pltpu.VMEM(features.shape, BF16), "pos": pltpu.VMEM(positions.shape, F32),
        "rows": pltpu.VMEM(send_rows.shape, jnp.int32), "radial": pltpu.VMEM(radial.shape, BF16),
        "mixing": pltpu.VMEM(mixing.shape, BF16), "readout": pltpu.VMEM(readout_row.shape, F32),
        "decay": pltpu.SMEM(decay.shape, F32), "home": pltpu.SMEM(pair_home.shape, jnp.int32),
        "other": pltpu.SMEM(pair_other.shape, jnp.int32), "kind": pltpu.SMEM(pair_kind.shape, jnp.int32),
        "image": pltpu.SMEM(pair_image.shape, jnp.int32),
        "home_row": pltpu.VMEM((1, pairs), jnp.int32), "other_row": pltpu.VMEM((1, pairs), jnp.int32),
        "kind_row": pltpu.VMEM((1, pairs), jnp.int32),
        "raw": pltpu.VMEM((8, TILE), jnp.int32), "plan_v": pltpu.VMEM((8, TILE), jnp.int32),
        "plan": pltpu.SMEM((8, TILE), jnp.int32),
        "sendf": pltpu.VMEM((2, TILE, channels), BF16), "sendp": pltpu.VMEM((2, 3, TILE), F32),
        "recvp": pltpu.VMEM((4, 3, TILE), F32), "ext": pltpu.VMEM((n_ext, TILE, channels), BF16),
        "tiles": pltpu.VMEM((n_ext, 3, TILE), F32), "col": pltpu.VMEM((n_ext, 3, TILE, TILE), F32),
        "moments": pltpu.VMEM((n_ext, 80, TILE), BF16),
        "sided": pltpu.VMEM((own, 2, 80, 2 * TILE), BF16), "hot": pltpu.VMEM((2, atoms, 2 * TILE), BF16),
        "first": pltpu.VMEM((n_ext, 8, TILE), F32), "second": pltpu.VMEM((n_ext, 8, TILE), F32),
        "kern_ab": pltpu.VMEM((pairs, TILE, TILE), BF16), "kern_ba": pltpu.VMEM((pairs, TILE, TILE), F32),
        "sums": pltpu.VMEM((pairs + 1, TILE, channels), BF16),
        "carry": pltpu.VMEM((TILE, channels), F32), "far": pltpu.VMEM((pairs + 1, 16, TILE), F32),
        "near": pltpu.VMEM((own, 16, TILE), F32),
        "msg": pltpu.VMEM((2, TILE // 2, channels), BF16), "msg_in": pltpu.VMEM((2, TILE // 2, channels), BF16),
        "chip": pltpu.VMEM((2, TILE // 2, channels), BF16), "twin": pltpu.VMEM((2, TILE // 2, channels), BF16), "chip_in": pltpu.VMEM((2, TILE // 2, channels), BF16),
        "slope": pltpu.VMEM((own, 2, TILE // 2, channels), BF16),
        "packed": pltpu.VMEM((own, 2, TILE // 2, channels), BF16), "radmix": pltpu.VMEM(radial.shape, BF16),
        "weights": pltpu.VMEM((own * kinds, TILE, channels), BF16),
        "gfeat": pltpu.VMEM((n_ext, *quarters), BF16), "side": pltpu.VMEM((4, 16, TILE), BF16),
        "gp": pltpu.VMEM((3, *quarters), BF16),
        "sb": pltpu.VMEM((3, *quarters), BF16),
        "rf": pltpu.VMEM((2, 2, 2, *quarters[1:]), BF16), "ro": pltpu.VMEM(quarters, BF16), "rs": pltpu.VMEM((4, 16, TILE), BF16),
        "mix": pltpu.VMEM((n_dom, mix_rows, mix_cols), F32), "rm": pltpu.VMEM((n_dom, mix_rows, mix_cols), F32),
        "part": pltpu.VMEM((n_rep, channels // n_rep, atoms), BF16),
        "eye": pltpu.VMEM((max(atoms, channels),) * 2, BF16),
        "pside": pltpu.VMEM((n_rep, 16, atoms), BF16),
        "load": dma((3,)), "sent": dma, "passed": pltpu.SemaphoreType.REGULAR, "r_pos": dma,
        "r_feat": dma((2, 2)), "near_sem": dma((6,)), "r_chip": dma((3,)),
        "r_rf": dma((2,)), "r_ro": dma, "r_rs": dma, "r_mix": dma,
    }

    def shape(dims, dtype):
        return jax.ShapeDtypeStruct(dims, dtype)

    results = pl.pallas_call(
        functools.partial(kernel, INPUTS + OUTPUTS + tuple(scratch), n_dom, n_rep),
        out_shape=(shape((atoms, channels), BF16), shape((3, atoms), F32), shape((6, atoms), F32),
                   shape((mix_rows, mix_cols), F32)),
        in_specs=[HBM] * len(INPUTS),
        out_specs=(VMEM,) * 4,
        scratch_shapes=list(scratch.values()),
        compiler_params=pltpu.CompilerParams(collective_id=0, has_side_effects=True, vmem_limit_bytes=48 << 20),
        name="layer",
    )(*[pltpu.with_memory_space_constraint(a, pltpu.HBM) for a in (
        features, positions, send_rows, radial, mixing, readout_row, decay, pair_home, pair_other, pair_kind,
        pair_image, *pair_rows)])
    return pl.pallas_call(
        copy_out,
        out_shape=tuple(shape(a.shape, a.dtype) for a in results),
        in_specs=[VMEM] * 4,
        out_specs=(HBM,) * 4,
        scratch_shapes=[dma],
        compiler_params=pltpu.CompilerParams(vmem_limit_bytes=4 << 20),
        name="copy_out",
    )(*results)


def solution(mesh):
    in_specs = (
        P("dom", None),
        P(None, "dom"),
        P(),
        P(),
        P(),
        P(),
        P(None, "dom"),
        P(("dom", "rep")),
        P(("dom", "rep")),
        P(("dom", "rep")),
        P(None, ("dom", "rep")),
    )
    out_specs = (P("dom", None), P(None, "dom"), P(None, "dom"), P("dom", "rep"))
    body = functools.partial(on_device, mesh.shape["dom"], mesh.shape["rep"])
    return jax.shard_map(body, mesh=mesh, in_specs=in_specs, out_specs=out_specs, check_vma=False)
```

```python
import functools
import types

import jax
import jax.numpy as jnp
from jax import lax
from jax.experimental import pallas as pl
from jax.experimental.pallas import tpu as pltpu
from jax.sharding import PartitionSpec as P

TILE = 128
OFFSETS = (1, -1, 2, -2)
CELL = 2.0
GROUP = 8
LOG2E = 1.4426950408889634
F32 = jnp.float32
BF16 = jnp.bfloat16
MESH = pl.DeviceIdType.MESH
VMEM = pl.BlockSpec(memory_space=pltpu.VMEM)
HBM = pl.BlockSpec(memory_space=pltpu.HBM)
INPUTS = ("feat_h", "pos_h", "rows_h", "radial_h", "mixing_h", "readout_h", "decay_h", "home_h", "other_h",
          "kind_h", "image_h", "home_row_h", "other_row_h", "kind_row_h")
OUTPUTS = ("out_feat", "out_force", "out_virial", "out_mix")


def nt(a, b):
    return lax.dot_general(a, b, (((1,), (1,)), ((), ())), preferred_element_type=F32)


def tn(a, b):
    return lax.dot_general(a, b, (((0,), (0,)), ((), ())), preferred_element_type=F32)


def mm(a, b):
    return jnp.dot(a, b, preferred_element_type=F32)


def split3(x):
    hi = x.astype(BF16)
    rest = x - hi.astype(F32)
    mid = rest.astype(BF16)
    low = (rest - mid.astype(F32)).astype(BF16)
    return hi, mid, low


def order_pairs(seg, lanes, subs):
    row = jnp.broadcast_to(seg, (TILE, TILE))
    col = jnp.transpose(row)
    before = (col < row) | ((col == row) & (subs < lanes))
    rank = jnp.sum(before.astype(jnp.int32), axis=0, keepdims=True)
    rank = jnp.transpose(jnp.broadcast_to(rank, (TILE, TILE)))
    order = jnp.sum(jnp.where(rank == lanes, subs, 0), axis=0, keepdims=True)
    upto = jnp.sum((col <= lanes).astype(jnp.int32), axis=0, keepdims=True)
    below = jnp.sum((col < lanes).astype(jnp.int32), axis=0, keepdims=True)
    return order, jnp.where(upto > below, upto, 0)


def kernel(names, n_dom, n_rep, *refs):
    m = types.SimpleNamespace(**dict(zip(names, refs)))
    d = lax.axis_index("dom")
    r = lax.axis_index("rep")
    y = lax.div(r, 2)
    c = lax.rem(r, 2)
    mate = 1 - c
    partner = r + 1 - 2 * c
    across = r + 2 - 4 * y
    cross = across + 1 - 2 * c
    atoms, channels = m.feat.shape
    own = atoms // TILE
    late = lax.div(n_dom - 1 - d, n_dom // 2)
    pairs = m.home.shape[0]
    back_group = pairs // 2
    kinds = m.radial.shape[0]
    n_ext = m.tiles.shape[0]
    size = TILE // 2
    halves = [pl.ds(i * size, size) for i in range(2)]

    def dom_at(o):
        return lax.rem(d + o + n_dom, n_dom)

    def at(dom, rep):
        return {"dom": dom, "rep": rep}

    groups = ((m.rows_h, m.rows), (m.feat_h, m.feat), (m.pos_h, m.pos)), (
        (m.home_row_h, m.home_row), (m.other_row_h, m.other_row), (m.kind_row_h, m.kind_row)), (
        (m.radial_h, m.radial), (m.decay_h, m.decay), (m.home_h, m.home), (m.other_h, m.other),
        (m.kind_h, m.kind), (m.image_h, m.image), (m.mixing_h, m.mixing), (m.readout_h, m.readout))
    loads = [[pltpu.make_async_copy(src, dst, m.load.at[i]) for src, dst in group]
             for i, group in enumerate(groups)]
    for copy in loads[0]:
        copy.start()
    barrier = pltpu.get_barrier_semaphore()
    mine = (c + 1, -(c + 1))
    theirs = (2 - c, c - 2)
    peers = [lax.rem(r + i, n_rep) for i in range(1, n_rep)]

    def hello(dom, rep):
        pl.semaphore_signal(barrier, inc=1, device_id=at(dom, rep), device_id_type=MESH)

    def greet(i, _):
        hello(lax.rem(d + i, n_dom), r)
        return 0

    lax.fori_loop(1, n_dom, greet, 0)
    for o in mine:
        hello(dom_at(o), partner)
    for o in theirs:
        hello(dom_at(o), partner)
    for q in peers:
        hello(d, q)
    for copy in loads[1] + loads[2]:
        copy.start()

    started = []

    def push(src, dst, rs, target):
        copy = pltpu.make_async_remote_copy(src, dst, m.sent, rs, device_id=target, device_id_type=MESH)
        copy.start()
        started.append(copy)

    def take(dst, rs):
        pltpu.make_async_remote_copy(dst, dst, m.sent, rs, device_id=at(d, partner), device_id_type=MESH).wait_recv()

    for copy in loads[0]:
        copy.wait()
    iota = lax.broadcasted_iota(jnp.int32, (atoms, TILE), 0)
    hots = []
    for q in range(2):
        hot = (iota == m.rows[pl.ds(2 * c + q, 1), :]).astype(F32)
        hots.append(hot.astype(BF16))
        m.sendp[q] = jnp.dot(m.pos[...], hot, precision=lax.Precision.HIGHEST, preferred_element_type=F32)
    for q in range(2):
        m.sendf[q] = tn(hots[q], m.feat[...]).astype(BF16)
    pl.semaphore_wait(barrier, 4 + n_rep - 1 + n_dom - 1)
    for q in (late, 1 - late):
        for i, rep in enumerate((r, partner)):
            push(m.sendp.at[q], m.recvp.at[2 * c + q], m.r_pos,
                 at(dom_at((c + 1) * (1 - 2 * q)), rep))
    for q in (late, 1 - late):
        for rows in halves:
            push(m.sendf.at[q, rows], m.ext.at[own + 2 * c + q, rows], m.r_feat.at[q, rows.start // size],
                 at(dom_at((c + 1) * (1 - 2 * q)), r))

    for copy in loads[1]:
        copy.wait()
    m.raw[...] = jnp.zeros_like(m.raw)
    for i, src in enumerate((m.home_row, m.kind_row, m.other_row)):
        m.raw[i:i + 1, :pairs] = src[...]
    raw = m.raw[...]
    lanes = lax.broadcasted_iota(jnp.int32, (TILE, TILE), 1)
    subs = lax.broadcasted_iota(jnp.int32, (TILE, TILE), 0)
    real = lanes[0:1] < pairs
    order_f, end_f = order_pairs(jnp.where(real, raw[0:1] * kinds + raw[1:2], TILE), lanes, subs)
    order_b, end_b = order_pairs(jnp.where(real, raw[2:3], TILE), lanes, subs)
    m.plan_v[...] = jnp.concatenate(
        [order_f, order_b, end_f, end_b, jnp.zeros((4, TILE), jnp.int32)], axis=0)
    plan_copy = pltpu.make_async_copy(m.plan_v, m.plan, m.load.at[0])
    plan_copy.start()

    def columns(j):
        for x in range(3):
            m.col[j, x] = jnp.transpose(jnp.broadcast_to(m.tiles[j][x:x + 1, :], (TILE, TILE)))

    def table(j):
        pos = m.tiles[j]
        x, yy, z = pos[0:1, :], pos[1:2, :], pos[2:3, :]
        zero = jnp.zeros((2, TILE), F32)
        one_rows = jnp.concatenate([x, yy, z, x, x, yy, zero], axis=0)
        two_rows = jnp.concatenate([x, yy, z, yy, z, z, zero], axis=0)
        m.first[j] = one_rows
        m.second[j] = two_rows
        stack = jnp.concatenate([one_rows * two_rows, one_rows, two_rows], axis=0)
        parts = [v.astype(F32) for v in split3(stack)]
        stack = jnp.concatenate([parts[0], jnp.ones((8, TILE), F32), parts[1], parts[2]], axis=0).astype(BF16)
        m.moments[j] = stack
        if j < own:
            m.sided[j, 0] = jnp.concatenate([stack, jnp.zeros_like(stack)], axis=1)
            m.sided[j, 1] = jnp.concatenate([jnp.zeros_like(stack), stack], axis=1)

    for j in range(own):
        m.tiles[j] = m.pos[:, j * TILE:(j + 1) * TILE]
        m.ext[j] = m.feat[j * TILE:(j + 1) * TILE, :]
        columns(j)
    for q in peers:
        pl.semaphore_signal(m.passed, inc=1, device_id=at(d, q), device_id_type=MESH)
    m.sums[0] = jnp.zeros_like(m.sums[0])
    for t in range(4):
        m.hot[t % 2, :, t // 2 * TILE:(t // 2 + 1) * TILE] = (iota == m.rows[t:t + 1, :]).astype(F32).astype(BF16)
    m.far[0] = jnp.zeros_like(m.far[0])
    m.near[...] = jnp.zeros_like(m.near)
    m.eye[...] = (lax.broadcasted_iota(jnp.int32, m.eye.shape, 0)
                  == lax.broadcasted_iota(jnp.int32, m.eye.shape, 1)).astype(F32).astype(BF16)
    for j in range(own):
        table(j)
    for copy in loads[2]:
        copy.wait()
    for k in range(kinds):
        m.radmix[k] = mm(m.radial[k], m.mixing[...]).astype(BF16)
    take(m.recvp, m.r_pos)
    for t in range(4):
        m.tiles[own + t] = m.recvp[t]

    def kernels(g, _):
        for u in range(GROUP):
            p = g * GROUP + u
            h, o, k = m.home[p], m.other[p], m.kind[p]
            row = m.tiles[o]
            d2 = None
            for x in range(3):
                sep = (row[x:x + 1, :] + m.image[x, p].astype(F32) * CELL) - m.col[h, x]
                d2 = sep * sep if d2 is None else d2 + sep * sep
            m.kern_ab[p] = jnp.exp2(d2 * (-LOG2E * m.decay[k])).astype(BF16)
        return 0

    def transposed(g, _):
        for u in range(GROUP):
            p = g * GROUP + u
            h, o, k = m.home[p], m.other[p], m.kind[p]
            row = m.tiles[h]
            d2 = None
            for x in range(3):
                sep = m.col[o, x] - (row[x:x + 1, :] - m.image[x, p].astype(F32) * CELL)
                d2 = sep * sep if d2 is None else d2 + sep * sep
            m.kern_ba[p] = jnp.exp2(d2 * (-LOG2E * m.decay[k]))
        return 0

    half_steps = pairs // GROUP // 2
    lax.fori_loop(0, half_steps, kernels, 0)
    for q in (late, 1 - late):
        t = own + 2 * c + q
        for rows in halves:
            take(m.ext.at[t, rows], m.r_feat.at[q, rows.start // size])
            push(m.ext.at[t, rows], m.ext.at[t, rows], m.near_sem.at[2], at(d, partner))
    lax.fori_loop(half_steps, pairs // GROUP, kernels, 0)
    plan_copy.wait()
    take(m.ext.at[pl.ds(own + 2 * mate, 2)], m.near_sem.at[2])

    def pair_at(row, i):
        return jnp.clip(m.plan[row, i], 0, pairs - 1)

    def sum_at(row, i):
        return jnp.clip(m.plan[row, i], 0, pairs)

    def seg_f(p):
        return m.home[p] * kinds + m.kind[p]

    def forward():
        acc = None
        for i in range(pairs):
            p = pair_at(0, i)
            part = mm(m.kern_ab[p], m.ext[m.other[p]])
            acc = part if i == 0 else acc * (seg_f(p) == seg_f(pair_at(0, i - 1))).astype(F32) + part
            m.sums[i + 1] = acc.astype(BF16)

    forward()

    def message(h):
        left = [m.sums[sum_at(2, h * kinds + k)] for k in range(kinds)]
        return mm(jnp.concatenate(left, axis=1), m.radial[...].reshape(kinds * channels, channels))

    m.msg[...] = message(mate).astype(BF16).reshape(m.msg.shape)
    for q in range(2):
        push(m.msg.at[q], m.msg_in.at[q], m.near_sem.at[q], at(d, partner))
    value = message(c).reshape(m.msg.shape)
    for q in range(2):
        take(m.msg_in.at[q], m.near_sem.at[q])
        m.chip[q] = (value[q] + m.msg_in[q].astype(F32)).astype(BF16)
        push(m.chip.at[q], m.chip_in.at[q], m.r_chip.at[q], at(d, across))
    def twin(near):
        return pltpu.make_async_remote_copy(
            m.chip.at[1], m.twin.at[1 - near], m.sent, m.near_sem.at[5] if near else m.r_chip.at[2],
            device_id=at(d, partner if near else cross), device_id_type=MESH)

    @pl.when(c == 0)
    def _():
        twin(0).start()
        twin(1).start()

    for t in range(4):
        columns(own + t)
        table(own + t)
    lax.fori_loop(0, pairs // GROUP, transposed, 0)
    def activate(one, two):
        low = (one.astype(F32) + two.astype(F32)).astype(BF16)
        mixed = mm(low, m.mixing[...])
        sig = jax.nn.sigmoid(mixed)
        return low, (m.readout[...] * sig * (1.0 + mixed * (1.0 - sig))).astype(BF16)

    def slope_copy(q):
        return pltpu.make_async_remote_copy(m.slope.at[c, q], m.slope.at[c, q], m.sent, m.near_sem.at[3],
                                            device_id=at(d, partner), device_id_type=MESH)

    for q in range(2):
        take(m.chip_in.at[q], m.r_chip.at[q])
        low, slope = activate(m.chip[q], m.chip_in[q])
        m.slope[c, q] = slope
        m.packed[c, q] = low
        if q == 0:
            slope_copy(q).start()
        else:
            @pl.when(c == 1)
            def _():
                slope_copy(q).start()
    push(m.packed.at[c], m.packed.at[c], m.near_sem.at[4], at(d, partner))

    @pl.when(c == 0)
    def _():
        take(m.slope.at[mate], m.near_sem.at[3])

    @pl.when(c == 1)
    def _():
        take(m.slope.at[mate, 0], m.near_sem.at[3])
        take(m.twin.at[0], m.near_sem.at[5])
        take(m.twin.at[1], m.r_chip.at[2])
        m.slope[mate, 1] = activate(m.twin[0], m.twin[1])[1]
    slope = m.slope[...].reshape(atoms, channels)
    for k in range(kinds):
        wide = nt(slope, m.radmix[k]).astype(BF16)
        for j in range(own):
            m.weights[j * kinds + k] = wide[j * TILE:(j + 1) * TILE]

    sub = lax.broadcasted_iota(jnp.int32, (8, TILE), 0)
    is_x1, is_y1 = (sub == 0) | (sub == 3) | (sub == 4), (sub == 1) | (sub == 5)
    is_x2, is_y2 = (sub == 0), (sub == 1) | (sub == 3)

    def combine(res, a, b):
        quad = res[0:8] + res[32:40] + res[56:64]
        lin1 = res[8:16] + res[40:48] + res[64:72]
        lin2 = res[16:24] + res[48:56] + res[72:80]
        one = res[24:32]
        force = lin1 - a * one
        virial = -0.5 * (quad - a * lin2 - b * lin1 + a * b * one)
        return jnp.concatenate([force, virial], axis=0)

    def pair_b(i):
        p = pair_at(1, i)
        last = pair_at(1, jnp.maximum(i - 1, 0))
        keep = (m.other[p] == m.other[last]).astype(F32)
        return p, m.home[p], m.other[p], m.kind[p], keep

    def spread_back():
        acc = None
        for i in range(pairs):
            p, h, _, k, keep = pair_b(i)
            part = mm(m.kern_ba[p].astype(BF16), m.weights[h * kinds + k])
            acc = part if i == 0 else acc * keep + part
            m.sums[i + 1] = acc.astype(BF16)

    def backward(g, _):
        found = []
        for u in range(back_group):
            i = g * back_group + u
            p, h, o, k, keep = pair_b(i)
            grad = nt(m.ext[o], m.weights[h * kinds + k])
            found.append((i, p, h, o, keep, ((-2.0 * m.decay[k]) * m.kern_ba[p] * grad).astype(BF16)))
        far = m.far[g * back_group]
        near = [m.near[j] for j in range(own)]
        results = []
        for one, two in zip(found[::2], found[1::2]):
            weight = jnp.concatenate([one[-1], two[-1]], axis=1)
            close = mm(jnp.concatenate([m.moments[one[3]], m.moments[two[3]]], axis=0), weight)
            beyond = nt(jnp.concatenate([m.sided[one[2], 0], m.sided[two[2], 1]], axis=0), weight)
            size = close.shape[0] // 2
            results += [(close[:size, :TILE], beyond[:size]), (close[size:, TILE:], beyond[size:])]
        for (i, p, h, o, keep, _), (close, beyond) in zip(found, results):
            shift = [m.image[x, p].astype(F32) * CELL for x in range(3)]
            s1 = jnp.where(is_x1, shift[0], jnp.where(is_y1, shift[1], shift[2]))
            s2 = jnp.where(is_x2, shift[0], jnp.where(is_y2, shift[1], shift[2]))
            near_side = combine(close, m.first[h] - s1, m.second[h] - s2)
            far_side = combine(beyond, m.first[o] + s1, m.second[o] + s2)
            for j in range(own):
                near[j] = near[j] + near_side * (h == j).astype(F32)
            far = far * keep + far_side
            m.far[i + 1] = far
        for j in range(own):
            m.near[j] = near[j]
        return 0

    spread_back()

    share = channels // n_rep
    slots = (2 - late, 1 + late, 0)
    away = [(slot, own + 2 * mate + slot - 1) for slot in slots[:2]] + [(0, mate)]
    held = [(slot, own + 2 * c + slot - 1) for slot in slots[:2]] + [(0, c)]

    def settle(group):
        total = jnp.concatenate([m.sums[sum_at(3, j)] for _, j in group], axis=0)
        turned = nt(m.eye[:channels, :channels], total).astype(BF16)
        for i, (_, j) in enumerate(group):
            m.gfeat[j] = turned[:, i * TILE:(i + 1) * TILE].reshape(n_rep, share, TILE)

    for group in (away[:1], away[1:]):
        settle(group)
        for slot, j in group:
            push(m.gfeat.at[j], m.gp.at[slot], m.near_sem.at[slot], at(d, partner))
    settle(held)
    lax.fori_loop(0, 1 - c, backward, 0)
    pl.semaphore_wait(m.passed, n_rep - 1)
    for place, (slot, j) in enumerate(held):
        take(m.gp.at[slot], m.near_sem.at[slot])
        m.sb[slot] = (m.gfeat[j].astype(F32) + m.gp[slot].astype(F32)).astype(BF16)
        if place < 2:
            for q in (across, cross, r, partner):
                push(m.sb.at[slot, q], m.rf.at[slot - 1, c, y], m.r_rf.at[slot - 1],
                     at(dom_at((c + 1) * (2 * slot - 3)), q))
    for q in (across, cross, partner):
        push(m.sb.at[0, q], m.ro.at[r], m.r_ro, at(d, q))
    m.ro[r] = m.sb[0, r]
    lax.fori_loop(1 - c, pairs // back_group, backward, 0)
    for t, o in enumerate(OFFSETS):
        m.side[t] = m.far[sum_at(3, own + t)].astype(BF16)
        push(m.side.at[t], m.rs.at[t], m.r_rs, at(dom_at(-o), r))
    take(m.packed.at[mate], m.near_sem.at[4])
    pick = (lax.broadcasted_iota(jnp.int32, (channels, share), 0)
            == lax.broadcasted_iota(jnp.int32, (channels, share), 1) + r * share).astype(BF16)
    cols = mm(m.slope[...].reshape(atoms, channels), pick).astype(BF16)
    m.mix[...] = tn(m.packed[...].reshape(atoms, channels), cols).reshape(m.mix.shape)
    def mix_copy(i):
        to = lax.rem(d + i, n_dom)
        return pltpu.make_async_remote_copy(m.mix.at[to], m.rm.at[d], m.sent, m.r_mix,
                                            device_id=at(to, r), device_id_type=MESH)

    lax.fori_loop(1, n_dom, lambda i, _: (mix_copy(i).start(), 0)[1], 0)
    take(m.ro.at[:n_rep - 1], m.r_ro)
    total = jnp.concatenate([m.ro[j].astype(F32) + m.ro[own + j].astype(F32) for j in range(own)], axis=1)
    def gather(group):
        take(m.rf.at[group], m.r_rf.at[group])
        both = nt(jnp.concatenate([m.rf[group, i].reshape(2 * share, TILE) for i in range(2)], axis=1), m.hot[group])
        return both[:share] + both[share:]

    total = total + gather(1 - late)
    m.part[r] = (total + gather(late)).astype(BF16)
    low, high = pl.ds(0, share // 2), pl.ds(share // 2, share // 2)
    push(m.part.at[r, high], m.part.at[r, high], m.r_chip.at[0], at(d, across))
    push(m.part.at[r, low], m.part.at[r, low], m.r_chip.at[1], at(d, across))
    push(m.part.at[r, low], m.part.at[r, low], m.r_chip.at[1], at(d, cross))
    push(m.part.at[r], m.part.at[r], m.near_sem.at[3], at(d, partner))
    take(m.rs, m.r_rs)
    spots = sum(nt(jnp.concatenate([m.rs[i], m.rs[i + 2]], axis=1), m.hot[i]) for i in range(2))
    here = jnp.concatenate([m.far[sum_at(3, j)] + m.near[j] for j in range(own)], axis=1)
    m.pside[r] = (here + spots).astype(BF16)
    for q in (across, cross, partner):
        push(m.pside.at[r], m.pside.at[r], m.r_pos, at(d, q))
    def finish(half):
        width = channels // 2
        turned = nt(m.eye[:atoms, :atoms], m.part[pl.ds(2 * half, 2)].reshape(width, atoms))
        m.out_feat[:, pl.ds(pl.multiple_of(half * width, TILE), width)] = turned.astype(BF16)

    take(m.part.at[partner], m.near_sem.at[3])
    finish(y)
    take(m.part.at[across, high], m.r_chip.at[0])
    push(m.part.at[across, high], m.part.at[across, high], m.near_sem.at[4], at(d, partner))
    take(m.rm.at[:n_dom - 1], m.r_mix)
    m.out_mix[...] = lax.fori_loop(1, n_dom, lambda i, v: v + m.rm[lax.rem(d + i, n_dom)], m.mix[d])
    take(m.pside.at[:n_rep - 1], m.r_pos)
    final = sum(m.pside[q].astype(F32) for q in range(n_rep))
    m.out_force[...] = final[0:3]
    m.out_virial[...] = final[8:14]
    take(m.part.at[pl.ds(2 * (1 - y), 2), low], m.r_chip.at[1])
    take(m.part.at[cross, high], m.near_sem.at[4])
    finish(1 - y)
    for copy in started + [slope_copy(0)]:
        copy.wait_send()

    @pl.when(c == 0)
    def _():
        twin(0).wait_send()
        twin(1).wait_send()

    @pl.when(c == 1)
    def _():
        slope_copy(1).wait_send()

    lax.fori_loop(1, n_dom, lambda i, _: (mix_copy(i).wait_send(), 0)[1], 0)


def copy_out(a, b, c, d, a_h, b_h, c_h, d_h, sem):
    copies = [pltpu.make_async_copy(src, dst, sem)
              for src, dst in ((a, a_h), (b, b_h), (c, c_h), (d, d_h))]
    for copy in copies:
        copy.start()
    for copy in copies:
        copy.wait()


def on_device(n_dom, n_rep, features, positions, radial, mixing, readout, decay, send_rows, pair_home,
              pair_other, pair_kind, pair_image):
    atoms, channels = features.shape
    own = atoms // TILE
    n_ext = own + len(OFFSETS)
    kinds = radial.shape[0]
    pairs = pair_home.shape[0]
    dma = pltpu.SemaphoreType.DMA
    mix_rows, mix_cols = channels // n_dom, channels // n_rep
    quarters = (n_rep, channels // n_rep, TILE)
    readout_row = readout.reshape(1, channels)
    pair_rows = [a.reshape(1, pairs) for a in (pair_home, pair_other, pair_kind)]

    scratch = {
        "feat": pltpu.VMEM(features.shape, BF16), "pos": pltpu.VMEM(positions.shape, F32),
        "rows": pltpu.VMEM(send_rows.shape, jnp.int32), "radial": pltpu.VMEM(radial.shape, BF16),
        "mixing": pltpu.VMEM(mixing.shape, BF16), "readout": pltpu.VMEM(readout_row.shape, F32),
        "decay": pltpu.SMEM(decay.shape, F32), "home": pltpu.SMEM(pair_home.shape, jnp.int32),
        "other": pltpu.SMEM(pair_other.shape, jnp.int32), "kind": pltpu.SMEM(pair_kind.shape, jnp.int32),
        "image": pltpu.SMEM(pair_image.shape, jnp.int32),
        "home_row": pltpu.VMEM((1, pairs), jnp.int32), "other_row": pltpu.VMEM((1, pairs), jnp.int32),
        "kind_row": pltpu.VMEM((1, pairs), jnp.int32),
        "raw": pltpu.VMEM((8, TILE), jnp.int32), "plan_v": pltpu.VMEM((8, TILE), jnp.int32),
        "plan": pltpu.SMEM((8, TILE), jnp.int32),
        "sendf": pltpu.VMEM((2, TILE, channels), BF16), "sendp": pltpu.VMEM((2, 3, TILE), F32),
        "recvp": pltpu.VMEM((4, 3, TILE), F32), "ext": pltpu.VMEM((n_ext, TILE, channels), BF16),
        "tiles": pltpu.VMEM((n_ext, 3, TILE), F32), "col": pltpu.VMEM((n_ext, 3, TILE, TILE), F32),
        "moments": pltpu.VMEM((n_ext, 80, TILE), BF16),
        "sided": pltpu.VMEM((own, 2, 80, 2 * TILE), BF16), "hot": pltpu.VMEM((2, atoms, 2 * TILE), BF16),
        "first": pltpu.VMEM((n_ext, 8, TILE), F32), "second": pltpu.VMEM((n_ext, 8, TILE), F32),
        "kern_ab": pltpu.VMEM((pairs, TILE, TILE), BF16), "kern_ba": pltpu.VMEM((pairs, TILE, TILE), F32),
        "sums": pltpu.VMEM((pairs + 1, TILE, channels), BF16), "far": pltpu.VMEM((pairs + 1, 16, TILE), F32),
        "near": pltpu.VMEM((own, 16, TILE), F32),
        "msg": pltpu.VMEM((2, TILE // 2, channels), BF16), "msg_in": pltpu.VMEM((2, TILE // 2, channels), BF16),
        "chip": pltpu.VMEM((2, TILE // 2, channels), BF16), "twin": pltpu.VMEM((2, TILE // 2, channels), BF16), "chip_in": pltpu.VMEM((2, TILE // 2, channels), BF16),
        "slope": pltpu.VMEM((own, 2, TILE // 2, channels), BF16),
        "packed": pltpu.VMEM((own, 2, TILE // 2, channels), BF16), "radmix": pltpu.VMEM(radial.shape, BF16),
        "weights": pltpu.VMEM((own * kinds, TILE, channels), BF16),
        "gfeat": pltpu.VMEM((n_ext, *quarters), BF16), "side": pltpu.VMEM((4, 16, TILE), BF16),
        "gp": pltpu.VMEM((3, *quarters), BF16),
        "sb": pltpu.VMEM((3, *quarters), BF16),
        "rf": pltpu.VMEM((2, 2, 2, *quarters[1:]), BF16), "ro": pltpu.VMEM(quarters, BF16), "rs": pltpu.VMEM((4, 16, TILE), BF16),
        "mix": pltpu.VMEM((n_dom, mix_rows, mix_cols), F32), "rm": pltpu.VMEM((n_dom, mix_rows, mix_cols), F32),
        "part": pltpu.VMEM((n_rep, channels // n_rep, atoms), BF16),
        "eye": pltpu.VMEM((max(atoms, channels),) * 2, BF16),
        "pside": pltpu.VMEM((n_rep, 16, atoms), BF16),
        "load": dma((3,)), "sent": dma, "passed": pltpu.SemaphoreType.REGULAR, "r_pos": dma,
        "r_feat": dma((2, 2)), "near_sem": dma((6,)), "r_chip": dma((3,)),
        "r_rf": dma((2,)), "r_ro": dma, "r_rs": dma, "r_mix": dma,
    }

    def shape(dims, dtype):
        return jax.ShapeDtypeStruct(dims, dtype)

    results = pl.pallas_call(
        functools.partial(kernel, INPUTS + OUTPUTS + tuple(scratch), n_dom, n_rep),
        out_shape=(shape((atoms, channels), BF16), shape((3, atoms), F32), shape((6, atoms), F32),
                   shape((mix_rows, mix_cols), F32)),
        in_specs=[HBM] * len(INPUTS),
        out_specs=(VMEM,) * 4,
        scratch_shapes=list(scratch.values()),
        compiler_params=pltpu.CompilerParams(collective_id=0, has_side_effects=True, vmem_limit_bytes=48 << 20),
        name="layer",
    )(*[pltpu.with_memory_space_constraint(a, pltpu.HBM) for a in (
        features, positions, send_rows, radial, mixing, readout_row, decay, pair_home, pair_other, pair_kind,
        pair_image, *pair_rows)])
    return pl.pallas_call(
        copy_out,
        out_shape=tuple(shape(a.shape, a.dtype) for a in results),
        in_specs=[VMEM] * 4,
        out_specs=(HBM,) * 4,
        scratch_shapes=[dma],
        compiler_params=pltpu.CompilerParams(vmem_limit_bytes=4 << 20),
        name="copy_out",
    )(*results)


def solution(mesh):
    in_specs = (
        P("dom", None),
        P(None, "dom"),
        P(),
        P(),
        P(),
        P(),
        P(None, "dom"),
        P(("dom", "rep")),
        P(("dom", "rep")),
        P(("dom", "rep")),
        P(None, ("dom", "rep")),
    )
    out_specs = (P("dom", None), P(None, "dom"), P(None, "dom"), P("dom", "rep"))
    body = functools.partial(on_device, mesh.shape["dom"], mesh.shape["rep"])
    return jax.shard_map(body, mesh=mesh, in_specs=in_specs, out_specs=out_specs, check_vma=False)
```

```python
import functools
import types

import jax
import jax.numpy as jnp
from jax import lax
from jax.experimental import pallas as pl
from jax.experimental.pallas import tpu as pltpu
from jax.sharding import PartitionSpec as P

TILE = 128
OFFSETS = (1, -1, 2, -2)
CELL = 2.0
GROUP = 12
WIDE_GROUP = 48
BACK_GROUP = 24
LOG2E = 1.4426950408889634
F32 = jnp.float32
BF16 = jnp.bfloat16
MESH = pl.DeviceIdType.MESH
VMEM = pl.BlockSpec(memory_space=pltpu.VMEM)
HBM = pl.BlockSpec(memory_space=pltpu.HBM)
INPUTS = ("feat_h", "pos_h", "rows_h", "radial_h", "mixing_h", "readout_h", "decay_h", "home_h", "other_h",
          "kind_h", "image_h", "home_row_h", "other_row_h", "kind_row_h")
OUTPUTS = ("out_feat", "out_force", "out_virial", "out_mix")


def nt(a, b):
    return lax.dot_general(a, b, (((1,), (1,)), ((), ())), preferred_element_type=F32)


def tn(a, b):
    return lax.dot_general(a, b, (((0,), (0,)), ((), ())), preferred_element_type=F32)


def mm(a, b):
    return jnp.dot(a, b, preferred_element_type=F32)


def split3(x):
    hi = x.astype(BF16)
    rest = x - hi.astype(F32)
    mid = rest.astype(BF16)
    low = (rest - mid.astype(F32)).astype(BF16)
    return hi, mid, low


def order_pairs(seg, lanes, subs):
    row = jnp.broadcast_to(seg, (TILE, TILE))
    col = jnp.transpose(row)
    before = (col < row) | ((col == row) & (subs < lanes))
    rank = jnp.sum(before.astype(jnp.int32), axis=0, keepdims=True)
    rank = jnp.transpose(jnp.broadcast_to(rank, (TILE, TILE)))
    order = jnp.sum(jnp.where(rank == lanes, subs, 0), axis=0, keepdims=True)
    upto = jnp.sum((col <= lanes).astype(jnp.int32), axis=0, keepdims=True)
    below = jnp.sum((col < lanes).astype(jnp.int32), axis=0, keepdims=True)
    return order, jnp.where(upto > below, upto, 0)


def kernel(names, n_dom, n_rep, *refs):
    m = types.SimpleNamespace(**dict(zip(names, refs)))
    d = lax.axis_index("dom")
    r = lax.axis_index("rep")
    y = lax.div(r, 2)
    c = lax.rem(r, 2)
    mate = 1 - c
    partner = r + 1 - 2 * c
    across = r + 2 - 4 * y
    cross = across + 1 - 2 * c
    atoms, channels = m.feat.shape
    own = atoms // TILE
    late = lax.div(n_dom - 1 - d, n_dom // 2)
    pairs = m.home.shape[0]
    kinds = m.radial.shape[0]
    n_ext = m.tiles.shape[0]
    size = TILE // 2
    halves = [pl.ds(i * size, size) for i in range(2)]

    def dom_at(o):
        return lax.rem(d + o + n_dom, n_dom)

    def at(dom, rep):
        return {"dom": dom, "rep": rep}

    groups = ((m.rows_h, m.rows), (m.feat_h, m.feat), (m.pos_h, m.pos)), (
        (m.home_row_h, m.home_row), (m.other_row_h, m.other_row), (m.kind_row_h, m.kind_row)), (
        (m.radial_h, m.radial), (m.decay_h, m.decay), (m.home_h, m.home), (m.other_h, m.other),
        (m.kind_h, m.kind), (m.image_h, m.image), (m.mixing_h, m.mixing), (m.readout_h, m.readout))
    loads = [[pltpu.make_async_copy(src, dst, m.load.at[i]) for src, dst in group]
             for i, group in enumerate(groups)]
    for copy in loads[0]:
        copy.start()
    barrier = pltpu.get_barrier_semaphore()
    mine = (c + 1, -(c + 1))
    theirs = (2 - c, c - 2)
    peers = [lax.rem(r + i, n_rep) for i in range(1, n_rep)]

    def hello(dom, rep):
        pl.semaphore_signal(barrier, inc=1, device_id=at(dom, rep), device_id_type=MESH)

    def greet(i, _):
        hello(lax.rem(d + i, n_dom), r)
        return 0

    lax.fori_loop(1, n_dom, greet, 0)
    for o in mine:
        hello(dom_at(o), partner)
    for o in theirs:
        hello(dom_at(o), partner)
    for q in peers:
        hello(d, q)
    for copy in loads[1] + loads[2]:
        copy.start()

    started = []

    def push(src, dst, rs, target):
        copy = pltpu.make_async_remote_copy(src, dst, m.sent, rs, device_id=target, device_id_type=MESH)
        copy.start()
        started.append(copy)

    def take(dst, rs):
        pltpu.make_async_remote_copy(dst, dst, m.sent, rs, device_id=at(d, partner), device_id_type=MESH).wait_recv()

    for copy in loads[0]:
        copy.wait()
    iota = lax.broadcasted_iota(jnp.int32, (atoms, TILE), 0)
    hots = []
    for q in range(2):
        hot = (iota == m.rows[pl.ds(2 * c + q, 1), :]).astype(F32)
        hots.append(hot.astype(BF16))
        m.sendp[q] = jnp.dot(m.pos[...], hot, precision=lax.Precision.HIGHEST, preferred_element_type=F32)
    for q in range(2):
        m.sendf[q] = tn(hots[q], m.feat[...]).astype(BF16)
    pl.semaphore_wait(barrier, 4 + n_rep - 1 + n_dom - 1)
    for q in (late, 1 - late):
        for i, rep in enumerate((r, partner)):
            push(m.sendp.at[q], m.recvp.at[2 * c + q], m.r_pos,
                 at(dom_at((c + 1) * (1 - 2 * q)), rep))
    for q in (late, 1 - late):
        for rows in halves:
            push(m.sendf.at[q, rows], m.ext.at[own + 2 * c + q, rows], m.r_feat.at[q, rows.start // size],
                 at(dom_at((c + 1) * (1 - 2 * q)), r))

    for copy in loads[1]:
        copy.wait()
    m.raw[...] = jnp.zeros_like(m.raw)
    for i, src in enumerate((m.home_row, m.kind_row, m.other_row)):
        m.raw[i:i + 1, :pairs] = src[...]
    raw = m.raw[...]
    lanes = lax.broadcasted_iota(jnp.int32, (TILE, TILE), 1)
    subs = lax.broadcasted_iota(jnp.int32, (TILE, TILE), 0)
    real = lanes[0:1] < pairs
    order_f, end_f = order_pairs(jnp.where(real, raw[0:1] * kinds + raw[1:2], TILE), lanes, subs)
    order_b, end_b = order_pairs(jnp.where(real, raw[2:3], TILE), lanes, subs)
    m.plan_v[...] = jnp.concatenate(
        [order_f, order_b, end_f, end_b, jnp.zeros((4, TILE), jnp.int32)], axis=0)
    plan_copy = pltpu.make_async_copy(m.plan_v, m.plan, m.load.at[0])
    plan_copy.start()

    def columns(j):
        for x in range(3):
            m.col[j, x] = jnp.transpose(jnp.broadcast_to(m.tiles[j][x:x + 1, :], (TILE, TILE)))

    def table(j):
        pos = m.tiles[j]
        x, yy, z = pos[0:1, :], pos[1:2, :], pos[2:3, :]
        zero = jnp.zeros((2, TILE), F32)
        one_rows = jnp.concatenate([x, yy, z, x, x, yy, zero], axis=0)
        two_rows = jnp.concatenate([x, yy, z, yy, z, z, zero], axis=0)
        m.first[j] = one_rows
        m.second[j] = two_rows
        stack = jnp.concatenate([one_rows * two_rows, one_rows, two_rows], axis=0)
        parts = [v.astype(F32) for v in split3(stack)]
        stack = jnp.concatenate([parts[0], jnp.ones((8, TILE), F32), parts[1], parts[2]], axis=0).astype(BF16)
        m.moments[j] = stack
        if j < own:
            m.sided[j, 0] = jnp.concatenate([stack, jnp.zeros_like(stack)], axis=1)
            m.sided[j, 1] = jnp.concatenate([jnp.zeros_like(stack), stack], axis=1)

    for j in range(own):
        m.tiles[j] = m.pos[:, j * TILE:(j + 1) * TILE]
        m.ext[j] = m.feat[j * TILE:(j + 1) * TILE, :]
        columns(j)
    for q in peers:
        pl.semaphore_signal(m.passed, inc=1, device_id=at(d, q), device_id_type=MESH)
    m.sums[0] = jnp.zeros_like(m.sums[0])
    m.carry[...] = jnp.zeros_like(m.carry)
    for t in range(4):
        m.hot[t % 2, :, t // 2 * TILE:(t // 2 + 1) * TILE] = (iota == m.rows[t:t + 1, :]).astype(F32).astype(BF16)
    m.far[0] = jnp.zeros_like(m.far[0])
    m.near[...] = jnp.zeros_like(m.near)
    m.eye[...] = (lax.broadcasted_iota(jnp.int32, m.eye.shape, 0)
                  == lax.broadcasted_iota(jnp.int32, m.eye.shape, 1)).astype(F32).astype(BF16)
    for j in range(own):
        table(j)
    for copy in loads[2]:
        copy.wait()
    for k in range(kinds):
        m.radmix[k] = mm(m.radial[k], m.mixing[...]).astype(BF16)
    take(m.recvp, m.r_pos)
    for t in range(4):
        m.tiles[own + t] = m.recvp[t]

    def kernels(g, _):
        for u in range(GROUP):
            p = g * GROUP + u
            h, o, k = m.home[p], m.other[p], m.kind[p]
            row = m.tiles[o]
            d2 = None
            for x in range(3):
                sep = (row[x:x + 1, :] + m.image[x, p].astype(F32) * CELL) - m.col[h, x]
                d2 = sep * sep if d2 is None else d2 + sep * sep
            m.kern_ab[p] = jnp.exp2(d2 * (-LOG2E * m.decay[k])).astype(BF16)
        return 0

    def transposed(g, _):
        for u in range(GROUP):
            p = g * GROUP + u
            h, o, k = m.home[p], m.other[p], m.kind[p]
            row = m.tiles[h]
            d2 = None
            for x in range(3):
                sep = m.col[o, x] - (row[x:x + 1, :] - m.image[x, p].astype(F32) * CELL)
                d2 = sep * sep if d2 is None else d2 + sep * sep
            m.kern_ba[p] = jnp.exp2(d2 * (-LOG2E * m.decay[k]))
        return 0

    half_steps = pairs // GROUP // 2
    lax.fori_loop(0, half_steps, kernels, 0)
    for q in (late, 1 - late):
        t = own + 2 * c + q
        for rows in halves:
            take(m.ext.at[t, rows], m.r_feat.at[q, rows.start // size])
            push(m.ext.at[t, rows], m.ext.at[t, rows], m.near_sem.at[2], at(d, partner))
    lax.fori_loop(half_steps, pairs // GROUP, kernels, 0)
    plan_copy.wait()
    take(m.ext.at[pl.ds(own + 2 * mate, 2)], m.near_sem.at[2])

    def pair_at(row, i):
        return jnp.clip(m.plan[row, i], 0, pairs - 1)

    def sum_at(row, i):
        return jnp.clip(m.plan[row, i], 0, pairs)

    def seg_f(p):
        return m.home[p] * kinds + m.kind[p]

    def forward(g, _):
        acc = m.carry[...]
        for u in range(WIDE_GROUP):
            i = g * WIDE_GROUP + u
            p = pair_at(0, i)
            last = pair_at(0, jnp.maximum(i - 1, 0))
            keep = (seg_f(p) == seg_f(last)).astype(F32)
            acc = acc * keep + mm(m.kern_ab[p], m.ext[m.other[p]])
            m.sums[i + 1] = acc.astype(BF16)
        m.carry[...] = acc
        return 0

    lax.fori_loop(0, pairs // WIDE_GROUP, forward, 0)

    def message(h):
        left = [m.sums[sum_at(2, h * kinds + k)] for k in range(kinds)]
        return mm(jnp.concatenate(left, axis=1), m.radial[...].reshape(kinds * channels, channels))

    m.msg[...] = message(mate).astype(BF16).reshape(m.msg.shape)
    for q in range(2):
        push(m.msg.at[q], m.msg_in.at[q], m.near_sem.at[q], at(d, partner))
    value = message(c).reshape(m.msg.shape)
    for q in range(2):
        take(m.msg_in.at[q], m.near_sem.at[q])
        m.chip[q] = (value[q] + m.msg_in[q].astype(F32)).astype(BF16)
        push(m.chip.at[q], m.chip_in.at[q], m.r_chip.at[q], at(d, across))
    def twin(near):
        return pltpu.make_async_remote_copy(
            m.chip.at[1], m.twin.at[1 - near], m.sent, m.near_sem.at[5] if near else m.r_chip.at[2],
            device_id=at(d, partner if near else cross), device_id_type=MESH)

    @pl.when(c == 0)
    def _():
        twin(0).start()
        twin(1).start()

    for t in range(4):
        columns(own + t)
        table(own + t)
    lax.fori_loop(0, pairs // GROUP, transposed, 0)
    def activate(one, two):
        low = (one.astype(F32) + two.astype(F32)).astype(BF16)
        mixed = mm(low, m.mixing[...])
        sig = jax.nn.sigmoid(mixed)
        return low, (m.readout[...] * sig * (1.0 + mixed * (1.0 - sig))).astype(BF16)

    def slope_copy(q):
        return pltpu.make_async_remote_copy(m.slope.at[c, q], m.slope.at[c, q], m.sent, m.near_sem.at[3],
                                            device_id=at(d, partner), device_id_type=MESH)

    for q in range(2):
        take(m.chip_in.at[q], m.r_chip.at[q])
        low, slope = activate(m.chip[q], m.chip_in[q])
        m.slope[c, q] = slope
        m.packed[c, q] = low
        if q == 0:
            slope_copy(q).start()
        else:
            @pl.when(c == 1)
            def _():
                slope_copy(q).start()
    push(m.packed.at[c], m.packed.at[c], m.near_sem.at[4], at(d, partner))

    @pl.when(c == 0)
    def _():
        take(m.slope.at[mate], m.near_sem.at[3])

    @pl.when(c == 1)
    def _():
        take(m.slope.at[mate, 0], m.near_sem.at[3])
        take(m.twin.at[0], m.near_sem.at[5])
        take(m.twin.at[1], m.r_chip.at[2])
        m.slope[mate, 1] = activate(m.twin[0], m.twin[1])[1]
    slope = m.slope[...].reshape(atoms, channels)
    for k in range(kinds):
        wide = nt(slope, m.radmix[k]).astype(BF16)
        for j in range(own):
            m.weights[j * kinds + k] = wide[j * TILE:(j + 1) * TILE]

    sub = lax.broadcasted_iota(jnp.int32, (8, TILE), 0)
    is_x1, is_y1 = (sub == 0) | (sub == 3) | (sub == 4), (sub == 1) | (sub == 5)
    is_x2, is_y2 = (sub == 0), (sub == 1) | (sub == 3)

    def combine(res, a, b):
        quad = res[0:8] + res[32:40] + res[56:64]
        lin1 = res[8:16] + res[40:48] + res[64:72]
        lin2 = res[16:24] + res[48:56] + res[72:80]
        one = res[24:32]
        force = lin1 - a * one
        virial = -0.5 * (quad - a * lin2 - b * lin1 + a * b * one)
        return jnp.concatenate([force, virial], axis=0)

    def pair_b(i):
        p = pair_at(1, i)
        last = pair_at(1, jnp.maximum(i - 1, 0))
        keep = (m.other[p] == m.other[last]).astype(F32)
        return p, m.home[p], m.other[p], m.kind[p], keep

    def spread_back(g, _):
        acc = m.carry[...]
        for u in range(WIDE_GROUP):
            i = g * WIDE_GROUP + u
            p, h, _, k, keep = pair_b(i)
            acc = acc * keep + mm(m.kern_ba[p].astype(BF16), m.weights[h * kinds + k])
            m.sums[i + 1] = acc.astype(BF16)
        m.carry[...] = acc
        return 0

    def backward(g, _):
        found = []
        for u in range(BACK_GROUP):
            i = g * BACK_GROUP + u
            p, h, o, k, keep = pair_b(i)
            grad = nt(m.ext[o], m.weights[h * kinds + k])
            found.append((i, p, h, o, keep, ((-2.0 * m.decay[k]) * m.kern_ba[p] * grad).astype(BF16)))
        far = m.far[g * BACK_GROUP]
        near = [m.near[j] for j in range(own)]
        results = []
        for one, two in zip(found[::2], found[1::2]):
            weight = jnp.concatenate([one[-1], two[-1]], axis=1)
            close = mm(jnp.concatenate([m.moments[one[3]], m.moments[two[3]]], axis=0), weight)
            beyond = nt(jnp.concatenate([m.sided[one[2], 0], m.sided[two[2], 1]], axis=0), weight)
            size = close.shape[0] // 2
            results += [(close[:size, :TILE], beyond[:size]), (close[size:, TILE:], beyond[size:])]
        for (i, p, h, o, keep, _), (close, beyond) in zip(found, results):
            shift = [m.image[x, p].astype(F32) * CELL for x in range(3)]
            s1 = jnp.where(is_x1, shift[0], jnp.where(is_y1, shift[1], shift[2]))
            s2 = jnp.where(is_x2, shift[0], jnp.where(is_y2, shift[1], shift[2]))
            near_side = combine(close, m.first[h] - s1, m.second[h] - s2)
            far_side = combine(beyond, m.first[o] + s1, m.second[o] + s2)
            for j in range(own):
                near[j] = near[j] + near_side * (h == j).astype(F32)
            far = far * keep + far_side
            m.far[i + 1] = far
        for j in range(own):
            m.near[j] = near[j]
        return 0

    m.carry[...] = jnp.zeros_like(m.carry)
    lax.fori_loop(0, pairs // WIDE_GROUP, spread_back, 0)

    share = channels // n_rep
    slots = (2 - late, 1 + late, 0)
    away = [(slot, own + 2 * mate + slot - 1) for slot in slots[:2]] + [(0, mate)]
    held = [(slot, own + 2 * c + slot - 1) for slot in slots[:2]] + [(0, c)]

    def settle(group):
        total = jnp.concatenate([m.sums[sum_at(3, j)] for _, j in group], axis=0)
        turned = nt(m.eye[:channels, :channels], total).astype(BF16)
        for i, (_, j) in enumerate(group):
            m.gfeat[j] = turned[:, i * TILE:(i + 1) * TILE].reshape(n_rep, share, TILE)

    for group in (away[:1], away[1:]):
        settle(group)
        for slot, j in group:
            push(m.gfeat.at[j], m.gp.at[slot], m.near_sem.at[slot], at(d, partner))
    settle(held)
    lax.fori_loop(0, 1 - c, backward, 0)
    pl.semaphore_wait(m.passed, n_rep - 1)
    for place, (slot, j) in enumerate(held):
        take(m.gp.at[slot], m.near_sem.at[slot])
        m.sb[slot] = (m.gfeat[j].astype(F32) + m.gp[slot].astype(F32)).astype(BF16)
        if place < 2:
            for q in (across, cross, r, partner):
                push(m.sb.at[slot, q], m.rf.at[slot - 1, c, y], m.r_rf.at[slot - 1],
                     at(dom_at((c + 1) * (2 * slot - 3)), q))
    for q in (across, cross, partner):
        push(m.sb.at[0, q], m.ro.at[r], m.r_ro, at(d, q))
    m.ro[r] = m.sb[0, r]
    lax.fori_loop(1 - c, pairs // BACK_GROUP, backward, 0)
    for t, o in enumerate(OFFSETS):
        m.side[t] = m.far[sum_at(3, own + t)].astype(BF16)
        push(m.side.at[t], m.rs.at[t], m.r_rs, at(dom_at(-o), r))
    take(m.packed.at[mate], m.near_sem.at[4])
    pick = (lax.broadcasted_iota(jnp.int32, (channels, share), 0)
            == lax.broadcasted_iota(jnp.int32, (channels, share), 1) + r * share).astype(BF16)
    cols = mm(m.slope[...].reshape(atoms, channels), pick).astype(BF16)
    m.mix[...] = tn(m.packed[...].reshape(atoms, channels), cols).reshape(m.mix.shape)
    def mix_copy(i):
        to = lax.rem(d + i, n_dom)
        return pltpu.make_async_remote_copy(m.mix.at[to], m.rm.at[d], m.sent, m.r_mix,
                                            device_id=at(to, r), device_id_type=MESH)

    lax.fori_loop(1, n_dom, lambda i, _: (mix_copy(i).start(), 0)[1], 0)
    take(m.ro.at[:n_rep - 1], m.r_ro)
    total = jnp.concatenate([m.ro[j].astype(F32) + m.ro[own + j].astype(F32) for j in range(own)], axis=1)
    def gather(group):
        take(m.rf.at[group], m.r_rf.at[group])
        both = nt(jnp.concatenate([m.rf[group, i].reshape(2 * share, TILE) for i in range(2)], axis=1), m.hot[group])
        return both[:share] + both[share:]

    total = total + gather(1 - late)
    m.part[r] = (total + gather(late)).astype(BF16)
    low, high = pl.ds(0, share - share // 4), pl.ds(share - share // 4, share // 4)
    push(m.part.at[r, high], m.part.at[r, high], m.r_chip.at[0], at(d, across))
    push(m.part.at[r, low], m.part.at[r, low], m.r_chip.at[1], at(d, across))
    push(m.part.at[r, low], m.part.at[r, low], m.r_chip.at[1], at(d, cross))
    push(m.part.at[r], m.part.at[r], m.near_sem.at[3], at(d, partner))
    take(m.rs, m.r_rs)
    spots = sum(nt(jnp.concatenate([m.rs[i], m.rs[i + 2]], axis=1), m.hot[i]) for i in range(2))
    here = jnp.concatenate([m.far[sum_at(3, j)] + m.near[j] for j in range(own)], axis=1)
    m.pside[r] = (here + spots).astype(BF16)
    for q in (across, cross, partner):
        push(m.pside.at[r], m.pside.at[r], m.r_pos, at(d, q))
    def finish(half):
        width = channels // 2
        turned = nt(m.eye[:atoms, :atoms], m.part[pl.ds(2 * half, 2)].reshape(width, atoms))
        m.out_feat[:, pl.ds(pl.multiple_of(half * width, TILE), width)] = turned.astype(BF16)

    take(m.part.at[partner], m.near_sem.at[3])
    finish(y)
    take(m.part.at[across, high], m.r_chip.at[0])
    push(m.part.at[across, high], m.part.at[across, high], m.near_sem.at[4], at(d, partner))
    take(m.rm.at[:n_dom - 1], m.r_mix)
    m.out_mix[...] = lax.fori_loop(1, n_dom, lambda i, v: v + m.rm[lax.rem(d + i, n_dom)], m.mix[d])
    take(m.pside.at[:n_rep - 1], m.r_pos)
    final = sum(m.pside[q].astype(F32) for q in range(n_rep))
    m.out_force[...] = final[0:3]
    m.out_virial[...] = final[8:14]
    take(m.part.at[pl.ds(2 * (1 - y), 2), low], m.r_chip.at[1])
    take(m.part.at[cross, high], m.near_sem.at[4])
    finish(1 - y)
    for copy in started + [slope_copy(0)]:
        copy.wait_send()

    @pl.when(c == 0)
    def _():
        twin(0).wait_send()
        twin(1).wait_send()

    @pl.when(c == 1)
    def _():
        slope_copy(1).wait_send()

    lax.fori_loop(1, n_dom, lambda i, _: (mix_copy(i).wait_send(), 0)[1], 0)


def copy_out(a, b, c, d, a_h, b_h, c_h, d_h, sem):
    copies = [pltpu.make_async_copy(src, dst, sem)
              for src, dst in ((a, a_h), (b, b_h), (c, c_h), (d, d_h))]
    for copy in copies:
        copy.start()
    for copy in copies:
        copy.wait()


def on_device(n_dom, n_rep, features, positions, radial, mixing, readout, decay, send_rows, pair_home,
              pair_other, pair_kind, pair_image):
    atoms, channels = features.shape
    own = atoms // TILE
    n_ext = own + len(OFFSETS)
    kinds = radial.shape[0]
    pairs = pair_home.shape[0]
    dma = pltpu.SemaphoreType.DMA
    mix_rows, mix_cols = channels // n_dom, channels // n_rep
    quarters = (n_rep, channels // n_rep, TILE)
    readout_row = readout.reshape(1, channels)
    pair_rows = [a.reshape(1, pairs) for a in (pair_home, pair_other, pair_kind)]

    scratch = {
        "feat": pltpu.VMEM(features.shape, BF16), "pos": pltpu.VMEM(positions.shape, F32),
        "rows": pltpu.VMEM(send_rows.shape, jnp.int32), "radial": pltpu.VMEM(radial.shape, BF16),
        "mixing": pltpu.VMEM(mixing.shape, BF16), "readout": pltpu.VMEM(readout_row.shape, F32),
        "decay": pltpu.SMEM(decay.shape, F32), "home": pltpu.SMEM(pair_home.shape, jnp.int32),
        "other": pltpu.SMEM(pair_other.shape, jnp.int32), "kind": pltpu.SMEM(pair_kind.shape, jnp.int32),
        "image": pltpu.SMEM(pair_image.shape, jnp.int32),
        "home_row": pltpu.VMEM((1, pairs), jnp.int32), "other_row": pltpu.VMEM((1, pairs), jnp.int32),
        "kind_row": pltpu.VMEM((1, pairs), jnp.int32),
        "raw": pltpu.VMEM((8, TILE), jnp.int32), "plan_v": pltpu.VMEM((8, TILE), jnp.int32),
        "plan": pltpu.SMEM((8, TILE), jnp.int32),
        "sendf": pltpu.VMEM((2, TILE, channels), BF16), "sendp": pltpu.VMEM((2, 3, TILE), F32),
        "recvp": pltpu.VMEM((4, 3, TILE), F32), "ext": pltpu.VMEM((n_ext, TILE, channels), BF16),
        "tiles": pltpu.VMEM((n_ext, 3, TILE), F32), "col": pltpu.VMEM((n_ext, 3, TILE, TILE), F32),
        "moments": pltpu.VMEM((n_ext, 80, TILE), BF16),
        "sided": pltpu.VMEM((own, 2, 80, 2 * TILE), BF16), "hot": pltpu.VMEM((2, atoms, 2 * TILE), BF16),
        "first": pltpu.VMEM((n_ext, 8, TILE), F32), "second": pltpu.VMEM((n_ext, 8, TILE), F32),
        "kern_ab": pltpu.VMEM((pairs, TILE, TILE), BF16), "kern_ba": pltpu.VMEM((pairs, TILE, TILE), F32),
        "sums": pltpu.VMEM((pairs + 1, TILE, channels), BF16),
        "carry": pltpu.VMEM((TILE, channels), F32), "far": pltpu.VMEM((pairs + 1, 16, TILE), F32),
        "near": pltpu.VMEM((own, 16, TILE), F32),
        "msg": pltpu.VMEM((2, TILE // 2, channels), BF16), "msg_in": pltpu.VMEM((2, TILE // 2, channels), BF16),
        "chip": pltpu.VMEM((2, TILE // 2, channels), BF16), "twin": pltpu.VMEM((2, TILE // 2, channels), BF16), "chip_in": pltpu.VMEM((2, TILE // 2, channels), BF16),
        "slope": pltpu.VMEM((own, 2, TILE // 2, channels), BF16),
        "packed": pltpu.VMEM((own, 2, TILE // 2, channels), BF16), "radmix": pltpu.VMEM(radial.shape, BF16),
        "weights": pltpu.VMEM((own * kinds, TILE, channels), BF16),
        "gfeat": pltpu.VMEM((n_ext, *quarters), BF16), "side": pltpu.VMEM((4, 16, TILE), BF16),
        "gp": pltpu.VMEM((3, *quarters), BF16),
        "sb": pltpu.VMEM((3, *quarters), BF16),
        "rf": pltpu.VMEM((2, 2, 2, *quarters[1:]), BF16), "ro": pltpu.VMEM(quarters, BF16), "rs": pltpu.VMEM((4, 16, TILE), BF16),
        "mix": pltpu.VMEM((n_dom, mix_rows, mix_cols), F32), "rm": pltpu.VMEM((n_dom, mix_rows, mix_cols), F32),
        "part": pltpu.VMEM((n_rep, channels // n_rep, atoms), BF16),
        "eye": pltpu.VMEM((max(atoms, channels),) * 2, BF16),
        "pside": pltpu.VMEM((n_rep, 16, atoms), BF16),
        "load": dma((3,)), "sent": dma, "passed": pltpu.SemaphoreType.REGULAR, "r_pos": dma,
        "r_feat": dma((2, 2)), "near_sem": dma((6,)), "r_chip": dma((3,)),
        "r_rf": dma((2,)), "r_ro": dma, "r_rs": dma, "r_mix": dma,
    }

    def shape(dims, dtype):
        return jax.ShapeDtypeStruct(dims, dtype)

    results = pl.pallas_call(
        functools.partial(kernel, INPUTS + OUTPUTS + tuple(scratch), n_dom, n_rep),
        out_shape=(shape((atoms, channels), BF16), shape((3, atoms), F32), shape((6, atoms), F32),
                   shape((mix_rows, mix_cols), F32)),
        in_specs=[HBM] * len(INPUTS),
        out_specs=(VMEM,) * 4,
        scratch_shapes=list(scratch.values()),
        compiler_params=pltpu.CompilerParams(collective_id=0, has_side_effects=True, vmem_limit_bytes=48 << 20),
        name="layer",
    )(*[pltpu.with_memory_space_constraint(a, pltpu.HBM) for a in (
        features, positions, send_rows, radial, mixing, readout_row, decay, pair_home, pair_other, pair_kind,
        pair_image, *pair_rows)])
    return pl.pallas_call(
        copy_out,
        out_shape=tuple(shape(a.shape, a.dtype) for a in results),
        in_specs=[VMEM] * 4,
        out_specs=(HBM,) * 4,
        scratch_shapes=[dma],
        compiler_params=pltpu.CompilerParams(vmem_limit_bytes=4 << 20),
        name="copy_out",
    )(*results)


def solution(mesh):
    in_specs = (
        P("dom", None),
        P(None, "dom"),
        P(),
        P(),
        P(),
        P(),
        P(None, "dom"),
        P(("dom", "rep")),
        P(("dom", "rep")),
        P(("dom", "rep")),
        P(None, ("dom", "rep")),
    )
    out_specs = (P("dom", None), P(None, "dom"), P(None, "dom"), P("dom", "rep"))
    body = functools.partial(on_device, mesh.shape["dom"], mesh.shape["rep"])
    return jax.shard_map(body, mesh=mesh, in_specs=in_specs, out_specs=out_specs, check_vma=False)
```
